32 devices in a mesh: dp: 2 (over x), fsdp: 16 (over z, y, core).
Axes of the slice: x: 2, y: 2, z: 4, core: 2. Of those that a mesh axis runs over, the one named last changes fastest.
Arguments:
- tokens: bfloat16 [32, 512, 768], P(('dp', 'fsdp')), may hold values from -6 to 6
- cotangent: bfloat16 [32, 512, 768], P(('dp', 'fsdp')), may hold values from -6 to 6
- time_embed: bfloat16 [32, 768], P(('dp', 'fsdp')), may hold values from -3 to 3
- cath_class: int32 [32], P(('dp', 'fsdp')), may hold values from 0 to 4
- cath_arch: int32 [32], P(('dp', 'fsdp')), may hold values from 0 to 42
- cath_topo: int32 [32], P(('dp', 'fsdp')), may hold values from 0 to 1471
- res_counts: int32 [32], P(('dp', 'fsdp')), may hold values from 256 to 512, as said below
- chain_ids: int32 [32, 512], P(('dp', 'fsdp')), may hold values from 0 to 1, as said below
- break_mask: int32 [32, 512], P(('dp', 'fsdp')), may hold values from 0 to 1, as said below
- w_ada: bfloat16 [768, 4608], P('fsdp'), may hold values from -0.21875 to 0.21875
- w_qkv: bfloat16 [768, 2304], P('fsdp'), may hold values from -0.21875 to 0.21875
- w_out: bfloat16 [768, 768], P('fsdp'), may hold values from -1.5 to 1.5
- w_gate: bfloat16 [768, 3072], P('fsdp'), may hold values from -0.21875 to 0.21875
- w_up: bfloat16 [768, 3072], P('fsdp'), may hold values from -0.21875 to 0.21875
- w_down: bfloat16 [3072, 768], P(None, 'fsdp'), may hold values from -0.21875 to 0.21875
- table_class: bfloat16 [5, 768], P(None, 'fsdp'), may hold values from -3 to 3
- table_arch: bfloat16 [43, 768], P(None, 'fsdp'), may hold values from -3 to 3
- table_topo: bfloat16 [1472, 768], P(None, 'fsdp'), may hold values from -3 to 3
- break_vec: bfloat16 [768], P('fsdp'), may hold values from -4 to 4
- pair_table: bfloat16 [128, 256], P(None, 'fsdp'), may hold values from -5 to 5
- pair_proj: bfloat16 [256, 12], P('fsdp'), may hold values from -0.375 to 0.375
Outputs:
- output: bfloat16 [32, 512, 768], P(('dp', 'fsdp'))
- d_tokens: bfloat16 [32, 512, 768], P(('dp', 'fsdp'))
- grad_ada: float32 [768, 4608], P('fsdp')
- grad_qkv: float32 [768, 2304], P('fsdp')
- grad_out: float32 [768, 768], P('fsdp')
- grad_gate: float32 [768, 3072], P('fsdp')
- grad_up: float32 [768, 3072], P('fsdp')
- grad_down: float32 [3072, 768], P(None, 'fsdp')
- grad_class: float32 [5, 768], P(None, 'fsdp')
- grad_arch: float32 [43, 768], P(None, 'fsdp')
- grad_topo: float32 [1472, 768], P(None, 'fsdp')
- grad_break: float32 [768], P('fsdp')
- grad_pair: float32 [128, 256], P(None, 'fsdp')
- grad_proj: float32 [256, 12], P('fsdp')
The draws below stay inside these ranges and needn't reach their ends.
Inputs may be any that keep to these rules, and one draw needn't show every extreme that they name: `res_counts`: keys at or past a window's count are padding. `chain_ids`: 0 up to a window's second chain, 1 from it on; never falls along a window. `break_mask`: 1 at the first residue of a window's second chain and after gaps in a crop, else 0; slot 0 is never marked.
All inputs are finite; a program needn't handle non-finite values.
Results may differ from the reference program's by a relative error of at most 0.015.
Values may be sent and summed in bfloat16 or wider, within the bound.
A program may use at most 256 MiB of HBM per device.

```python
import math
import jax
import jax.numpy as jnp
from jax import lax

D = 768
HEADS = 12
FF = 3072
PAIR = 256
PAIR_CLS = 128
CATH_C = 5
CATH_A = 43
CATH_T = 1472
L = 512
WINDOWS = 32


def chain_layout(key):
    base = jax.random.fold_in(key, 7)
    split_key, choose_key, gap_key = jax.random.split(base, 3)
    starts = jax.random.randint(split_key, (WINDOWS,), L // 4, 3 * L // 4)
    two_chains = jax.random.randint(choose_key, (WINDOWS,), 0, 2).at[0].set(1)
    starts = jnp.where(two_chains == 1, starts, L)
    position = jnp.arange(L, dtype=jnp.int32)
    chains = (position[None, :] >= starts[:, None]).astype(jnp.int32)
    gaps = (jax.random.randint(gap_key, (WINDOWS, L), 0, 32) == 0) & (position[None, :] > 0)
    breaks = ((position[None, :] == starts[:, None]) | gaps).astype(jnp.int32)
    return (chains, breaks)


def draw_chain_ids(key, part):
    return chain_layout(key)[0]


def draw_break_mask(key, part):
    return chain_layout(key)[1]


def draw_res_counts(key, part):
    counts = jax.random.randint(jax.random.fold_in(key, 3), (WINDOWS,), L // 2, L + 1)
    return counts.at[0].set(L).at[1].set(L // 2).astype(jnp.int32)


def with_ends(array, rng, least, top_value):
    place = [jax.random.randint(jax.random.fold_in(rng, axis), (), 0, length) for axis, length in enumerate(array.shape)]
    widest = array.shape.index(max(array.shape))
    beside = place[:widest] + [(place[widest] + 1) % array.shape[widest]] + place[widest + 1:]
    return array.at[tuple(place)].set(least).at[tuple(beside)].set(top_value)


def raised(values, own_key, source, target, shards_of, factor):
    owner, partner = [(jnp.arange(values.shape[dim]) // (values.shape[dim] // shards_of)).reshape([-1 if axis == dim else 1 for axis in range(values.ndim)]) for dim in (source, target)]
    chosen = jax.random.permutation(own_key, shards_of)[partner]
    strong = (owner == chosen) | (owner == (partner + shards_of // 2) % shards_of)
    return jnp.where(strong, factor * values, values)


def block_levels(rng, dims, pieces, low, top_value):
    gain, own = 1.0, jax.random.fold_in(rng, 6)
    for dim, blocks in pieces:
        draws = jnp.exp(jax.random.uniform(jax.random.fold_in(own, dim), (blocks,), jnp.float32, low / len(pieces), top_value / len(pieces)))
        gain = gain * jnp.repeat(draws, dims[dim] // blocks).reshape([-1 if axis == dim else 1 for axis in range(len(dims))])
    return gain


def scatter_about(own_key, extent, deviation, most, pieces=(), held_as=jnp.bfloat16):
    values = jax.random.normal(own_key, extent, jnp.float32) * deviation
    if len(pieces) > 0:
        values = block_levels(own_key, extent, pieces, -0.22, 0.18) * values
    return jnp.clip(values, min=-most, max=most).astype(held_as)


def bell_draw_with(own_key, shape, width, most, cuts, heavy, kind=jnp.bfloat16):
    array = width * jax.random.normal(own_key, shape, jnp.float32)
    if cuts:
        array = array * block_levels(own_key, shape, cuts, -0.22, 0.18)
    return jnp.clip(raised(array, jax.random.fold_in(own_key, 3), *heavy), -most, most).astype(kind)


def setup_inputs(seed: int = 0) -> dict:
    key_list = jax.random.split(jax.random.key(seed), 22)
    return {
        "tokens": scatter_about(key_list[0], (WINDOWS, L, D), 1.0, 6.0, ((0, 32),)),
        "cotangent": bell_draw_with(key_list[1], (WINDOWS, L, D), 1.0, 6.0, ((0, 32),), (0, 2, 32, 2.75)),
        "time_embed": scatter_about(key_list[2], (WINDOWS, D), 0.5, 3.0, ((0, 32),)),
        "cath_class": with_ends(jax.random.randint(key_list[3], (WINDOWS,), 0, CATH_C), jax.random.fold_in(key_list[3], 1), 0, CATH_C - 1).astype(jnp.int32),
        "cath_arch": with_ends(jax.random.randint(key_list[4], (WINDOWS,), 0, CATH_A), jax.random.fold_in(key_list[4], 1), 0, CATH_A - 1).astype(jnp.int32),
        "cath_topo": with_ends(jax.random.randint(key_list[5], (WINDOWS,), 0, CATH_T), jax.random.fold_in(key_list[5], 1), 0, CATH_T - 1).astype(jnp.int32),
        "res_counts": draw_res_counts(jax.random.fold_in(key_list[21], 71), 0),
        "chain_ids": draw_chain_ids(jax.random.fold_in(key_list[21], 71), 0),
        "break_mask": draw_break_mask(jax.random.fold_in(key_list[21], 71), 0),
        "w_ada": scatter_about(key_list[9], (D, 6 * D), D ** -0.5, 0.21875, ((0, 16),)),
        "w_qkv": scatter_about(key_list[10], (D, 3 * D), D ** -0.5, 0.21875, ((0, 16),)),
        "w_out": scatter_about(key_list[11], (D, D), (D // 48) ** -0.5, 1.5, ((0, 16),)),
        "w_gate": scatter_about(key_list[12], (D, FF), D ** -0.5, 0.21875, ((0, 16),)),
        "w_up": scatter_about(key_list[13], (D, FF), D ** -0.5, 0.21875, ((0, 16),)),
        "w_down": scatter_about(key_list[14], (FF, D), (FF // 4) ** -0.5, 0.21875, ((1, 16),)),
        "table_class": scatter_about(key_list[15], (CATH_C, D), 0.5, 3.0, ((1, 16),)),
        "table_arch": scatter_about(key_list[16], (CATH_A, D), 0.5, 3.0, ((1, 16),)),
        "table_topo": scatter_about(key_list[17], (CATH_T, D), 0.5, 3.0, ((1, 16),)),
        "break_vec": scatter_about(key_list[18], (D,), 1.0, 4.0, ((0, 16),)),
        "pair_table": scatter_about(key_list[19], (PAIR_CLS, PAIR), 1.0, 5.0, ((1, 16),)),
        "pair_proj": scatter_about(key_list[20], (PAIR, HEADS), PAIR ** -0.5, 0.375, ((0, 16),)),
    }


@jax.custom_vjp
def low(v):
    return lax.optimization_barrier(v.astype(jnp.bfloat16)).astype(jnp.float32)

@jax.custom_vjp
def low_back(v):
    return v

def low_keep(v):
    return (low(v), None)

def low_pass(kept, grad):
    return (grad,)

def back_keep(v):
    return (v, None)

def back_low(kept, grad):
    return (low(grad),)
low.defvjp(low_keep, low_pass)
low_back.defvjp(back_keep, back_low)
epsilon = 1e-05
highest = lax.Precision.HIGHEST

def normalize(values):
    centred = values - lax.optimization_barrier(jnp.mean(values, axis=-1, keepdims=True))
    return centred * lax.rsqrt(lax.optimization_barrier(jnp.mean(centred * centred, axis=-1, keepdims=True)) + epsilon)

def pair_classes(chains, class_count):
    length = chains.shape[-1]
    position = jnp.arange(length, dtype=jnp.int32)
    reach = class_count // 2 - 1
    offset = jnp.clip(position[:, None] - position[None, :], -reach, reach) + reach
    same_chain = chains[..., :, None] == chains[..., None, :]
    return jnp.where(same_chain, offset, class_count - 1)

def reference(tokens, cotangent, time_embed, cath_class, cath_arch, cath_topo, res_counts, chain_ids, break_mask, w_ada, w_qkv, w_out, w_gate, w_up, w_down, table_class, table_arch, table_topo, break_vec, pair_table, pair_proj):
    float_args = (w_ada, w_qkv, w_out, w_gate, w_up, w_down, table_class, table_arch, table_topo, break_vec, pair_table, pair_proj)
    weights = tuple((source.astype(jnp.float32) for source in float_args))
    group_size = math.gcd(WINDOWS, max(1, 4096 // L))
    steps_count = WINDOWS // group_size

    def run_group(layer_w, bias_table, inputs):
        qkv_w, out_w, gate_w, up_w, down_w, break_w = layer_w
        resid_in, ada_rows, chains, counts, breaks = inputs
        shift_one, scale_one, gate_one, shift_two, scale_two, gate_two = jnp.split(ada_rows[:, None, :], 6, axis=2)
        h_one = low(normalize(resid_in) * (1.0 + scale_one) + shift_one + breaks.astype(jnp.float32)[:, :, None] * break_w)
        proj_qkv = low_back(low(jnp.einsum('gld,de->gle', h_one, qkv_w, precision=highest)))
        head_count = bias_table.shape[1]
        shaped = proj_qkv.reshape(group_size, L, 3, head_count, D // head_count)
        queries, key_rows, value_rows = (shaped[:, :, 0], shaped[:, :, 1], shaped[:, :, 2])
        pair_bias_map = jnp.moveaxis(bias_table[pair_classes(chains, bias_table.shape[0])], -1, 1)
        scores = jnp.einsum('gqhd,gkhd->ghqk', queries, key_rows, precision=highest) * (D // head_count) ** (-0.5)
        scores = scores + pair_bias_map
        live_keys = jnp.arange(L, dtype=jnp.int32)[None, :] < counts[:, None]
        scores = low_back(jnp.where(live_keys[:, None, None, :], scores, -1e+30))
        attn_probs = low(jax.nn.softmax(scores, axis=-1))
        attended = jnp.einsum('ghqk,gkhd->gqhd', attn_probs, value_rows, precision=highest)
        attended = low_back(low(attended.reshape(group_size, L, D)))
        attn_proj = low_back(jnp.einsum('gld,de->gle', attended, out_w, precision=highest))
        middle = resid_in + gate_one * attn_proj
        h_two = low(normalize(middle) * (1.0 + scale_two) + shift_two)
        gate_pre = low_back(jnp.einsum('gld,df->glf', h_two, gate_w, precision=highest))
        up_pre = low_back(jnp.einsum('gld,df->glf', h_two, up_w, precision=highest))
        activated = low(jax.nn.silu(gate_pre) * up_pre)
        ffn_out = low_back(jnp.einsum('glf,fd->gld', activated, down_w, precision=highest))
        return middle + gate_two * ffn_out
    checked = jax.checkpoint(run_group)

    def full_forward(resid_all, weights):
        ada_w, qkv_w, out_w, gate_w, up_w, down_w, class_t, arch_t, topo_t, break_w, pair_t, proj_w = weights
        pre_act = time_embed.astype(jnp.float32) + class_t[cath_class] + arch_t[cath_arch] + topo_t[cath_topo]
        ada_rows = low_back(jnp.dot(low(jax.nn.silu(pre_act)), ada_w, precision=highest))
        bias_table = low(jnp.dot(low(normalize(pair_t)), proj_w, precision=highest))
        layer_w = (qkv_w, out_w, gate_w, up_w, down_w, break_w)

        def map_step(inputs):
            return checked(layer_w, bias_table, inputs)
        inputs = (resid_all.reshape(steps_count, group_size, L, D), ada_rows.reshape(steps_count, group_size, 6 * D), chain_ids.reshape(steps_count, group_size, L), res_counts.reshape(steps_count, group_size), break_mask.reshape(steps_count, group_size, L))
        outputs = lax.map(map_step, inputs)
        return outputs.reshape(WINDOWS, L, D)
    output, pullback = jax.vjp(full_forward, tokens.astype(jnp.float32), weights)
    d_tokens, grads = pullback(cotangent.astype(jnp.float32))
    return (output.astype(jnp.bfloat16), d_tokens.astype(jnp.bfloat16), grads[0], grads[1], grads[2], grads[3], grads[4], grads[5], grads[6], grads[7], grads[8], grads[9], grads[10], grads[11])
```

```python
from functools import partial

import jax
import jax.numpy as jnp
from jax import lax
from jax.experimental import pallas as pl
from jax.experimental.pallas import tpu as pltpu
from jax.sharding import PartitionSpec as P

epsilon = 1e-05
highest = lax.Precision.HIGHEST


def matmul(left, right):
    return jnp.dot(left, right, preferred_element_type=jnp.float32)


def matmul_t(left, right):
    return lax.dot_general(
        left, right, (((1,), (1,)), ((), ())), preferred_element_type=jnp.float32
    )


def matmul_tn(left, right):
    return lax.dot_general(
        left, right, (((0,), (0,)), ((), ())), preferred_element_type=jnp.float32
    )


def exact_tn(left, right):
    return lax.dot_general(
        left, right, (((0,), (0,)), ((), ())), precision=highest, preferred_element_type=jnp.float32
    )


def exact_nt(left, right):
    return lax.dot_general(
        left, right, (((1,), (1,)), ((), ())), precision=highest, preferred_element_type=jnp.float32
    )


def normalize(values):
    centred = values - jnp.mean(values, axis=-1, keepdims=True)
    inv_std = lax.rsqrt(jnp.mean(centred * centred, axis=-1, keepdims=True) + epsilon)
    return (centred * inv_std, inv_std)


def normalize_back(normed, inv_std, grad):
    return inv_std * (
        grad
        - jnp.mean(grad, axis=-1, keepdims=True)
        - normed * jnp.mean(grad * normed, axis=-1, keepdims=True)
    )


def pair_classes(chain_row, class_count):
    length = chain_row.shape[0]
    position = jnp.arange(length, dtype=jnp.int32)
    reach = class_count // 2 - 1
    offset = jnp.clip(position[:, None] - position[None, :], -reach, reach) + reach
    return jnp.where(chain_row[:, None] == chain_row[None, :], offset, class_count - 1)


def pair_bias(classes, bias_table):
    length = classes.shape[0]
    step_rows = min(length, 128)
    class_ids = jnp.arange(bias_table.shape[0], dtype=jnp.int32)

    def one_block(row_block):
        onehot = (row_block[:, :, None] == class_ids).astype(jnp.bfloat16)
        return jnp.einsum("ijc,ch->hij", onehot, bias_table, preferred_element_type=jnp.float32)

    pieces = lax.map(one_block, classes.reshape(length // step_rows, step_rows, length))
    return jnp.transpose(pieces, (1, 0, 2, 3)).reshape(bias_table.shape[1], length, length)


def pair_bias_back(classes, d_scores, class_count):
    head_count, length = (d_scores.shape[0], d_scores.shape[1])
    step_rows = min(length, 128)
    block_count = length // step_rows
    class_ids = jnp.arange(class_count, dtype=jnp.int32)
    grad_blocks = jnp.transpose(
        d_scores.reshape(head_count, block_count, step_rows, length), (1, 0, 2, 3)
    )

    def add_block(running, inputs):
        row_block, grad_block = inputs
        onehot = (row_block[:, :, None] == class_ids).astype(jnp.bfloat16)
        return (
            running
            + jnp.einsum("hij,ijc->ch", grad_block, onehot, preferred_element_type=jnp.float32),
            None,
        )

    start = jnp.zeros((class_count, head_count), jnp.float32)
    summed, unused = lax.scan(
        add_block, start, (classes.reshape(block_count, step_rows, length), grad_blocks)
    )
    return summed


def split_heads(qkv_win, head_count):
    length, triple = qkv_win.shape
    shaped = qkv_win.reshape(length, 3, head_count, triple // (3 * head_count))
    return (shaped[:, 0], shaped[:, 1], shaped[:, 2])


def window_scores(qkv_win, chain_row, count_win, bias_table):
    length = qkv_win.shape[0]
    queries, key_rows, value_rows = split_heads(qkv_win, bias_table.shape[1])
    classes = pair_classes(chain_row, bias_table.shape[0])
    score_scale = queries.shape[-1] ** (-0.5)
    scores = (
        jnp.einsum("qhd,khd->hqk", queries, key_rows, preferred_element_type=jnp.float32)
        * score_scale
    )
    scores = scores + pair_bias(classes, bias_table)
    live_keys = jnp.arange(length, dtype=jnp.int32) < count_win
    scores = jnp.where(live_keys[None, None, :], scores, -1e30)
    return (scores, queries, key_rows, value_rows, classes, score_scale)


def attend(inputs, bias_table):
    qkv_win, chain_row, count_win = inputs
    scores, queries, key_rows, value_rows, classes, score_scale = window_scores(
        qkv_win, chain_row, count_win, bias_table
    )
    highest_score = jnp.max(scores, axis=-1, keepdims=True)
    exponent = jnp.exp(scores - highest_score)
    row_total = jnp.sum(exponent, axis=-1, keepdims=True)
    attn_probs = (exponent / row_total).astype(jnp.bfloat16)
    attended = jnp.einsum(
        "hqk,khd->qhd", attn_probs, value_rows, preferred_element_type=jnp.float32
    )
    attended = attended.reshape(qkv_win.shape[0], -1).astype(jnp.bfloat16)
    return (attended, (highest_score + jnp.log(row_total))[:, :, 0])


def attend_back(inputs, bias_table):
    qkv_win, chain_row, count_win, log_total, d_attended = inputs
    scores, queries, key_rows, value_rows, classes, score_scale = window_scores(
        qkv_win, chain_row, count_win, bias_table
    )
    attn_probs = jnp.exp(scores - log_total[:, :, None])
    d_heads = d_attended.reshape(queries.shape)
    d_probs = jnp.einsum("qhd,khd->hqk", d_heads, value_rows, preferred_element_type=jnp.float32)
    d_scores = attn_probs * (d_probs - jnp.sum(attn_probs * d_probs, axis=-1, keepdims=True))
    d_scores = d_scores.astype(jnp.bfloat16)
    d_values = jnp.einsum(
        "hqk,qhd->khd", attn_probs.astype(jnp.bfloat16), d_heads, preferred_element_type=jnp.float32
    )
    d_queries = (
        jnp.einsum("hqk,khd->qhd", d_scores, key_rows, preferred_element_type=jnp.float32)
        * score_scale
    )
    d_keys = (
        jnp.einsum("hqk,qhd->khd", d_scores, queries, preferred_element_type=jnp.float32)
        * score_scale
    )
    d_qkv = (
        jnp.stack([d_queries, d_keys, d_values], axis=1)
        .reshape(qkv_win.shape[0], -1)
        .astype(jnp.bfloat16)
    )
    return (d_qkv, pair_bias_back(classes, d_scores, bias_table.shape[0]))


def forward(
    tokens,
    time_embed,
    cath_class,
    cath_arch,
    cath_topo,
    res_counts,
    chain_ids,
    break_mask,
    attn_set,
    mlp_set,
):
    ada_all, qkv_all, out_all, class_all, arch_all, topo_all, break_all, pair_all, proj_all = (
        attn_set
    )
    gate_all, up_all, down_all = mlp_set
    windows, length, model_width = tokens.shape
    row_count = windows * length
    pre_act = time_embed.astype(jnp.float32)
    onehots = []
    for labels, lookup in ((cath_class, class_all), (cath_arch, arch_all), (cath_topo, topo_all)):
        onehot = (labels[:, None] == jnp.arange(lookup.shape[0], dtype=jnp.int32)[None, :]).astype(
            jnp.bfloat16
        )
        pre_act = pre_act + matmul(onehot, lookup)
        onehots.append(onehot)
    cond_low = jax.nn.silu(pre_act).astype(jnp.bfloat16)
    ada_rows = matmul(cond_low, ada_all)
    shift_one, scale_one, gate_one, shift_two, scale_two, gate_two = [
        portion[:, None, :] for portion in jnp.split(ada_rows, 6, axis=1)
    ]
    resid_in = tokens.astype(jnp.float32)
    normed_one, inv_one = normalize(resid_in)
    break_rows = break_mask.astype(jnp.float32)[:, :, None]
    h_one_low = (
        normed_one * (1.0 + scale_one) + shift_one + break_rows * break_all.astype(jnp.float32)
    )
    h_one_low = h_one_low.astype(jnp.bfloat16).reshape(row_count, model_width)
    proj_qkv = (
        matmul(h_one_low, qkv_all).astype(jnp.bfloat16).reshape(windows, length, 3 * model_width)
    )
    pair_normed, pair_inv = normalize(pair_all.astype(jnp.float32))
    pair_low = pair_normed.astype(jnp.bfloat16)
    bias_table = matmul(pair_low, proj_all).astype(jnp.bfloat16)
    attended, log_total = lax.map(
        partial(attend, bias_table=bias_table), (proj_qkv, chain_ids, res_counts)
    )
    attended_rows = attended.reshape(row_count, model_width)
    attn_proj = matmul(attended_rows, out_all).reshape(windows, length, model_width)
    middle = resid_in + gate_one * attn_proj
    normed_two, inv_two = normalize(middle)
    h_two_low = (
        (normed_two * (1.0 + scale_two) + shift_two)
        .astype(jnp.bfloat16)
        .reshape(row_count, model_width)
    )
    gate_pre = matmul(h_two_low, gate_all)
    up_pre = matmul(h_two_low, up_all)
    activated = (jax.nn.silu(gate_pre) * up_pre).astype(jnp.bfloat16)
    ffn_out = matmul(activated, down_all).reshape(windows, length, model_width)
    output = middle + gate_two * ffn_out
    return {
        "output": output,
        "pre_act": pre_act,
        "onehots": onehots,
        "cond_low": cond_low,
        "scales": (scale_one, gate_one, scale_two, gate_two),
        "normed_one": normed_one,
        "inv_one": inv_one,
        "break_rows": break_rows,
        "h_one_low": h_one_low,
        "proj_qkv": proj_qkv,
        "pair_normed": pair_normed,
        "pair_inv": pair_inv,
        "pair_low": pair_low,
        "bias_table": bias_table,
        "log_total": log_total,
        "attended_rows": attended_rows,
        "attn_proj": attn_proj,
        "normed_two": normed_two,
        "inv_two": inv_two,
        "h_two_low": h_two_low,
        "gate_pre": gate_pre,
        "up_pre": up_pre,
        "activated": activated,
        "ffn_out": ffn_out,
    }


def shards(
    tokens,
    cotangent,
    time_embed,
    cath_class,
    cath_arch,
    cath_topo,
    res_counts,
    chain_ids,
    break_mask,
    w_ada,
    w_qkv,
    w_out,
    w_gate,
    w_up,
    w_down,
    table_class,
    table_arch,
    table_topo,
    break_vec,
    pair_table,
    pair_proj,
):
    attn_set = (
        lax.all_gather(w_ada, "fsdp", axis=0, tiled=True),
        lax.all_gather(w_qkv, "fsdp", axis=0, tiled=True),
        lax.all_gather(w_out, "fsdp", axis=0, tiled=True),
        lax.all_gather(table_class, "fsdp", axis=1, tiled=True),
        lax.all_gather(table_arch, "fsdp", axis=1, tiled=True),
        lax.all_gather(table_topo, "fsdp", axis=1, tiled=True),
        lax.all_gather(break_vec, "fsdp", axis=0, tiled=True),
        lax.all_gather(pair_table, "fsdp", axis=1, tiled=True),
        lax.all_gather(pair_proj, "fsdp", axis=0, tiled=True),
    )
    mlp_set = (
        lax.all_gather(w_gate, "fsdp", axis=0, tiled=True),
        lax.all_gather(w_up, "fsdp", axis=0, tiled=True),
        lax.all_gather(w_down, "fsdp", axis=1, tiled=True),
    )
    saved = forward(
        tokens,
        time_embed,
        cath_class,
        cath_arch,
        cath_topo,
        res_counts,
        chain_ids,
        break_mask,
        attn_set,
        mlp_set,
    )
    output = saved["output"].astype(jnp.bfloat16)
    attn_set = (
        lax.all_gather(w_ada, "fsdp", axis=0, tiled=True),
        lax.all_gather(w_qkv, "fsdp", axis=0, tiled=True),
        lax.all_gather(w_out, "fsdp", axis=0, tiled=True),
        lax.all_gather(table_class, "fsdp", axis=1, tiled=True),
        lax.all_gather(table_arch, "fsdp", axis=1, tiled=True),
        lax.all_gather(table_topo, "fsdp", axis=1, tiled=True),
        lax.all_gather(break_vec, "fsdp", axis=0, tiled=True),
        lax.all_gather(pair_table, "fsdp", axis=1, tiled=True),
        lax.all_gather(pair_proj, "fsdp", axis=0, tiled=True),
    )
    mlp_set = (
        lax.all_gather(w_gate, "fsdp", axis=0, tiled=True),
        lax.all_gather(w_up, "fsdp", axis=0, tiled=True),
        lax.all_gather(w_down, "fsdp", axis=1, tiled=True),
    )
    saved = forward(
        tokens,
        time_embed,
        cath_class,
        cath_arch,
        cath_topo,
        res_counts,
        chain_ids,
        break_mask,
        attn_set,
        mlp_set,
    )
    ada_all, qkv_all, out_all, class_all, arch_all, topo_all, break_all, pair_all, proj_all = (
        attn_set
    )
    gate_all, up_all, down_all = mlp_set
    windows, length, model_width = tokens.shape
    row_count = windows * length
    scale_one, gate_one, scale_two, gate_two = saved["scales"]
    grad_rows = cotangent.astype(jnp.float32)
    ffn_out = saved["ffn_out"]
    d_ffn = (gate_two * grad_rows).astype(jnp.bfloat16).reshape(row_count, model_width)
    d_gate_two = jnp.sum(grad_rows * ffn_out, axis=1)
    grad_down = matmul_tn(saved["activated"], d_ffn)
    d_act = matmul_t(d_ffn, down_all)
    gate_pre, up_pre = (saved["gate_pre"], saved["up_pre"])
    sigma = jax.nn.sigmoid(gate_pre)
    d_gate_pre = (d_act * up_pre * sigma * (1.0 + gate_pre * (1.0 - sigma))).astype(jnp.bfloat16)
    d_up_pre = (d_act * gate_pre * sigma).astype(jnp.bfloat16)
    h_two_low = saved["h_two_low"]
    grad_gate = matmul_tn(h_two_low, d_gate_pre)
    grad_up = matmul_tn(h_two_low, d_up_pre)
    d_h_two = (matmul_t(d_gate_pre, gate_all) + matmul_t(d_up_pre, up_all)).reshape(
        windows, length, model_width
    )
    normed_two = saved["normed_two"]
    d_scale_two = jnp.sum(d_h_two * normed_two, axis=1)
    d_shift_two = jnp.sum(d_h_two, axis=1)
    d_middle = grad_rows + normalize_back(normed_two, saved["inv_two"], d_h_two * (1.0 + scale_two))
    d_gate_one = jnp.sum(d_middle * saved["attn_proj"], axis=1)
    d_attn = (gate_one * d_middle).astype(jnp.bfloat16).reshape(row_count, model_width)
    grad_out = matmul_tn(saved["attended_rows"], d_attn)
    d_attended = (
        matmul_t(d_attn, out_all).astype(jnp.bfloat16).reshape(windows, length, model_width)
    )
    bias_table = saved["bias_table"]
    d_qkv, bias_grads = lax.map(
        partial(attend_back, bias_table=bias_table),
        (saved["proj_qkv"], chain_ids, res_counts, saved["log_total"], d_attended),
    )
    d_bias_table = jnp.sum(bias_grads, axis=0)
    d_qkv = d_qkv.reshape(row_count, 3 * model_width)
    h_one_low = saved["h_one_low"]
    grad_qkv = matmul_tn(h_one_low, d_qkv)
    d_h_one = matmul_t(d_qkv, qkv_all).reshape(windows, length, model_width)
    normed_one = saved["normed_one"]
    d_scale_one = jnp.sum(d_h_one * normed_one, axis=1)
    d_shift_one = jnp.sum(d_h_one, axis=1)
    grad_break = jnp.sum(d_h_one * saved["break_rows"], axis=(0, 1))
    d_tokens = d_middle + normalize_back(normed_one, saved["inv_one"], d_h_one * (1.0 + scale_one))
    d_ada = jnp.concatenate(
        [d_shift_one, d_scale_one, d_gate_one, d_shift_two, d_scale_two, d_gate_two], axis=1
    ).astype(jnp.bfloat16)
    grad_ada = matmul_tn(saved["cond_low"], d_ada)
    pre_act = saved["pre_act"]
    sigma_pre = jax.nn.sigmoid(pre_act)
    d_pre = matmul_t(d_ada, ada_all) * sigma_pre * (1.0 + pre_act * (1.0 - sigma_pre))
    onehots = saved["onehots"]
    grad_class = exact_tn(onehots[0].astype(jnp.float32), d_pre)
    grad_arch = exact_tn(onehots[1].astype(jnp.float32), d_pre)
    grad_topo = exact_tn(onehots[2].astype(jnp.float32), d_pre)
    grad_proj = exact_tn(saved["pair_low"].astype(jnp.float32), d_bias_table)
    d_pair_normed = exact_nt(d_bias_table, proj_all.astype(jnp.float32))
    grad_pair = normalize_back(saved["pair_normed"], saved["pair_inv"], d_pair_normed)
    attn_parts = (
        lax.psum_scatter(grad_ada, "fsdp", scatter_dimension=0, tiled=True),
        lax.psum_scatter(grad_qkv, "fsdp", scatter_dimension=0, tiled=True),
        lax.psum_scatter(grad_out, "fsdp", scatter_dimension=0, tiled=True),
        lax.psum_scatter(grad_class, "fsdp", scatter_dimension=1, tiled=True),
        lax.psum_scatter(grad_arch, "fsdp", scatter_dimension=1, tiled=True),
        lax.psum_scatter(grad_topo, "fsdp", scatter_dimension=1, tiled=True),
        lax.psum_scatter(grad_break, "fsdp", scatter_dimension=0, tiled=True),
        lax.psum_scatter(grad_pair, "fsdp", scatter_dimension=1, tiled=True),
        lax.psum_scatter(grad_proj, "fsdp", scatter_dimension=0, tiled=True),
    )
    mlp_parts = (
        lax.psum_scatter(grad_gate, "fsdp", scatter_dimension=0, tiled=True),
        lax.psum_scatter(grad_up, "fsdp", scatter_dimension=0, tiled=True),
        lax.psum_scatter(grad_down, "fsdp", scatter_dimension=1, tiled=True),
    )
    owned = (
        lax.psum(attn_parts[0].astype(jnp.bfloat16), "dp").astype(jnp.float32),
        lax.psum(attn_parts[1].astype(jnp.bfloat16), "dp").astype(jnp.float32),
        lax.psum(attn_parts[2].astype(jnp.bfloat16), "dp").astype(jnp.float32),
        lax.psum(mlp_parts[0].astype(jnp.bfloat16), "dp").astype(jnp.float32),
        lax.psum(mlp_parts[1].astype(jnp.bfloat16), "dp").astype(jnp.float32),
        lax.psum(mlp_parts[2].astype(jnp.bfloat16), "dp").astype(jnp.float32),
        lax.psum(attn_parts[3].astype(jnp.bfloat16), "dp").astype(jnp.float32),
        lax.psum(attn_parts[4].astype(jnp.bfloat16), "dp").astype(jnp.float32),
        lax.psum(attn_parts[5].astype(jnp.bfloat16), "dp").astype(jnp.float32),
        lax.psum(attn_parts[6].astype(jnp.bfloat16), "dp").astype(jnp.float32),
        lax.psum(attn_parts[7].astype(jnp.bfloat16), "dp").astype(jnp.float32),
        lax.psum(attn_parts[8].astype(jnp.bfloat16), "dp").astype(jnp.float32),
    )
    return (
        output,
        d_tokens.astype(jnp.bfloat16),
        owned[0],
        owned[1],
        owned[2],
        owned[3],
        owned[4],
        owned[5],
        owned[6],
        owned[7],
        owned[8],
        owned[9],
        owned[10],
        owned[11],
    )


mesh_ids = pl.DeviceIdType.MESH
f32 = jnp.float32
b16 = jnp.bfloat16
core_count = 2
chip_count = 8
shard_rows = 48
chunk_cols = 3072
chunk_count = 4
side_cols = 768
ring_cols = 2304
job_cols = 384
jobs_in_chunk = 6
job_count = 24
ahead = 3
gather_stride = 2
scatter_stride = 2
grad_buffers = 3
plan = (1, 1, 1, 1, 1, 1, 1, 1, 1, 1, 5)
ahead_plan = (2, 2, 2, 2, 2)


def dot_nn(left, right):
    return jnp.dot(left, right, preferred_element_type=f32)


def dot_nt(left, right):
    return lax.dot_general(left, right, (((1,), (1,)), ((), ())), preferred_element_type=f32)


def dot_tn(left, right):
    return lax.dot_general(left, right, (((0,), (0,)), ((), ())), preferred_element_type=f32)


def on(condition, body):
    if isinstance(condition, bool):
        if condition:
            body()
    else:
        pl.when(condition)(body)


def both(first, second):
    if isinstance(first, bool) and isinstance(second, bool):
        return first and second
    return jnp.logical_and(first, second)


def quot(value, by):
    return value // by if isinstance(value, int) else lax.div(value, by)


def modulo(value, by):
    return value % by if isinstance(value, int) else lax.rem(value, by)


def aligned(value, by=128):
    return value if isinstance(value, int) else pl.multiple_of(value, by)


class Place:
    def __init__(self):
        self.x = lax.axis_index("dp")
        self.f = lax.axis_index("fsdp")
        self.me = self.x * 16 + self.f
        self.c = lax.rem(self.f, 2)
        self.cy = lax.div(self.f, 2)
        y = lax.rem(self.cy, 2)
        z = lax.div(self.cy, 2)
        self.p = z * (1 - y) + (7 - z) * y

    def chip(self, position):
        position = lax.rem(position + 16, 8)
        half = lax.div(position, 4)
        return 2 * position * (1 - half) + (15 - 2 * position) * half

    def ring_id(self, position):
        return (self.x, self.chip(position) * 2 + self.c)

    def plane_id(self):
        return (1 - self.x, self.f)

    def core_id(self):
        return (self.x, self.cy * 2 + 1 - self.c)


def greet_all(at):
    barrier = pltpu.get_barrier_semaphore()

    @pl.loop(1, 32)
    def _(step):
        other = lax.rem(at.me + step, 32)
        pl.semaphore_signal(
            barrier,
            inc=1,
            device_id=(lax.div(other, 16), lax.rem(other, 16)),
            device_id_type=mesh_ids,
        )

    pl.semaphore_wait(barrier, 31)


def remote(src, dst, send_sem, recv_sem, device_id):
    return pltpu.make_async_remote_copy(
        src_ref=src,
        dst_ref=dst,
        send_sem=send_sem,
        recv_sem=recv_sem,
        device_id=device_id,
        device_id_type=mesh_ids,
    )


def job_column(at, job):
    chunk = quot(job, jobs_in_chunk)
    inner = modulo(job, jobs_in_chunk)
    base = chunk * chunk_cols + inner * job_cols
    if isinstance(job, int):
        return aligned(base + (at.x * ring_cols if inner < 2 else 0))
    side = 1 - jnp.minimum(lax.div(inner, 2), 1)
    return aligned(base + side * at.x * ring_cols)


class Gather:
    def __init__(self, at, packed, held, sems):
        self.at = at
        self.packed = packed
        self.held = held
        (
            self.ring_send,
            self.ring_recv,
            self.side_send,
            self.side_recv,
            self.core_send,
            self.core_recv,
        ) = sems

    def ring(self, job, step, way, hop):
        at = self.at
        sign = 1 - 2 * way
        column = pl.ds(job_column(at, job), job_cols)
        block = self.held.at[at.chip(at.p - (step + hop) * sign), at.c, :, column]
        src = self.packed.at[:, column] if step == 0 and hop == 0 else block
        return remote(
            src,
            block,
            self.ring_send.at[job, step, way],
            self.ring_recv.at[job, step, way],
            at.ring_id(at.p + sign),
        )

    def relay(self, job, step, way):
        at = self.at
        sign = 1 - 2 * way
        column = pl.ds(job_column(at, job), job_cols)
        block = self.held.at[at.chip(at.p - (step + 1) * sign), at.c, :, column]
        self.pass_on(block, block, job)

    def pass_on(self, src, dst, job):
        at = self.at
        chunk = quot(job, jobs_in_chunk)
        inner = modulo(job, jobs_in_chunk)
        slot = chunk * 2
        remote(
            src, dst, self.core_send.at[slot], self.core_recv.at[slot], at.core_id()
        ).start()

        def across():
            spot = chunk * 2 + inner
            remote(
                src, dst, self.side_send.at[spot], self.side_recv.at[spot], at.plane_id()
            ).start()

        on(inner < 2, across)

    def side(self, job, mine):
        at = self.at
        chunk = quot(job, jobs_in_chunk)
        inner = modulo(job, jobs_in_chunk)
        owner = at.x if mine else 1 - at.x
        column = aligned(chunk * chunk_cols + inner * job_cols + owner * ring_cols)
        block = self.held.at[:, at.c, :, pl.ds(column, job_cols)]
        slot = chunk * 2 + inner
        return remote(
            block, block, self.side_send.at[slot], self.side_recv.at[slot], at.plane_id()
        )

    def core(self, chunk, part, mine):
        at = self.at
        if part == 0:
            column, width = chunk * chunk_cols + at.x * side_cols, ring_cols
        else:
            column, width = chunk * chunk_cols + (1 - at.x) * ring_cols, side_cols
        row = at.c if mine else 1 - at.c
        block = self.held.at[:, row, :, pl.ds(aligned(column), width)]
        slot = chunk * 2 + part
        return remote(block, block, self.core_send.at[slot], self.core_recv.at[slot], at.core_id())

    def start(self, job):
        self.ring(job, 0, 0, 0).start()
        self.ring(job, 0, 1, 0).start()
        at = self.at
        column = pl.ds(job_column(at, job), job_cols)
        self.pass_on(self.packed.at[:, column], self.held.at[at.cy, at.c, :, column], job)

    def tick(self, tau):
        def valid(job):
            return both(job >= 0, job < job_count)

        for step in (4, 3, 2, 1):
            job = tau - step * gather_stride

            def advance(job=job, step=step):
                if step < 4:
                    ways = (0, 1)
                else:
                    ways = (modulo(job, 2),)
                for way in ways:
                    self.ring(job, step - 1, way, 1).wait_recv()
                if step < 3:
                    self.ring(job, step, 0, 0).start()
                    self.ring(job, step, 1, 0).start()
                elif step == 3:
                    self.ring(job, 3, modulo(job, 2), 0).start()
                for way in ways:
                    self.relay(job, step - 1, way)

            on(valid(job), advance)
        on(valid(tau + ahead), lambda: self.start(tau + ahead))

        late = tau - 4 * gather_stride - jobs_in_chunk

        def side_done():
            chunk = quot(late, jobs_in_chunk)
            self.side(chunk * jobs_in_chunk, False).wait_recv()
            self.side(chunk * jobs_in_chunk + 1, False).wait_recv()
            self.core(chunk, 1, True).start()

        on(both(valid(late), modulo(late + 60, jobs_in_chunk) == 0), side_done)

    def arrive(self, chunk):
        self.core(chunk, 0, False).wait_recv()
        self.core(chunk, 1, False).wait_recv()

    def finish(self):
        @pl.loop(0, job_count)
        def _(job):
            for step in range(3):
                self.ring(job, step, 0, 0).wait_send()
                self.ring(job, step, 1, 0).wait_send()
            self.ring(job, 3, lax.rem(job, 2), 0).wait_send()

        for chunk in range(chunk_count):
            for inner in range(2):
                self.side(chunk * jobs_in_chunk + inner, True).wait_send()
                self.core(chunk, inner, True).wait_send()


def class_map(class_count):
    spot = lax.broadcasted_iota(jnp.int32, (512, class_count), 0)
    spot = jnp.where(spot < 384, spot, spot - 512)
    reach = class_count // 2 - 1
    label = jnp.clip(128 - spot, -reach, reach) + reach
    kind = lax.broadcasted_iota(jnp.int32, (512, class_count), 1)
    return (label == kind).astype(f32).astype(b16)


def forward_kernel(
    packed,
    tokens,
    cotangent,
    first_note,
    pair_note,
    ada_shard,
    tables,
    rows,
    output,
    held_out,
    h_one_out,
    qkv_out,
    probs_out,
    attended_out,
    proj_out,
    middle_out,
    h_two_out,
    gate_out,
    up_out,
    act_out,
    ada_out,
    d_gate_two_out,
    pre_out,
    note_out,
    pair_out,
    held,
    note_in,
    pair_in,
    part_rows,
    part_in,
    normed,
    h_one,
    qkv,
    bias,
    edges,
    probs,
    attended,
    proj,
    middle,
    h_two,
    gate,
    up,
    act,
    total,
    out_low,
    ring_send,
    ring_recv,
    side_send,
    side_recv,
    core_send,
    core_recv,
    note_send,
    note_recv,
    pair_send,
    pair_recv,
    part_send,
    part_recv,
    local_sem,
    probs_sem,
    out_sem,
):
    at = Place()
    gather = Gather(
        at, packed, held, (ring_send, ring_recv, side_send, side_recv, core_send, core_recv)
    )
    greet_all(at)

    def lead(index):
        for tau in range(sum(ahead_plan[:index]), sum(ahead_plan[: index + 1])):
            gather.tick(1 + tau)

    def note_copy(step, mine):
        other = lax.rem(at.me + step, 32)
        slot = at.me if mine else other
        return remote(
            first_note.at[lax.rem(other, 16)],
            note_in.at[slot],
            note_send.at[step],
            note_recv.at[slot],
            (lax.div(other, 16), lax.rem(other, 16)),
        )

    def pair_copy(step, mine):
        other = lax.rem(at.f + step, 16)
        slot = at.f if mine else other
        return remote(
            pair_note, pair_in.at[slot], pair_send.at[step], pair_recv.at[slot], (at.x, other)
        )

    def part_copy(step, mine):
        other = lax.rem(at.f + step, 16)
        slot = at.f if mine else other
        return remote(
            part_rows.at[other],
            part_in.at[slot],
            part_send.at[step],
            part_recv.at[slot],
            (at.x, other),
        )

    pl.loop(1, 32)(lambda step: note_copy(step, True).start())
    pl.loop(1, 16)(lambda step: pair_copy(step, True).start())
    for job in range(ahead + 1):
        gather.start(job)
    local = []
    for chunk in range(chunk_count):
        column = pl.ds(aligned(chunk * chunk_cols + at.x * side_cols), ring_cols)
        copy = pltpu.make_async_copy(
            packed.at[:, column], held.at[at.cy, at.c, :, column], local_sem.at[chunk]
        )
        copy.start()
        local.append(copy)
    note_in[at.me] = first_note[at.f]
    pair_in[at.f] = pair_note[...]
    values = tokens[...].astype(f32)
    centred = values - jnp.mean(values, axis=-1, keepdims=True)
    spread = jnp.mean(centred * centred, axis=-1, keepdims=True)
    normed[...] = centred * lax.rsqrt(spread + epsilon)
    for copy in local:
        copy.wait()
    lead(0)

    @pl.loop(1, 32)
    def _(step):
        note_copy(step, False).wait_recv()

    for window in range(32):
        note_out[window : window + 1, :] = note_in[window]
    notes = note_out[...]
    kind = lax.broadcasted_iota(jnp.int32, (32, tables.shape[1]), 1).astype(f32)
    hit = (kind == notes[:, 48:49]) | (kind == notes[:, 49:50]) | (kind == notes[:, 50:51])
    pre = notes[:, 0:48] + dot_nt(hit.astype(f32).astype(b16), tables[...])
    pre_out[...] = jnp.zeros_like(pre_out)
    pre_out[:, 0:48] = pre
    group = pre_out[pl.ds(pl.multiple_of(at.x * 16, 16), 16), :][:, 0:48]
    cond = (group * (1.0 / (1.0 + jnp.exp(-group)))).astype(b16)
    partial_rows = dot_nn(cond, ada_shard[...])
    for row in range(16):
        part_rows[row] = partial_rows[row : row + 1, :].astype(b16)
    lead(1)

    @pl.loop(1, 16)
    def _(step):
        pair_copy(step, False).wait_recv()

    gathered = pair_in[...].reshape(256, 384)
    features = gathered[:, 0:128].astype(f32)
    features = features - jnp.mean(features, axis=0, keepdims=True)
    features = features * lax.rsqrt(jnp.mean(features * features, axis=0, keepdims=True) + epsilon)
    table = dot_tn(gathered[:, 128:256], features.astype(b16))[0:16, :].astype(b16)
    table_wide = table.astype(f32)
    edges[0] = jnp.broadcast_to(table_wide[:, 126:127], (16, 128))
    edges[1] = jnp.broadcast_to(table_wide[:, 0:1], (16, 128))
    edges[2] = jnp.broadcast_to(table_wide[:, 127:128], (16, 128))
    spots = dot_nt(table, class_map(128))
    for head in range(12):
        line = jnp.broadcast_to(spots[head : head + 1, :], (128, 512))
        bias[head] = pltpu.roll(line, 0, 1, stride=1, stride_axis=0)[:, 0:384]
    pl.loop(1, 16)(lambda step: part_copy(step, True).start())
    lead(2)

    breaks = jnp.sum(pair_in[:, :, 256:384].astype(f32), axis=0)
    break_row = jnp.concatenate([breaks[row : row + 1, :] for row in range(6)], axis=1)
    mark_row = rows[1:2, :].astype(b16)
    lead(3)

    @pl.loop(1, 16)
    def _(step):
        part_copy(step, False).wait_recv()

    part_in[at.f] = part_rows[at.f]
    adaptive = part_in[0].astype(f32)
    for row in range(1, 16):
        adaptive = adaptive + part_in[row].astype(f32)
    ada_out[...] = adaptive
    shift_one = adaptive[:, 0:768]
    scale_one = adaptive[:, 768:1536]
    gate_one = adaptive[:, 1536:2304]
    shift_two = adaptive[:, 2304:3072]
    scale_two = adaptive[:, 3072:3840]
    gate_two = adaptive[:, 3840:4608]
    lead(4)
    first = normed[...] * (1.0 + scale_one) + shift_one
    h_one[...] = (first + dot_tn(mark_row, break_row.astype(b16))).astype(b16)
    outgoing = []

    def emit(src, dst):
        copy = pltpu.make_async_copy(src, dst, out_sem.at[len(outgoing)])
        copy.start()
        outgoing.append(copy)

    emit(h_one, h_one_out)
    emit(pair_in, pair_out)
    for tau in range(1 + sum(ahead_plan), 15):
        gather.tick(tau)

    def weights(column, width):
        return held[:, :, :, column : column + width].reshape(768, width)

    def settle(chunk):
        gather.arrive(chunk)
        column = pl.ds(chunk * chunk_cols, chunk_cols)
        emit(held.at[:, :, :, column], held_out.at[:, :, :, column])

    settle(0)
    for piece in range(3):
        span = slice(piece * 768, piece * 768 + 768)
        qkv[:, span] = dot_nn(h_one[...], weights(piece * 768, 768)).astype(b16)
        if piece < 2:
            gather.tick(15 + piece)
    emit(qkv, qkv_out)
    chain_row = rows[0:1, :]
    pad_row = rows[2:3, :]
    first_size = 512.0 - jnp.sum(chain_row, axis=1, keepdims=True)
    low_lane = lax.broadcasted_iota(jnp.int32, (1, 128), 1) < 64
    line_number = lax.broadcasted_iota(jnp.int32, (128, 128), 0).astype(f32)

    def probs_copy(pair):
        slot = modulo(pair, 2)
        return pltpu.make_async_copy(
            probs.at[slot], probs_out.at[pl.ds(pair * 2, 2)], probs_sem.at[slot]
        )

    @pl.loop(0, 6)
    def _(pair):
        lane = pl.multiple_of(pair * 128, 128)
        slot = lax.rem(pair, 2)
        on(pair >= 2, lambda: probs_copy(pair - 2).wait())
        queries = qkv[:, pl.ds(lane, 128)] * jnp.asarray(0.125, b16)
        keys = qkv[:, pl.ds(768 + lane, 128)]
        content = qkv[:, pl.ds(1536 + lane, 128)]
        mixed = []
        for half in range(2):
            head = pair * 2 + half
            own = low_lane if half == 0 else jnp.logical_not(low_lane)
            raw = dot_nt(jnp.where(own, queries, jnp.zeros_like(queries)), keys)
            far_low = edges[0, pl.ds(head, 1), :]
            far_high = edges[1, pl.ds(head, 1), :]
            apart = edges[2, pl.ds(head, 1), :]
            for block in range(4):
                chain_here = (line_number + 128.0 * block >= first_size).astype(f32)
                tiles = []
                for other in range(4):
                    offset = block - other
                    if offset > 1:
                        near = far_low
                    elif offset < -1:
                        near = far_high
                    else:
                        near = bias[head, :, (1 - offset) * 128 : (2 - offset) * 128]
                    there = chain_row[:, other * 128 : other * 128 + 128]
                    near = jnp.where(chain_here == there, near, apart)
                    tiles.append(
                        raw[block * 128 : block * 128 + 128, other * 128 : other * 128 + 128]
                        + near
                        + pad_row[:, other * 128 : other * 128 + 128]
                    )
                scores = jnp.concatenate(tiles, axis=1)
                scores = jnp.exp(scores - jnp.max(scores, axis=1, keepdims=True))
                scores = scores * (1.0 / jnp.sum(scores, axis=1, keepdims=True))
                probs[slot, half, block * 128 : block * 128 + 128, :] = scores.astype(b16)
            mixed.append(dot_nn(probs[slot, half], content))
        attended[:, pl.ds(lane, 128)] = jnp.where(low_lane, mixed[0], mixed[1]).astype(b16)
        probs_copy(pair).start()
        spot = 17 + pair + lax.div(pair, 2)
        gather.tick(spot)
        on(lax.rem(pair, 2) == 1, lambda: gather.tick(spot + 1))

    emit(attended, attended_out)
    projected = dot_nn(attended[...], weights(2304, 768))
    proj[...] = projected.astype(b16)
    middle[...] = tokens[...].astype(f32) + gate_one * projected
    emit(proj, proj_out)
    emit(middle, middle_out)
    gather.tick(26)
    values = middle[...]
    centred = values - jnp.mean(values, axis=-1, keepdims=True)
    spread = jnp.mean(centred * centred, axis=-1, keepdims=True)
    second = centred * lax.rsqrt(spread + epsilon) * (1.0 + scale_two) + shift_two
    h_two[...] = second.astype(b16)
    emit(h_two, h_two_out)
    gather.tick(27)

    settle(1)
    for piece in range(4):
        span = slice(piece * 768, piece * 768 + 768)
        gate[:, span] = dot_nn(h_two[...], weights(3072 + piece * 768, 768)).astype(b16)
        if piece % 2 == 1:
            gather.tick(28 + piece // 2)
    emit(gate, gate_out)
    settle(2)
    for piece in range(4):
        span = slice(piece * 768, piece * 768 + 768)
        raised = dot_nn(h_two[...], weights(6144 + piece * 768, 768))
        gated = gate[:, span].astype(f32)
        up[:, span] = raised.astype(b16)
        act[:, span] = (gated * (1.0 / (1.0 + jnp.exp(-gated))) * raised).astype(b16)
        if piece < 3:
            gather.tick(30 + piece)
    emit(up, up_out)
    emit(act, act_out)
    settle(3)
    total[...] = dot_nt(act[...], weights(9216, 3072))
    fed = total[...]
    d_gate_two_out[...] = jnp.sum(cotangent[...].astype(f32) * fed, axis=0, keepdims=True)
    out_low[...] = (middle[...] + gate_two * fed).astype(b16)
    emit(out_low, output)

    probs_copy(4).wait()
    probs_copy(5).wait()
    gather.finish()
    for copy in outgoing:
        copy.wait()

    @pl.loop(1, 32)
    def _(step):
        note_copy(step, True).wait_send()

    @pl.loop(1, 16)
    def _(step):
        pair_copy(step, True).wait_send()
        part_copy(step, True).wait_send()


def run_forward(packed, tokens, cotangent, first_note, pair_note, ada_shard, tables, rows):
    anywhere = pl.BlockSpec(memory_space=pl.ANY)
    near = pl.BlockSpec(memory_space=pltpu.VMEM)
    shape = jax.ShapeDtypeStruct
    dma = pltpu.SemaphoreType.DMA
    vmem = pltpu.VMEM
    width = 768
    outs = [
        (shape((512, width), b16), anywhere),
        (shape((8, 2, 48, 12288), b16), anywhere),
        (shape((512, width), b16), anywhere),
        (shape((512, 3 * width), b16), anywhere),
        (shape((12, 512, 512), b16), anywhere),
        (shape((512, width), b16), anywhere),
        (shape((512, width), b16), anywhere),
        (shape((512, width), f32), anywhere),
        (shape((512, width), b16), anywhere),
        (shape((512, 3072), b16), anywhere),
        (shape((512, 3072), b16), anywhere),
        (shape((512, 3072), b16), anywhere),
        (shape((1, 4608), f32), near),
        (shape((1, width), f32), near),
        (shape((32, 128), f32), near),
        (shape((32, 128), f32), near),
        (shape((16, 16, 384), b16), anywhere),
    ]
    scratch = [
        vmem((8, 2, 48, 12288), b16),
        vmem((32, 1, 128), f32),
        vmem((16, 16, 384), b16),
        vmem((16, 1, 4608), b16),
        vmem((16, 1, 4608), b16),
        vmem((512, width), f32),
        vmem((512, width), b16),
        vmem((512, 3 * width), b16),
        vmem((12, 128, 384), f32),
        vmem((3, 16, 128), f32),
        vmem((2, 2, 512, 512), b16),
        vmem((512, width), b16),
        vmem((512, width), b16),
        vmem((512, width), f32),
        vmem((512, width), b16),
        vmem((512, 3072), b16),
        vmem((512, 3072), b16),
        vmem((512, 3072), b16),
        vmem((512, width), f32),
        vmem((512, width), b16),
        dma((job_count, 4, 2)),
        dma((job_count, 4, 2)),
        dma((8,)),
        dma((8,)),
        dma((8,)),
        dma((8,)),
        dma((32,)),
        dma((32,)),
        dma((16,)),
        dma((16,)),
        dma((16,)),
        dma((16,)),
        dma((4,)),
        dma((2,)),
        dma((24,)),
    ]
    return pl.pallas_call(
        forward_kernel,
        name="forward",
        out_shape=[one for one, _ in outs],
        in_specs=[anywhere] + [near] * 7,
        out_specs=[spec for _, spec in outs],
        scratch_shapes=scratch,
        compiler_params=pltpu.CompilerParams(
            collective_id=0, has_side_effects=True, vmem_limit_bytes=66_000_000
        ),
    )(packed, tokens, cotangent, first_note, pair_note, ada_shard, tables, rows)


side_jobs = 2
messages_in_job = 7


class Scatter:
    def __init__(self, at, grads, ring_in, core_in, side_in, last_in, summed, sems):
        self.at = at
        self.grads = grads
        self.ring_in = ring_in
        self.core_in = core_in
        self.side_in = side_in
        self.last_in = last_in
        self.summed = summed
        self.now = 0
        self.begun = []
        (
            self.ring_send,
            self.ring_recv,
            self.core_send,
            self.core_recv,
            self.side_send,
            self.side_recv,
            self.last_send,
            self.last_recv,
            self.credit,
        ) = sems

    def column(self, job, owner):
        inner = modulo(job, jobs_in_chunk)
        outer = quot(inner, 4)
        return aligned(inner * job_cols + side_cols + outer * (owner * ring_cols - ring_cols))

    def block(self, job, position):
        at = self.at
        buffer = modulo(quot(job, jobs_in_chunk), grad_buffers)
        span = pl.ds(self.column(job, at.x), job_cols)
        return self.grads.at[buffer, at.chip(position), at.c, :, span]

    def slot(self, job, step, way):
        return job * messages_in_job + (0 if step == 0 else 2 * step - 1 + way)

    def ring(self, job, step, way):
        at = self.at
        sign = 1 - 2 * way
        slot = self.slot(job, step, way)
        return remote(
            self.block(job, at.p + (4 - step) * sign),
            self.ring_in.at[slot],
            self.ring_send.at[slot],
            self.ring_recv.at[slot],
            at.ring_id(at.p + sign),
        )

    def absorb(self, job, step, way):
        self.ring(job, step, way).wait_recv()
        sign = 1 - 2 * way
        own = self.block(job, self.at.p + (3 - step) * sign)
        came = self.ring_in[self.slot(job, step, way)]
        own[...] = (own[...].astype(f32) + came.astype(f32)).astype(b16)

    def core(self, turn, piece):
        at = self.at
        span = pl.ds(piece * side_cols, side_cols)
        return remote(
            self.grads.at[turn % grad_buffers, :, 1 - at.c, :, span],
            self.core_in.at[turn % 2, piece],
            self.core_send.at[turn, piece],
            self.core_recv.at[turn, piece],
            at.core_id(),
        )

    def core_start(self, turn, piece):
        if turn >= 2:
            pl.semaphore_wait(self.credit.at[turn % 2, piece], 1)
        self.core(turn, piece).start()

    def core_add(self, turn, piece):
        at = self.at
        self.core(turn, piece).wait_recv()
        span = pl.ds(piece * side_cols, side_cols)

        @pl.loop(0, chip_count)
        def _(chip):
            own = self.grads.at[turn % grad_buffers, chip, at.c, :, span]
            came = self.core_in[turn % 2, piece, chip]
            own[...] = (own[...].astype(f32) + came.astype(f32)).astype(b16)

        if turn < 2:
            pl.semaphore_signal(
                self.credit.at[turn % 2, piece],
                inc=1,
                device_id=at.core_id(),
                device_id_type=mesh_ids,
            )

    def side(self, turn, half):
        at = self.at
        span = pl.ds(aligned((1 - at.x) * ring_cols + half * job_cols), job_cols)
        slot = turn * side_jobs + half
        return remote(
            self.grads.at[modulo(turn, grad_buffers), :, at.c, :, span],
            self.side_in.at[slot],
            self.side_send.at[slot],
            self.side_recv.at[slot],
            at.plane_id(),
        )

    def side_add(self, turn, half):
        at = self.at
        self.side(turn, half).wait_recv()
        span = pl.ds(aligned(at.x * ring_cols + half * job_cols), job_cols)

        @pl.loop(0, chip_count)
        def _(chip):
            own = self.grads.at[modulo(turn, grad_buffers), chip, at.c, :, span]
            came = self.side_in[turn * side_jobs + half, chip]
            own[...] = (own[...].astype(f32) + came.astype(f32)).astype(b16)

    def last(self, job):
        return remote(
            self.block(job, self.at.p),
            self.last_in.at[job],
            self.last_send.at[job],
            self.last_recv.at[job],
            self.at.plane_id(),
        )

    def store(self, job):
        at = self.at
        self.last(job).wait_recv()
        turn = quot(job, jobs_in_chunk)
        inner = modulo(job, jobs_in_chunk)
        if isinstance(job, int):
            chunk = (3, 1, 2, 0)[turn]
        else:
            chunk = turn + 3 * (1 - jnp.minimum(turn, 1)) - 3 * lax.div(turn, 3)
        base = chunk * chunk_cols
        mine = self.block(job, at.p)[...].astype(f32)
        other = self.last_in[job].astype(f32)

        def whole():
            span = pl.ds(aligned(base + self.column(job, at.x)), job_cols)
            self.summed[:, span] = mine + other

        def halves():
            span = pl.ds(aligned(base + self.column(job, at.x)), job_cols)
            self.summed[:, span] = mine
            span = pl.ds(aligned(base + self.column(job, 1 - at.x)), job_cols)
            self.summed[:, span] = other

        on(inner < 4, whole)
        on(inner >= 4, halves)

    def begin(self, turn, beside, wait=0):
        first = self.now + wait
        assert not self.begun or first >= self.begun[-1][0] + self.begun[-1][2]
        base = turn * jobs_in_chunk
        self.begun.append((first, base + 4, 2) if beside else (first, base, 4))

    def step(self, count=1):
        for _ in range(count):
            self.tick(self.now)
            self.now += 1

    def drain(self):
        last = self.begun[-1][0] + 2 + 4 * scatter_stride + 2
        pl.loop(self.now, last)(self.tick)
        self.now = last

    def tick(self, tau):
        def each(age, body):
            spot = tau - age
            if isinstance(spot, int):
                for first, base, count in self.begun:
                    if 0 <= spot - first < count:
                        body(base + spot - first)
                return
            job = jnp.int32(-1)
            for first, base, count in self.begun:
                inside = jnp.logical_and(spot >= first, spot < first + count)
                job = jnp.where(inside, spot - first + base, job)
            pl.when(job >= 0)(lambda: body(job))

        def two(step, body):
            def run(job):
                body(job, step, 0)
                body(job, step, 1)

            return run

        def start(job, step, way):
            self.ring(job, step, way).start()

        gap = scatter_stride
        each(4 * gap, two(3, self.absorb))
        each(3 * gap, two(2, self.absorb))
        each(2 * gap, two(1, self.absorb))
        each(gap, lambda job: self.absorb(job, 0, modulo(job, 2)))

        def beside(job):
            inner = modulo(job, jobs_in_chunk)
            turn = quot(job, jobs_in_chunk)
            on(inner == 4, lambda: self.side_add(turn, 0))
            on(inner == 5, lambda: self.side_add(turn, 1))

        each(0, beside)
        each(3 * gap, two(3, start))
        each(2 * gap, two(2, start))
        each(gap, two(1, start))
        each(0, lambda job: start(job, 0, modulo(job, 2)))
        each(4 * gap, lambda job: self.last(job).start())
        each(4 * gap + 2, self.store)

    def sent(self, turns):
        @pl.loop(turns[0] * jobs_in_chunk, turns[-1] * jobs_in_chunk + jobs_in_chunk)
        def _(job):
            self.ring(job, 0, lax.rem(job, 2)).wait_send()
            for step in range(1, 4):
                self.ring(job, step, 0).wait_send()
                self.ring(job, step, 1).wait_send()
            self.last(job).wait_send()

        for turn in turns:
            for piece in range(4):
                self.core(turn, piece).wait_send()
            for half in range(2):
                self.side(turn, half).wait_send()


def halves_of(values):
    high = values.astype(b16)
    return high, (values - high.astype(f32)).astype(b16)


def backward_kernel(
    held,
    probs_all,
    h_one_all,
    qkv_all,
    attended_all,
    proj_all,
    middle_all,
    h_two_all,
    gate_all,
    up_all,
    act_all,
    tokens_all,
    cotangent_all,
    adaptive,
    d_gate_two,
    pre_all,
    notes,
    pair_all,
    ada_shard,
    rows,
    d_tokens_out,
    summed,
    grad_ada,
    grad_tables,
    grad_pair,
    grad_proj,
    grad_break,
    grads,
    ring_in,
    core_in,
    side_in,
    last_in,
    piece_in,
    probs,
    d_scores,
    cot,
    act,
    gate,
    up,
    hidden,
    mid,
    d_mid,
    d_hid,
    proj,
    low,
    sums,
    lines,
    far,
    note_wide,
    note_low,
    vector_in,
    vector_wide,
    d_ada_all,
    pair_work,
    ring_send,
    ring_recv,
    core_send,
    core_recv,
    side_send,
    side_recv,
    last_send,
    last_recv,
    credit,
    load_sem,
    piece_sem,
    probs_sem,
    vector_send,
    vector_recv,
    share_send,
    share_recv,
):
    at = Place()
    scatter = Scatter(
        at,
        grads,
        ring_in,
        core_in,
        side_in,
        last_in,
        summed,
        (
            ring_send,
            ring_recv,
            core_send,
            core_recv,
            side_send,
            side_recv,
            last_send,
            last_recv,
            credit,
        ),
    )
    loads = []

    def load(src, dst):
        copy = pltpu.make_async_copy(src, dst, load_sem.at[len(loads)])
        copy.start()
        loads.append(copy)
        return copy

    cot_load = load(cotangent_all, cot)
    act_load = load(act_all, act)
    piece_order = [9216 + 768 * n for n in range(4)]
    for n in range(4):
        piece_order += [3072 + 768 * n, 6144 + 768 * n]
    piece_order += [2304, 0, 768, 1536]

    def piece_copy(index):
        column = pl.ds(piece_order[index], side_cols)
        return pltpu.make_async_copy(
            held.at[:, :, :, column], piece_in.at[index % 4], piece_sem.at[index % 4]
        )

    def piece(index):
        piece_copy(index).wait()
        return piece_in[index % 4].reshape(768, 768)

    def piece_used(index):
        if index + 4 < len(piece_order):
            piece_copy(index + 4).start()

    for index in range(4):
        piece_copy(index).start()
    gate_load = load(gate_all, gate)
    up_load = load(up_all, up)
    hidden_load = load(h_two_all, hidden)
    mid_load = load(middle_all, mid)
    proj_load = load(proj_all, proj)

    def probs_copy(pair):
        slot = modulo(pair, 2)
        return pltpu.make_async_copy(
            probs_all.at[pl.ds(pair * 2, 2)], probs.at[slot], probs_sem.at[slot]
        )

    probs_copy(0).start()
    probs_copy(1).start()
    greet_all(at)
    scale_one = adaptive[:, 768:1536]
    gate_one = adaptive[:, 1536:2304]
    scale_two = adaptive[:, 3072:3840]
    gate_two = adaptive[:, 3840:4608]
    sums[...] = jnp.zeros_like(sums)

    def put(turn, part, left, right):
        span = slice(part * 768, part * 768 + 768)
        grads[turn % grad_buffers, :, :, :, span] = (
            dot_tn(left, right).astype(b16).reshape(8, 2, 48, 768)
        )
        scatter.core_start(turn, part)

    def merge(turn):
        scatter.core_add(turn, 0)
        scatter.core_add(turn, 3)
        scatter.side(turn, 0).start()
        scatter.side(turn, 1).start()
        scatter.core_add(turn, 1)
        scatter.core_add(turn, 2)
        scatter.begin(turn, False)

    cot_load.wait()
    low[...] = (gate_two * cot[...].astype(f32)).astype(b16)
    act_load.wait()
    for part in (0, 3, 1, 2):
        put(0, part, low[...], act[:, part * 768 : part * 768 + 768])
    qkv_load = load(qkv_all, act.at[:, 0:2304])
    attended_load = load(attended_all, act.at[:, 2304:3072])
    gate_load.wait()
    up_load.wait()
    for part in range(4):
        d_hid[...] = dot_nn(low[...], piece(part))
        piece_used(part)
        span = slice(part * 768, part * 768 + 768)

        @pl.loop(0, 8)
        def _(block):
            line = pl.ds(pl.multiple_of(block * 64, 64), 64)
            d_act = d_hid[line, :]
            gated = gate[line, span].astype(f32)
            raised = up[line, span].astype(f32)
            sigma = 1.0 / (1.0 + jnp.exp(-gated))
            scaled = d_act * sigma
            gate[line, span] = (scaled * raised * (1.0 + gated * (1.0 - sigma))).astype(b16)
            up[line, span] = (scaled * gated).astype(b16)

        if part == 0:
            merge(0)
        scatter.step(plan[0])
    hidden_load.wait()
    for part in (0, 3):
        put(1, part, hidden[...], gate[:, part * 768 : part * 768 + 768])
    scatter.step(plan[1])
    for part in (1, 2):
        put(1, part, hidden[...], gate[:, part * 768 : part * 768 + 768])
    scatter.step(plan[1])
    for part in (0, 3):
        put(2, part, hidden[...], up[:, part * 768 : part * 768 + 768])
    merge(1)
    scatter.begin(0, True, 4)
    scatter.step(plan[2])
    for part in (1, 2):
        put(2, part, hidden[...], up[:, part * 768 : part * 768 + 768])
    scatter.step(plan[2])
    h_one_load = load(h_one_all, hidden)
    for part in range(4):
        span = slice(part * 768, part * 768 + 768)
        product = dot_nt(gate[:, span], piece(4 + 2 * part))
        piece_used(4 + 2 * part)
        product = product + dot_nt(up[:, span], piece(5 + 2 * part))
        piece_used(5 + 2 * part)
        if part == 0:
            d_hid[...] = product
        else:
            d_hid[...] += product
        scatter.step(plan[3])
    merge(2)
    scatter.begin(1, True, 4)
    scatter.begin(2, True, 12)
    mid_load.wait()
    proj_load.wait()

    @pl.loop(0, 8)
    def _(block):
        line = pl.ds(pl.multiple_of(block * 64, 64), 64)
        values = mid[line, :]
        centred = values - jnp.mean(values, axis=-1, keepdims=True)
        inverse = lax.rsqrt(jnp.mean(centred * centred, axis=-1, keepdims=True) + epsilon)
        centred = centred * inverse
        grad = d_hid[line, :]
        sums[0:1, :] += jnp.sum(grad, axis=0, keepdims=True)
        sums[1:2, :] += jnp.sum(grad * centred, axis=0, keepdims=True)
        grad = grad * (1.0 + scale_two)
        grad = grad - jnp.mean(grad, axis=-1, keepdims=True) - centred * jnp.mean(
            grad * centred, axis=-1, keepdims=True
        )
        grad = cot[line, :].astype(f32) + inverse * grad
        d_mid[line, :] = grad
        sums[2:3, :] += jnp.sum(grad * proj[line, :].astype(f32), axis=0, keepdims=True)
        low[line, :] = (gate_one * grad).astype(b16)

    tokens_load = load(tokens_all, proj)
    scatter.step(plan[4])
    cot[...] = dot_nt(low[...], piece(12)).astype(b16)
    piece_used(12)
    qkv_load.wait()
    attended_load.wait()
    scatter.step(plan[4])
    start_tick = scatter.now

    chain_row = rows[0:1, :]
    first_size = 512.0 - jnp.sum(chain_row, axis=1, keepdims=True)
    low_lane = lax.broadcasted_iota(jnp.int32, (1, 128), 1) < 64
    line_number = lax.broadcasted_iota(jnp.int32, (128, 128), 0).astype(f32)
    lines[...] = jnp.zeros_like(lines)
    far[...] = jnp.zeros_like(far)

    @pl.loop(0, 6)
    def _(pair):
        lane = pl.multiple_of(pair * 128, 128)
        slot = lax.rem(pair, 2)
        probs_copy(pair).wait()
        queries = act[:, pl.ds(lane, 128)] * jnp.asarray(0.125, b16)
        keys = act[:, pl.ds(768 + lane, 128)]
        content = act[:, pl.ds(1536 + lane, 128)]
        d_out = cot[:, pl.ds(lane, 128)]
        d_queries, d_keys, d_content = [], [], []
        for half in range(2):
            head = pair * 2 + half
            own = low_lane if half == 0 else jnp.logical_not(low_lane)
            d_own = jnp.where(own, d_out, jnp.zeros_like(d_out))
            d_probs = dot_nt(d_own, content)
            band = [None, None, None]
            low_sum = jnp.zeros((128, 128), f32)
            high_sum = jnp.zeros((128, 128), f32)
            apart = jnp.zeros((128, 128), f32)
            for block in range(4):
                line = slice(block * 128, block * 128 + 128)
                here = probs[slot, half, line, :].astype(f32)
                weighted = here * d_probs[line, :]
                weighted = weighted - here * jnp.sum(weighted, axis=1, keepdims=True)
                d_scores[line, :] = weighted.astype(b16)
                chain_here = (line_number + 128.0 * block >= first_size).astype(f32)
                for other in range(4):
                    tile = weighted[:, other * 128 : other * 128 + 128]
                    there = chain_row[:, other * 128 : other * 128 + 128]
                    same = jnp.where(chain_here == there, tile, jnp.zeros_like(tile))
                    apart = apart + (tile - same)
                    offset = block - other
                    if offset > 1:
                        low_sum = low_sum + same
                    elif offset < -1:
                        high_sum = high_sum + same
                    elif band[1 - offset] is None:
                        band[1 - offset] = same
                    else:
                        band[1 - offset] = band[1 - offset] + same
            far[0, pl.ds(head, 1), :] = jnp.sum(low_sum, axis=0, keepdims=True)
            far[1, pl.ds(head, 1), :] = jnp.sum(high_sum, axis=0, keepdims=True)
            far[2, pl.ds(head, 1), :] = jnp.sum(apart, axis=0, keepdims=True)
            folded = jnp.concatenate(band + [jnp.zeros((128, 128), f32)], axis=1)
            size = 64
            while size >= 1:
                folded = folded[0:size, :] + pltpu.roll(
                    folded[size : 2 * size, :], 512 - size, 1
                )
                size = size // 2
            lines[pl.ds(head, 1), :] = folded
            d_here = d_scores[...]
            d_queries.append(dot_nn(d_here, keys))
            masked = jnp.where(own, queries, jnp.zeros_like(queries))
            d_keys.append(dot_tn(d_here, masked))
            d_content.append(dot_tn(probs[slot, half], d_own))
            if half == 0:
                for extra in range(plan[5]):
                    scatter.tick(start_tick + (plan[5] + plan[6]) * pair + extra)
        gate[:, pl.ds(lane, 128)] = (
            jnp.where(low_lane, d_queries[0], d_queries[1]) * 0.125
        ).astype(b16)
        gate[:, pl.ds(768 + lane, 128)] = (d_keys[0] + d_keys[1]).astype(b16)
        gate[:, pl.ds(1536 + lane, 128)] = (d_content[0] + d_content[1]).astype(b16)
        on(pair < 4, lambda: probs_copy(pair + 2).start())
        for extra in range(plan[6]):
            scatter.tick(start_tick + (plan[5] + plan[6]) * pair + plan[5] + extra)

    scatter.now += 6 * (plan[5] + plan[6])
    if grad_buffers == 3:
        done = scatter.begun[2][0] + 2 + 4 * scatter_stride + 2
        assert scatter.now >= done and scatter.begun[2][1] == 4
        scatter.sent([0])
    put(3, 3, act[:, 2304:3072], low[...])
    h_one_load.wait()
    put(3, 0, hidden[...], gate[:, 0:768])
    scatter.step(plan[7])
    put(3, 1, hidden[...], gate[:, 768:1536])
    put(3, 2, hidden[...], gate[:, 1536:2304])
    for part in range(3):
        product = dot_nt(gate[:, part * 768 : part * 768 + 768], piece(13 + part))
        if part == 0:
            d_hid[...] = product
        else:
            d_hid[...] += product
        if part == 0:
            merge(3)
            scatter.begin(3, True, plan[10])
        scatter.step(plan[8])
    tokens_load.wait()

    @pl.loop(0, 8)
    def _(block):
        line = pl.ds(pl.multiple_of(block * 64, 64), 64)
        values = proj[line, :].astype(f32)
        centred = values - jnp.mean(values, axis=-1, keepdims=True)
        inverse = lax.rsqrt(jnp.mean(centred * centred, axis=-1, keepdims=True) + epsilon)
        centred = centred * inverse
        grad = d_hid[line, :]
        sums[3:4, :] += jnp.sum(grad, axis=0, keepdims=True)
        sums[4:5, :] += jnp.sum(grad * centred, axis=0, keepdims=True)
        cot[line, :] = grad.astype(b16)
        grad = grad * (1.0 + scale_one)
        grad = grad - jnp.mean(grad, axis=-1, keepdims=True) - centred * jnp.mean(
            grad * centred, axis=-1, keepdims=True
        )
        low[line, :] = (d_mid[line, :] + inverse * grad).astype(b16)

    tokens_store = load(low, d_tokens_out)
    break_sum = dot_nn(jnp.broadcast_to(rows[1:2, :], (8, 512)).astype(b16), cot[...])
    scatter.step(plan[9])

    scale = class_map(128)
    line_high, line_low = halves_of(lines[...])
    d_table = dot_nn(line_high, scale) + dot_nn(line_low, scale)
    kind = lax.broadcasted_iota(jnp.int32, (16, 128), 1)
    for index, label in ((0, 126), (1, 0), (2, 127)):
        total = jnp.sum(far[index], axis=1, keepdims=True)
        d_table = d_table + jnp.where(kind == label, total, jnp.zeros_like(d_table))
    vectors = [sums[3:4, :], sums[4:5, :], sums[2:3, :], sums[0:1, :], sums[1:2, :]]
    vectors.append(d_gate_two[...])
    for index in range(6):
        for part in range(6):
            note_wide[index * 6 + part : index * 6 + part + 1, :] = vectors[index][
                :, part * 128 : part * 128 + 128
            ]
    note_wide[36:48, :] = d_table[0:12, :]
    for part in range(6):
        note_wide[48 + part : 49 + part, :] = break_sum[0:1, part * 128 : part * 128 + 128]
    note_wide[54:64, :] = jnp.zeros((10, 128), f32)
    note_low[...] = note_wide[...].astype(b16)
    vector_in[at.x, at.cy, at.c] = note_low[...]
    scatter.step(plan[9])

    def vector_copy(step, mine):
        other = lax.rem(at.cy + step, 8)
        slot = at.cy if mine else other
        return remote(
            note_low,
            vector_in.at[at.x, slot, at.c],
            vector_send.at[step],
            vector_recv.at[slot],
            (at.x, other * 2 + at.c),
        )

    def plane_copy(plane):
        block = vector_in.at[plane, :, at.c]
        return remote(block, block, share_send.at[0], share_recv.at[0], at.plane_id())

    def pair_copy(core):
        block = vector_in.at[:, :, core]
        return remote(block, block, share_send.at[1], share_recv.at[1], at.core_id())

    for step in range(1, 8):
        vector_copy(step, True).start()
    scatter.step(plan[9])
    for step in range(1, 8):
        vector_copy(step, False).wait_recv()
    plane_copy(at.x).start()
    scatter.step(plan[9])
    plane_copy(1 - at.x).wait_recv()
    pair_copy(at.c).start()
    scatter.step(plan[9])
    pair_copy(1 - at.c).wait_recv()
    total = jnp.zeros((64, 128), f32)
    for plane in range(2):
        vector_wide[...] = vector_in[plane].reshape(1024, 128).astype(f32)
        for part in range(36):
            d_ada_all[plane * 16 : plane * 16 + 16, part * 128 : part * 128 + 128] = vector_wide[
                pl.ds(part, 16, stride=64), :
            ].astype(b16)
        for window in range(16):
            total = total + vector_wide[window * 64 : window * 64 + 64, :]
    note_wide[...] = total
    pre = pre_all[...]
    sigma = 1.0 / (1.0 + jnp.exp(-pre))
    grad_ada[...] = dot_tn((pre * sigma).astype(b16)[:, 0:48], d_ada_all[...])
    d_pre = dot_nt(d_ada_all[...], ada_shard[...])
    pre, sigma = pre[:, 0:48], sigma[:, 0:48]
    d_pre = d_pre * sigma * (1.0 + pre * (1.0 - sigma))
    scatter.step(plan[9])
    labels = notes[...]
    kind = lax.broadcasted_iota(jnp.int32, (32, grad_tables.shape[1]), 1).astype(f32)
    hit = (kind == labels[:, 48:49]) | (kind == labels[:, 49:50]) | (kind == labels[:, 50:51])
    hit = hit.astype(f32).astype(b16)
    high, rest = halves_of(d_pre)
    grad_tables[...] = dot_tn(high, hit) + dot_tn(rest, hit)
    scatter.step(plan[9])
    grad_break[...] = note_wide[48:56, :]
    d_table = note_wide[36:52, :]
    keep = lax.broadcasted_iota(jnp.int32, (16, 128), 0) < 12
    d_table = jnp.where(keep, d_table, jnp.zeros_like(d_table))
    gathered = pair_all[...].reshape(256, 384)
    features = gathered[:, 0:128].astype(f32)
    features = features - jnp.mean(features, axis=0, keepdims=True)
    inverse = lax.rsqrt(jnp.mean(features * features, axis=0, keepdims=True) + epsilon)
    features = features * inverse
    high, rest = halves_of(d_table)
    pair_low = features.astype(b16)
    pair_work[:, 0:16] = dot_nt(pair_low, high) + dot_nt(pair_low, rest)
    mine = pl.ds(pl.multiple_of(at.f * 16, 16), 16)
    grad_proj[...] = pair_work[mine, :]
    weights = gathered[:, 128:144]
    grad = dot_nn(weights, high) + dot_nn(weights, rest)
    grad = inverse * (
        grad
        - jnp.mean(grad, axis=0, keepdims=True)
        - features * jnp.mean(grad * features, axis=0, keepdims=True)
    )
    pair_work[...] = grad
    grad_pair[...] = pair_work[mine, :]
    scatter.drain()
    scatter.sent([1, 2, 3] if grad_buffers == 3 else [0, 1, 2, 3])
    tokens_store.wait()
    for step in range(1, 8):
        vector_copy(step, True).wait_send()
    plane_copy(at.x).wait_send()
    pair_copy(at.c).wait_send()


def run_backward(saved, tokens, cotangent, ada_shard, rows, table_rows):
    (
        held,
        h_one,
        qkv,
        probs,
        attended,
        proj,
        middle,
        h_two,
        gate,
        up,
        act,
        adaptive,
        d_gate_two,
        pre,
        notes,
        pair_all,
    ) = saved
    anywhere = pl.BlockSpec(memory_space=pl.ANY)
    near = pl.BlockSpec(memory_space=pltpu.VMEM)
    shape = jax.ShapeDtypeStruct
    dma = pltpu.SemaphoreType.DMA
    vmem = pltpu.VMEM
    width = 768
    outs = [
        (shape((512, width), b16), anywhere),
        (shape((48, 12288), f32), near),
        (shape((48, 4608), f32), near),
        (shape((48, table_rows), f32), near),
        (shape((16, 128), f32), near),
        (shape((16, 128), f32), near),
        (shape((8, 128), f32), near),
    ]
    ring_slots = job_count * messages_in_job
    scratch = [
        vmem((grad_buffers, 8, 2, 48, chunk_cols), b16),
        vmem((ring_slots, 48, job_cols), b16),
        vmem((2, 4, 8, 48, side_cols), b16),
        vmem((8, 8, 48, job_cols), b16),
        vmem((job_count, 48, job_cols), b16),
        vmem((4, 8, 2, 48, side_cols), b16),
        vmem((2, 2, 512, 512), b16),
        vmem((512, 512), b16),
        vmem((512, width), b16),
        vmem((512, 3072), b16),
        vmem((512, 3072), b16),
        vmem((512, 3072), b16),
        vmem((512, width), b16),
        vmem((512, width), f32),
        vmem((512, width), f32),
        vmem((512, width), f32),
        vmem((512, width), b16),
        vmem((512, width), b16),
        vmem((8, width), f32),
        vmem((16, 512), f32),
        vmem((3, 16, 128), f32),
        vmem((64, 128), f32),
        vmem((64, 128), b16),
        vmem((2, 8, 2, 64, 128), b16),
        vmem((1024, 128), f32),
        vmem((32, 4608), b16),
        vmem((256, 128), f32),
        dma((ring_slots,)),
        dma((ring_slots,)),
        dma((4, 4)),
        dma((4, 4)),
        dma((8,)),
        dma((8,)),
        dma((job_count,)),
        dma((job_count,)),
        pltpu.SemaphoreType.REGULAR((2, 4)),
        dma((16,)),
        dma((4,)),
        dma((2,)),
        dma((8,)),
        dma((8,)),
        dma((2,)),
        dma((2,)),
    ]
    return pl.pallas_call(
        backward_kernel,
        name="backward",
        out_shape=[one for one, _ in outs],
        in_specs=[anywhere] * 13 + [near] * 7,
        out_specs=[spec for _, spec in outs],
        scratch_shapes=scratch,
        compiler_params=pltpu.CompilerParams(
            collective_id=1, has_side_effects=True, vmem_limit_bytes=67_043_328
        ),
    )(
        held,
        probs,
        h_one,
        qkv,
        attended,
        proj,
        middle,
        h_two,
        gate,
        up,
        act,
        tokens,
        cotangent,
        adaptive,
        d_gate_two,
        pre,
        notes,
        pair_all,
        ada_shard,
        rows,
    )


def pack_kernel(
    time_embed,
    cath_class,
    cath_arch,
    cath_topo,
    res_counts,
    chain_ids,
    break_mask,
    w_qkv,
    w_out,
    w_gate,
    w_up,
    w_down,
    table_class,
    table_arch,
    table_topo,
    break_vec,
    pair_table,
    pair_proj,
    packed,
    first_note,
    pair_note,
    tables,
    rows,
):
    packed[:, 0:2304] = w_qkv[...]
    packed[:, 2304:3072] = w_out[...]
    packed[:, 3072:6144] = w_gate[...]
    packed[:, 6144:9216] = w_up[...]
    packed[:, 9216:12288] = w_down[...]
    lane = lax.broadcasted_iota(jnp.int32, (1, 128), 1)
    marks = jnp.zeros((1, 128), f32)
    for index, labels in enumerate((cath_class, cath_arch, cath_topo)):
        label = (labels[0] + 128 * index).astype(f32)
        marks = jnp.where(lane == 48 + index, label, marks)
    embed = time_embed[...].astype(f32)
    for owner in range(16):
        first_note[owner] = marks
        first_note[owner, :, 0:48] = embed[:, owner * 48 : owner * 48 + 48]
    shard = lax.axis_index("fsdp") * 48
    unit = lax.broadcasted_iota(jnp.int32, (128, 128), 0)
    unit = (unit == lax.broadcasted_iota(jnp.int32, (128, 128), 1)).astype(f32).astype(b16)
    pair_note[:, 0:128] = pair_table[...]
    pair_note[:, 128:256] = jnp.zeros((16, 128), b16)
    pair_note[:, 128:140] = pair_proj[...]
    spot = lax.broadcasted_iota(jnp.int32, (48, 2048), 1) - shard
    spot = (spot == lax.broadcasted_iota(jnp.int32, (48, 2048), 0)).astype(f32).astype(b16)
    placed = dot_nn(jnp.broadcast_to(break_vec[...].astype(f32), (16, 48)).astype(b16), spot)
    line = lax.broadcasted_iota(jnp.int32, (16, 128), 0)
    breaks = jnp.zeros((16, 128), f32)
    for row in range(16):
        breaks = jnp.where(line == row, placed[:, row * 128 : row * 128 + 128], breaks)
    pair_note[:, 256:384] = breaks.astype(b16)
    for index, lookup in enumerate((table_class, table_arch)):
        block = dot_tn(lookup[...], unit[0 : lookup.shape[0], :])
        tables[:, index * 128 : index * 128 + 128] = block.astype(b16)
    tables[:, 256:] = table_topo[...]
    rows[0:1, :] = chain_ids[...].astype(f32)
    rows[1:2, :] = break_mask[...].astype(f32)
    position = lax.broadcasted_iota(jnp.int32, (1, 512), 1)
    rows[2:3, :] = jnp.where(position < res_counts[0], 0.0, -1e30)
    rows[3:8, :] = jnp.zeros((5, 512), f32)


def forward_inputs(
    time_embed,
    cath_class,
    cath_arch,
    cath_topo,
    res_counts,
    chain_ids,
    break_mask,
    w_qkv,
    w_out,
    w_gate,
    w_up,
    w_down,
    table_class,
    table_arch,
    table_topo,
    break_vec,
    pair_table,
    pair_proj,
):
    near = pl.BlockSpec(memory_space=pltpu.VMEM)
    flat = pl.BlockSpec(memory_space=pltpu.SMEM)
    count = 256 + table_topo.shape[0]
    shape = jax.ShapeDtypeStruct
    return pl.pallas_call(
        pack_kernel,
        name="pack",
        out_shape=[
            shape((48, 12288), b16),
            shape((16, 1, 128), f32),
            shape((16, 384), b16),
            shape((48, count), b16),
            shape((8, 512), f32),
        ],
        in_specs=[near] + [flat] * 4 + [near] * 13,
        out_specs=[near] * 5,
    )(
        time_embed,
        cath_class,
        cath_arch,
        cath_topo,
        res_counts,
        chain_ids,
        break_mask,
        w_qkv,
        w_out,
        w_gate,
        w_up,
        w_down.T,
        table_class,
        table_arch,
        table_topo.T,
        break_vec[None, :],
        pair_table.T,
        pair_proj,
    )


def unpack_kernel(
    summed,
    ada_in,
    tables,
    pair_in,
    proj_in,
    break_in,
    grad_ada,
    grad_qkv,
    grad_out,
    grad_gate,
    grad_up,
    grad_down,
    grad_class,
    grad_arch,
    grad_topo,
    grad_break,
    grad_pair,
    grad_proj,
):
    grad_ada[...] = ada_in[...]
    grad_qkv[...] = summed[:, 0:2304]
    grad_out[...] = summed[:, 2304:3072]
    grad_gate[...] = summed[:, 3072:6144]
    grad_up[...] = summed[:, 6144:9216]
    grad_down[...] = summed[:, 9216:12288]
    grad_class[...] = tables[:, 0:128].T[0 : grad_class.shape[0], :]
    grad_arch[...] = tables[:, 128:256].T[0 : grad_arch.shape[0], :]
    grad_topo[...] = tables[:, 256:]
    shard = lax.axis_index("fsdp") * 48
    total = jnp.zeros((1, 48), f32)
    for owner in range(16):
        row, column = divmod(owner * 48, 128)
        width = min(48, 128 - column)
        piece = break_in[row : row + 1, column : column + width]
        if width < 48:
            piece = jnp.concatenate([piece, break_in[row + 1 : row + 2, 0 : 48 - width]], axis=1)
        total = jnp.where(shard == owner * 48, piece, total)
    grad_break[...] = total
    grad_pair[...] = pair_in[...]
    grad_proj[...] = proj_in[:, 0:12]


def run_unpack(summed, ada, tables, pair, proj, breaks, sizes):
    near = pl.BlockSpec(memory_space=pltpu.VMEM)
    shape = jax.ShapeDtypeStruct
    outs = [
        (48, 4608),
        (48, 2304),
        (48, 768),
        (48, 3072),
        (48, 3072),
        (48, 3072),
        (sizes[0], 48),
        (sizes[1], 48),
        (48, sizes[2]),
        (1, 48),
        (16, 128),
        (16, 12),
    ]
    return pl.pallas_call(
        unpack_kernel,
        name="unpack",
        out_shape=[shape(one, f32) for one in outs],
        in_specs=[near] * 6,
        out_specs=[near] * 12,
    )(summed, ada, tables, pair, proj, breaks)


def fast_shards(
    tokens,
    cotangent,
    time_embed,
    cath_class,
    cath_arch,
    cath_topo,
    res_counts,
    chain_ids,
    break_mask,
    w_ada,
    w_qkv,
    w_out,
    w_gate,
    w_up,
    w_down,
    table_class,
    table_arch,
    table_topo,
    break_vec,
    pair_table,
    pair_proj,
):
    packed, first_note, pair_note, tables, rows = forward_inputs(
        time_embed,
        cath_class,
        cath_arch,
        cath_topo,
        res_counts,
        chain_ids,
        break_mask,
        w_qkv,
        w_out,
        w_gate,
        w_up,
        w_down,
        table_class,
        table_arch,
        table_topo,
        break_vec,
        pair_table,
        pair_proj,
    )
    output, *saved = run_forward(
        packed, tokens[0], cotangent[0], first_note, pair_note, w_ada, tables, rows
    )
    d_tokens, summed, grad_ada, grad_tables, grad_pair, grad_proj, grad_break = run_backward(
        saved, tokens[0], cotangent[0], w_ada, rows, tables.shape[1]
    )
    sizes = (table_class.shape[0], table_arch.shape[0], table_topo.shape[0])
    grads = run_unpack(summed, grad_ada, grad_tables, grad_pair, grad_proj, grad_break, sizes)
    return (
        output[None],
        d_tokens[None],
        *grads[:5],
        grads[5].T,
        grads[6],
        grads[7],
        grads[8].T,
        grads[9][0],
        grads[10].T,
        grads[11],
    )


def solution(mesh):
    in_specs = (
        P(("dp", "fsdp"), None, None),
        P(("dp", "fsdp"), None, None),
        P(("dp", "fsdp"), None),
        P(("dp", "fsdp")),
        P(("dp", "fsdp")),
        P(("dp", "fsdp")),
        P(("dp", "fsdp")),
        P(("dp", "fsdp"), None),
        P(("dp", "fsdp"), None),
        P("fsdp", None),
        P("fsdp", None),
        P("fsdp", None),
        P("fsdp", None),
        P("fsdp", None),
        P(None, "fsdp"),
        P(None, "fsdp"),
        P(None, "fsdp"),
        P(None, "fsdp"),
        P("fsdp"),
        P(None, "fsdp"),
        P("fsdp", None),
    )
    out_specs = (
        P(("dp", "fsdp"), None, None),
        P(("dp", "fsdp"), None, None),
        P("fsdp", None),
        P("fsdp", None),
        P("fsdp", None),
        P("fsdp", None),
        P("fsdp", None),
        P(None, "fsdp"),
        P(None, "fsdp"),
        P(None, "fsdp"),
        P(None, "fsdp"),
        P("fsdp"),
        P(None, "fsdp"),
        P("fsdp", None),
    )
    sizes = dict(mesh.shape)
    body = fast_shards if (sizes["dp"], sizes["fsdp"]) == (2, 16) else shards
    return jax.shard_map(body, mesh=mesh, in_specs=in_specs, out_specs=out_specs, check_vma=False)
```

```python
from functools import partial

import jax
import jax.numpy as jnp
from jax import lax
from jax.experimental import pallas as pl
from jax.experimental.pallas import tpu as pltpu
from jax.sharding import PartitionSpec as P

epsilon = 1e-05
highest = lax.Precision.HIGHEST


def matmul(left, right):
    return jnp.dot(left, right, preferred_element_type=jnp.float32)


def matmul_t(left, right):
    return lax.dot_general(
        left, right, (((1,), (1,)), ((), ())), preferred_element_type=jnp.float32
    )


def matmul_tn(left, right):
    return lax.dot_general(
        left, right, (((0,), (0,)), ((), ())), preferred_element_type=jnp.float32
    )


def exact_tn(left, right):
    return lax.dot_general(
        left, right, (((0,), (0,)), ((), ())), precision=highest, preferred_element_type=jnp.float32
    )


def exact_nt(left, right):
    return lax.dot_general(
        left, right, (((1,), (1,)), ((), ())), precision=highest, preferred_element_type=jnp.float32
    )


def normalize(values):
    centred = values - jnp.mean(values, axis=-1, keepdims=True)
    inv_std = lax.rsqrt(jnp.mean(centred * centred, axis=-1, keepdims=True) + epsilon)
    return (centred * inv_std, inv_std)


def normalize_back(normed, inv_std, grad):
    return inv_std * (
        grad
        - jnp.mean(grad, axis=-1, keepdims=True)
        - normed * jnp.mean(grad * normed, axis=-1, keepdims=True)
    )


def pair_classes(chain_row, class_count):
    length = chain_row.shape[0]
    position = jnp.arange(length, dtype=jnp.int32)
    reach = class_count // 2 - 1
    offset = jnp.clip(position[:, None] - position[None, :], -reach, reach) + reach
    return jnp.where(chain_row[:, None] == chain_row[None, :], offset, class_count - 1)


def pair_bias(classes, bias_table):
    length = classes.shape[0]
    step_rows = min(length, 128)
    class_ids = jnp.arange(bias_table.shape[0], dtype=jnp.int32)

    def one_block(row_block):
        onehot = (row_block[:, :, None] == class_ids).astype(jnp.bfloat16)
        return jnp.einsum("ijc,ch->hij", onehot, bias_table, preferred_element_type=jnp.float32)

    pieces = lax.map(one_block, classes.reshape(length // step_rows, step_rows, length))
    return jnp.transpose(pieces, (1, 0, 2, 3)).reshape(bias_table.shape[1], length, length)


def pair_bias_back(classes, d_scores, class_count):
    head_count, length = (d_scores.shape[0], d_scores.shape[1])
    step_rows = min(length, 128)
    block_count = length // step_rows
    class_ids = jnp.arange(class_count, dtype=jnp.int32)
    grad_blocks = jnp.transpose(
        d_scores.reshape(head_count, block_count, step_rows, length), (1, 0, 2, 3)
    )

    def add_block(running, inputs):
        row_block, grad_block = inputs
        onehot = (row_block[:, :, None] == class_ids).astype(jnp.bfloat16)
        return (
            running
            + jnp.einsum("hij,ijc->ch", grad_block, onehot, preferred_element_type=jnp.float32),
            None,
        )

    start = jnp.zeros((class_count, head_count), jnp.float32)
    summed, unused = lax.scan(
        add_block, start, (classes.reshape(block_count, step_rows, length), grad_blocks)
    )
    return summed


def split_heads(qkv_win, head_count):
    length, triple = qkv_win.shape
    shaped = qkv_win.reshape(length, 3, head_count, triple // (3 * head_count))
    return (shaped[:, 0], shaped[:, 1], shaped[:, 2])


def window_scores(qkv_win, chain_row, count_win, bias_table):
    length = qkv_win.shape[0]
    queries, key_rows, value_rows = split_heads(qkv_win, bias_table.shape[1])
    classes = pair_classes(chain_row, bias_table.shape[0])
    score_scale = queries.shape[-1] ** (-0.5)
    scores = (
        jnp.einsum("qhd,khd->hqk", queries, key_rows, preferred_element_type=jnp.float32)
        * score_scale
    )
    scores = scores + pair_bias(classes, bias_table)
    live_keys = jnp.arange(length, dtype=jnp.int32) < count_win
    scores = jnp.where(live_keys[None, None, :], scores, -1e30)
    return (scores, queries, key_rows, value_rows, classes, score_scale)


def attend(inputs, bias_table):
    qkv_win, chain_row, count_win = inputs
    scores, queries, key_rows, value_rows, classes, score_scale = window_scores(
        qkv_win, chain_row, count_win, bias_table
    )
    highest_score = jnp.max(scores, axis=-1, keepdims=True)
    exponent = jnp.exp(scores - highest_score)
    row_total = jnp.sum(exponent, axis=-1, keepdims=True)
    attn_probs = (exponent / row_total).astype(jnp.bfloat16)
    attended = jnp.einsum(
        "hqk,khd->qhd", attn_probs, value_rows, preferred_element_type=jnp.float32
    )
    attended = attended.reshape(qkv_win.shape[0], -1).astype(jnp.bfloat16)
    return (attended, (highest_score + jnp.log(row_total))[:, :, 0])


def attend_back(inputs, bias_table):
    qkv_win, chain_row, count_win, log_total, d_attended = inputs
    scores, queries, key_rows, value_rows, classes, score_scale = window_scores(
        qkv_win, chain_row, count_win, bias_table
    )
    attn_probs = jnp.exp(scores - log_total[:, :, None])
    d_heads = d_attended.reshape(queries.shape)
    d_probs = jnp.einsum("qhd,khd->hqk", d_heads, value_rows, preferred_element_type=jnp.float32)
    d_scores = attn_probs * (d_probs - jnp.sum(attn_probs * d_probs, axis=-1, keepdims=True))
    d_scores = d_scores.astype(jnp.bfloat16)
    d_values = jnp.einsum(
        "hqk,qhd->khd", attn_probs.astype(jnp.bfloat16), d_heads, preferred_element_type=jnp.float32
    )
    d_queries = (
        jnp.einsum("hqk,khd->qhd", d_scores, key_rows, preferred_element_type=jnp.float32)
        * score_scale
    )
    d_keys = (
        jnp.einsum("hqk,qhd->khd", d_scores, queries, preferred_element_type=jnp.float32)
        * score_scale
    )
    d_qkv = (
        jnp.stack([d_queries, d_keys, d_values], axis=1)
        .reshape(qkv_win.shape[0], -1)
        .astype(jnp.bfloat16)
    )
    return (d_qkv, pair_bias_back(classes, d_scores, bias_table.shape[0]))


def forward(
    tokens,
    time_embed,
    cath_class,
    cath_arch,
    cath_topo,
    res_counts,
    chain_ids,
    break_mask,
    attn_set,
    mlp_set,
):
    ada_all, qkv_all, out_all, class_all, arch_all, topo_all, break_all, pair_all, proj_all = (
        attn_set
    )
    gate_all, up_all, down_all = mlp_set
    windows, length, model_width = tokens.shape
    row_count = windows * length
    pre_act = time_embed.astype(jnp.float32)
    onehots = []
    for labels, lookup in ((cath_class, class_all), (cath_arch, arch_all), (cath_topo, topo_all)):
        onehot = (labels[:, None] == jnp.arange(lookup.shape[0], dtype=jnp.int32)[None, :]).astype(
            jnp.bfloat16
        )
        pre_act = pre_act + matmul(onehot, lookup)
        onehots.append(onehot)
    cond_low = jax.nn.silu(pre_act).astype(jnp.bfloat16)
    ada_rows = matmul(cond_low, ada_all)
    shift_one, scale_one, gate_one, shift_two, scale_two, gate_two = [
        portion[:, None, :] for portion in jnp.split(ada_rows, 6, axis=1)
    ]
    resid_in = tokens.astype(jnp.float32)
    normed_one, inv_one = normalize(resid_in)
    break_rows = break_mask.astype(jnp.float32)[:, :, None]
    h_one_low = (
        normed_one * (1.0 + scale_one) + shift_one + break_rows * break_all.astype(jnp.float32)
    )
    h_one_low = h_one_low.astype(jnp.bfloat16).reshape(row_count, model_width)
    proj_qkv = (
        matmul(h_one_low, qkv_all).astype(jnp.bfloat16).reshape(windows, length, 3 * model_width)
    )
    pair_normed, pair_inv = normalize(pair_all.astype(jnp.float32))
    pair_low = pair_normed.astype(jnp.bfloat16)
    bias_table = matmul(pair_low, proj_all).astype(jnp.bfloat16)
    attended, log_total = lax.map(
        partial(attend, bias_table=bias_table), (proj_qkv, chain_ids, res_counts)
    )
    attended_rows = attended.reshape(row_count, model_width)
    attn_proj = matmul(attended_rows, out_all).reshape(windows, length, model_width)
    middle = resid_in + gate_one * attn_proj
    normed_two, inv_two = normalize(middle)
    h_two_low = (
        (normed_two * (1.0 + scale_two) + shift_two)
        .astype(jnp.bfloat16)
        .reshape(row_count, model_width)
    )
    gate_pre = matmul(h_two_low, gate_all)
    up_pre = matmul(h_two_low, up_all)
    activated = (jax.nn.silu(gate_pre) * up_pre).astype(jnp.bfloat16)
    ffn_out = matmul(activated, down_all).reshape(windows, length, model_width)
    output = middle + gate_two * ffn_out
    return {
        "output": output,
        "pre_act": pre_act,
        "onehots": onehots,
        "cond_low": cond_low,
        "scales": (scale_one, gate_one, scale_two, gate_two),
        "normed_one": normed_one,
        "inv_one": inv_one,
        "break_rows": break_rows,
        "h_one_low": h_one_low,
        "proj_qkv": proj_qkv,
        "pair_normed": pair_normed,
        "pair_inv": pair_inv,
        "pair_low": pair_low,
        "bias_table": bias_table,
        "log_total": log_total,
        "attended_rows": attended_rows,
        "attn_proj": attn_proj,
        "normed_two": normed_two,
        "inv_two": inv_two,
        "h_two_low": h_two_low,
        "gate_pre": gate_pre,
        "up_pre": up_pre,
        "activated": activated,
        "ffn_out": ffn_out,
    }


def shards(
    tokens,
    cotangent,
    time_embed,
    cath_class,
    cath_arch,
    cath_topo,
    res_counts,
    chain_ids,
    break_mask,
    w_ada,
    w_qkv,
    w_out,
    w_gate,
    w_up,
    w_down,
    table_class,
    table_arch,
    table_topo,
    break_vec,
    pair_table,
    pair_proj,
):
    attn_set = (
        lax.all_gather(w_ada, "fsdp", axis=0, tiled=True),
        lax.all_gather(w_qkv, "fsdp", axis=0, tiled=True),
        lax.all_gather(w_out, "fsdp", axis=0, tiled=True),
        lax.all_gather(table_class, "fsdp", axis=1, tiled=True),
        lax.all_gather(table_arch, "fsdp", axis=1, tiled=True),
        lax.all_gather(table_topo, "fsdp", axis=1, tiled=True),
        lax.all_gather(break_vec, "fsdp", axis=0, tiled=True),
        lax.all_gather(pair_table, "fsdp", axis=1, tiled=True),
        lax.all_gather(pair_proj, "fsdp", axis=0, tiled=True),
    )
    mlp_set = (
        lax.all_gather(w_gate, "fsdp", axis=0, tiled=True),
        lax.all_gather(w_up, "fsdp", axis=0, tiled=True),
        lax.all_gather(w_down, "fsdp", axis=1, tiled=True),
    )
    saved = forward(
        tokens,
        time_embed,
        cath_class,
        cath_arch,
        cath_topo,
        res_counts,
        chain_ids,
        break_mask,
        attn_set,
        mlp_set,
    )
    output = saved["output"].astype(jnp.bfloat16)
    attn_set = (
        lax.all_gather(w_ada, "fsdp", axis=0, tiled=True),
        lax.all_gather(w_qkv, "fsdp", axis=0, tiled=True),
        lax.all_gather(w_out, "fsdp", axis=0, tiled=True),
        lax.all_gather(table_class, "fsdp", axis=1, tiled=True),
        lax.all_gather(table_arch, "fsdp", axis=1, tiled=True),
        lax.all_gather(table_topo, "fsdp", axis=1, tiled=True),
        lax.all_gather(break_vec, "fsdp", axis=0, tiled=True),
        lax.all_gather(pair_table, "fsdp", axis=1, tiled=True),
        lax.all_gather(pair_proj, "fsdp", axis=0, tiled=True),
    )
    mlp_set = (
        lax.all_gather(w_gate, "fsdp", axis=0, tiled=True),
        lax.all_gather(w_up, "fsdp", axis=0, tiled=True),
        lax.all_gather(w_down, "fsdp", axis=1, tiled=True),
    )
    saved = forward(
        tokens,
        time_embed,
        cath_class,
        cath_arch,
        cath_topo,
        res_counts,
        chain_ids,
        break_mask,
        attn_set,
        mlp_set,
    )
    ada_all, qkv_all, out_all, class_all, arch_all, topo_all, break_all, pair_all, proj_all = (
        attn_set
    )
    gate_all, up_all, down_all = mlp_set
    windows, length, model_width = tokens.shape
    row_count = windows * length
    scale_one, gate_one, scale_two, gate_two = saved["scales"]
    grad_rows = cotangent.astype(jnp.float32)
    ffn_out = saved["ffn_out"]
    d_ffn = (gate_two * grad_rows).astype(jnp.bfloat16).reshape(row_count, model_width)
    d_gate_two = jnp.sum(grad_rows * ffn_out, axis=1)
    grad_down = matmul_tn(saved["activated"], d_ffn)
    d_act = matmul_t(d_ffn, down_all)
    gate_pre, up_pre = (saved["gate_pre"], saved["up_pre"])
    sigma = jax.nn.sigmoid(gate_pre)
    d_gate_pre = (d_act * up_pre * sigma * (1.0 + gate_pre * (1.0 - sigma))).astype(jnp.bfloat16)
    d_up_pre = (d_act * gate_pre * sigma).astype(jnp.bfloat16)
    h_two_low = saved["h_two_low"]
    grad_gate = matmul_tn(h_two_low, d_gate_pre)
    grad_up = matmul_tn(h_two_low, d_up_pre)
    d_h_two = (matmul_t(d_gate_pre, gate_all) + matmul_t(d_up_pre, up_all)).reshape(
        windows, length, model_width
    )
    normed_two = saved["normed_two"]
    d_scale_two = jnp.sum(d_h_two * normed_two, axis=1)
    d_shift_two = jnp.sum(d_h_two, axis=1)
    d_middle = grad_rows + normalize_back(normed_two, saved["inv_two"], d_h_two * (1.0 + scale_two))
    d_gate_one = jnp.sum(d_middle * saved["attn_proj"], axis=1)
    d_attn = (gate_one * d_middle).astype(jnp.bfloat16).reshape(row_count, model_width)
    grad_out = matmul_tn(saved["attended_rows"], d_attn)
    d_attended = (
        matmul_t(d_attn, out_all).astype(jnp.bfloat16).reshape(windows, length, model_width)
    )
    bias_table = saved["bias_table"]
    d_qkv, bias_grads = lax.map(
        partial(attend_back, bias_table=bias_table),
        (saved["proj_qkv"], chain_ids, res_counts, saved["log_total"], d_attended),
    )
    d_bias_table = jnp.sum(bias_grads, axis=0)
    d_qkv = d_qkv.reshape(row_count, 3 * model_width)
    h_one_low = saved["h_one_low"]
    grad_qkv = matmul_tn(h_one_low, d_qkv)
    d_h_one = matmul_t(d_qkv, qkv_all).reshape(windows, length, model_width)
    normed_one = saved["normed_one"]
    d_scale_one = jnp.sum(d_h_one * normed_one, axis=1)
    d_shift_one = jnp.sum(d_h_one, axis=1)
    grad_break = jnp.sum(d_h_one * saved["break_rows"], axis=(0, 1))
    d_tokens = d_middle + normalize_back(normed_one, saved["inv_one"], d_h_one * (1.0 + scale_one))
    d_ada = jnp.concatenate(
        [d_shift_one, d_scale_one, d_gate_one, d_shift_two, d_scale_two, d_gate_two], axis=1
    ).astype(jnp.bfloat16)
    grad_ada = matmul_tn(saved["cond_low"], d_ada)
    pre_act = saved["pre_act"]
    sigma_pre = jax.nn.sigmoid(pre_act)
    d_pre = matmul_t(d_ada, ada_all) * sigma_pre * (1.0 + pre_act * (1.0 - sigma_pre))
    onehots = saved["onehots"]
    grad_class = exact_tn(onehots[0].astype(jnp.float32), d_pre)
    grad_arch = exact_tn(onehots[1].astype(jnp.float32), d_pre)
    grad_topo = exact_tn(onehots[2].astype(jnp.float32), d_pre)
    grad_proj = exact_tn(saved["pair_low"].astype(jnp.float32), d_bias_table)
    d_pair_normed = exact_nt(d_bias_table, proj_all.astype(jnp.float32))
    grad_pair = normalize_back(saved["pair_normed"], saved["pair_inv"], d_pair_normed)
    attn_parts = (
        lax.psum_scatter(grad_ada, "fsdp", scatter_dimension=0, tiled=True),
        lax.psum_scatter(grad_qkv, "fsdp", scatter_dimension=0, tiled=True),
        lax.psum_scatter(grad_out, "fsdp", scatter_dimension=0, tiled=True),
        lax.psum_scatter(grad_class, "fsdp", scatter_dimension=1, tiled=True),
        lax.psum_scatter(grad_arch, "fsdp", scatter_dimension=1, tiled=True),
        lax.psum_scatter(grad_topo, "fsdp", scatter_dimension=1, tiled=True),
        lax.psum_scatter(grad_break, "fsdp", scatter_dimension=0, tiled=True),
        lax.psum_scatter(grad_pair, "fsdp", scatter_dimension=1, tiled=True),
        lax.psum_scatter(grad_proj, "fsdp", scatter_dimension=0, tiled=True),
    )
    mlp_parts = (
        lax.psum_scatter(grad_gate, "fsdp", scatter_dimension=0, tiled=True),
        lax.psum_scatter(grad_up, "fsdp", scatter_dimension=0, tiled=True),
        lax.psum_scatter(grad_down, "fsdp", scatter_dimension=1, tiled=True),
    )
    owned = (
        lax.psum(attn_parts[0].astype(jnp.bfloat16), "dp").astype(jnp.float32),
        lax.psum(attn_parts[1].astype(jnp.bfloat16), "dp").astype(jnp.float32),
        lax.psum(attn_parts[2].astype(jnp.bfloat16), "dp").astype(jnp.float32),
        lax.psum(mlp_parts[0].astype(jnp.bfloat16), "dp").astype(jnp.float32),
        lax.psum(mlp_parts[1].astype(jnp.bfloat16), "dp").astype(jnp.float32),
        lax.psum(mlp_parts[2].astype(jnp.bfloat16), "dp").astype(jnp.float32),
        lax.psum(attn_parts[3].astype(jnp.bfloat16), "dp").astype(jnp.float32),
        lax.psum(attn_parts[4].astype(jnp.bfloat16), "dp").astype(jnp.float32),
        lax.psum(attn_parts[5].astype(jnp.bfloat16), "dp").astype(jnp.float32),
        lax.psum(attn_parts[6].astype(jnp.bfloat16), "dp").astype(jnp.float32),
        lax.psum(attn_parts[7].astype(jnp.bfloat16), "dp").astype(jnp.float32),
        lax.psum(attn_parts[8].astype(jnp.bfloat16), "dp").astype(jnp.float32),
    )
    return (
        output,
        d_tokens.astype(jnp.bfloat16),
        owned[0],
        owned[1],
        owned[2],
        owned[3],
        owned[4],
        owned[5],
        owned[6],
        owned[7],
        owned[8],
        owned[9],
        owned[10],
        owned[11],
    )


mesh_ids = pl.DeviceIdType.MESH
f32 = jnp.float32
b16 = jnp.bfloat16
core_count = 2
chip_count = 8
shard_rows = 48
chunk_cols = 3072
chunk_count = 4
side_cols = 768
ring_cols = 2304
job_cols = 384
jobs_in_chunk = 6
job_count = 24
ahead = 3
gather_stride = 2
scatter_stride = 2
grad_buffers = 3
plan = (1, 1, 1, 1, 1, 1, 1, 1, 1, 1, 5)
ahead_plan = (2, 2, 2, 2, 2)


def dot_nn(left, right):
    return jnp.dot(left, right, preferred_element_type=f32)


def dot_nt(left, right):
    return lax.dot_general(left, right, (((1,), (1,)), ((), ())), preferred_element_type=f32)


def dot_tn(left, right):
    return lax.dot_general(left, right, (((0,), (0,)), ((), ())), preferred_element_type=f32)


def on(condition, body):
    if isinstance(condition, bool):
        if condition:
            body()
    else:
        pl.when(condition)(body)


def both(first, second):
    if isinstance(first, bool) and isinstance(second, bool):
        return first and second
    return jnp.logical_and(first, second)


def quot(value, by):
    return value // by if isinstance(value, int) else lax.div(value, by)


def modulo(value, by):
    return value % by if isinstance(value, int) else lax.rem(value, by)


def aligned(value, by=128):
    return value if isinstance(value, int) else pl.multiple_of(value, by)


class Place:
    def __init__(self):
        self.x = lax.axis_index("dp")
        self.f = lax.axis_index("fsdp")
        self.me = self.x * 16 + self.f
        self.c = lax.rem(self.f, 2)
        self.cy = lax.div(self.f, 2)
        y = lax.rem(self.cy, 2)
        z = lax.div(self.cy, 2)
        self.p = z * (1 - y) + (7 - z) * y

    def chip(self, position):
        position = lax.rem(position + 16, 8)
        half = lax.div(position, 4)
        return 2 * position * (1 - half) + (15 - 2 * position) * half

    def ring_id(self, position):
        return (self.x, self.chip(position) * 2 + self.c)

    def plane_id(self):
        return (1 - self.x, self.f)

    def core_id(self):
        return (self.x, self.cy * 2 + 1 - self.c)


def greet_all(at):
    barrier = pltpu.get_barrier_semaphore()

    @pl.loop(1, 32)
    def _(step):
        other = lax.rem(at.me + step, 32)
        pl.semaphore_signal(
            barrier,
            inc=1,
            device_id=(lax.div(other, 16), lax.rem(other, 16)),
            device_id_type=mesh_ids,
        )

    pl.semaphore_wait(barrier, 31)


def remote(src, dst, send_sem, recv_sem, device_id):
    return pltpu.make_async_remote_copy(
        src_ref=src,
        dst_ref=dst,
        send_sem=send_sem,
        recv_sem=recv_sem,
        device_id=device_id,
        device_id_type=mesh_ids,
    )


def job_column(at, job):
    chunk = quot(job, jobs_in_chunk)
    inner = modulo(job, jobs_in_chunk)
    base = chunk * chunk_cols + inner * job_cols
    if isinstance(job, int):
        return aligned(base + (at.x * ring_cols if inner < 2 else 0))
    side = 1 - jnp.minimum(lax.div(inner, 2), 1)
    return aligned(base + side * at.x * ring_cols)


class Gather:
    def __init__(self, at, packed, held, sems):
        self.at = at
        self.packed = packed
        self.held = held
        (
            self.ring_send,
            self.ring_recv,
            self.side_send,
            self.side_recv,
            self.core_send,
            self.core_recv,
        ) = sems

    def ring(self, job, step, way, hop):
        at = self.at
        sign = 1 - 2 * way
        column = pl.ds(job_column(at, job), job_cols)
        block = self.held.at[at.chip(at.p - (step + hop) * sign), at.c, :, column]
        src = self.packed.at[:, column] if step == 0 and hop == 0 else block
        return remote(
            src,
            block,
            self.ring_send.at[job, step, way],
            self.ring_recv.at[job, step, way],
            at.ring_id(at.p + sign),
        )

    def relay(self, job, step, way):
        at = self.at
        sign = 1 - 2 * way
        column = pl.ds(job_column(at, job), job_cols)
        block = self.held.at[at.chip(at.p - (step + 1) * sign), at.c, :, column]
        self.pass_on(block, block, job)

    def pass_on(self, src, dst, job):
        at = self.at
        chunk = quot(job, jobs_in_chunk)
        inner = modulo(job, jobs_in_chunk)
        slot = chunk * 2
        remote(
            src, dst, self.core_send.at[slot], self.core_recv.at[slot], at.core_id()
        ).start()

        def across():
            spot = chunk * 2 + inner
            remote(
                src, dst, self.side_send.at[spot], self.side_recv.at[spot], at.plane_id()
            ).start()

        on(inner < 2, across)

    def side(self, job, mine):
        at = self.at
        chunk = quot(job, jobs_in_chunk)
        inner = modulo(job, jobs_in_chunk)
        owner = at.x if mine else 1 - at.x
        column = aligned(chunk * chunk_cols + inner * job_cols + owner * ring_cols)
        block = self.held.at[:, at.c, :, pl.ds(column, job_cols)]
        slot = chunk * 2 + inner
        return remote(
            block, block, self.side_send.at[slot], self.side_recv.at[slot], at.plane_id()
        )

    def core(self, chunk, part, mine):
        at = self.at
        if part == 0:
            column, width = chunk * chunk_cols + at.x * side_cols, ring_cols
        else:
            column, width = chunk * chunk_cols + (1 - at.x) * ring_cols, side_cols
        row = at.c if mine else 1 - at.c
        block = self.held.at[:, row, :, pl.ds(aligned(column), width)]
        slot = chunk * 2 + part
        return remote(block, block, self.core_send.at[slot], self.core_recv.at[slot], at.core_id())

    def start(self, job):
        self.ring(job, 0, 0, 0).start()
        self.ring(job, 0, 1, 0).start()
        at = self.at
        column = pl.ds(job_column(at, job), job_cols)
        self.pass_on(self.packed.at[:, column], self.held.at[at.cy, at.c, :, column], job)

    def tick(self, tau):
        def valid(job):
            return both(job >= 0, job < job_count)

        for step in (4, 3, 2, 1):
            job = tau - step * gather_stride

            def advance(job=job, step=step):
                if step < 4:
                    ways = (0, 1)
                else:
                    ways = (modulo(job, 2),)
                for way in ways:
                    self.ring(job, step - 1, way, 1).wait_recv()
                if step < 3:
                    self.ring(job, step, 0, 0).start()
                    self.ring(job, step, 1, 0).start()
                elif step == 3:
                    self.ring(job, 3, modulo(job, 2), 0).start()
                for way in ways:
                    self.relay(job, step - 1, way)

            on(valid(job), advance)
        on(valid(tau + ahead), lambda: self.start(tau + ahead))

        late = tau - 4 * gather_stride - jobs_in_chunk

        def side_done():
            chunk = quot(late, jobs_in_chunk)
            self.side(chunk * jobs_in_chunk, False).wait_recv()
            self.side(chunk * jobs_in_chunk + 1, False).wait_recv()
            self.core(chunk, 1, True).start()

        on(both(valid(late), modulo(late + 60, jobs_in_chunk) == 0), side_done)

    def arrive(self, chunk):
        self.core(chunk, 0, False).wait_recv()
        self.core(chunk, 1, False).wait_recv()

    def finish(self):
        @pl.loop(0, job_count)
        def _(job):
            for step in range(3):
                self.ring(job, step, 0, 0).wait_send()
                self.ring(job, step, 1, 0).wait_send()
            self.ring(job, 3, lax.rem(job, 2), 0).wait_send()

        for chunk in range(chunk_count):
            for inner in range(2):
                self.side(chunk * jobs_in_chunk + inner, True).wait_send()
                self.core(chunk, inner, True).wait_send()


def class_map(class_count):
    spot = lax.broadcasted_iota(jnp.int32, (512, class_count), 0)
    spot = jnp.where(spot < 384, spot, spot - 512)
    reach = class_count // 2 - 1
    label = jnp.clip(128 - spot, -reach, reach) + reach
    kind = lax.broadcasted_iota(jnp.int32, (512, class_count), 1)
    return (label == kind).astype(f32).astype(b16)


def forward_kernel(
    packed,
    tokens,
    cotangent,
    first_note,
    pair_note,
    ada_shard,
    tables,
    rows,
    output,
    held_out,
    h_one_out,
    qkv_out,
    probs_out,
    attended_out,
    proj_out,
    middle_out,
    h_two_out,
    gate_out,
    up_out,
    act_out,
    ada_out,
    d_gate_two_out,
    pre_out,
    note_out,
    pair_out,
    held,
    note_in,
    pair_in,
    part_rows,
    part_in,
    normed,
    h_one,
    qkv,
    bias,
    edges,
    probs,
    attended,
    proj,
    middle,
    h_two,
    gate,
    up,
    act,
    total,
    out_low,
    ring_send,
    ring_recv,
    side_send,
    side_recv,
    core_send,
    core_recv,
    note_send,
    note_recv,
    pair_send,
    pair_recv,
    part_send,
    part_recv,
    local_sem,
    probs_sem,
    out_sem,
):
    at = Place()
    gather = Gather(
        at, packed, held, (ring_send, ring_recv, side_send, side_recv, core_send, core_recv)
    )
    greet_all(at)

    def lead(index):
        for tau in range(sum(ahead_plan[:index]), sum(ahead_plan[: index + 1])):
            gather.tick(1 + tau)

    def note_copy(step, mine):
        other = lax.rem(at.me + step, 32)
        slot = at.me if mine else other
        return remote(
            first_note.at[lax.rem(other, 16)],
            note_in.at[slot],
            note_send.at[step],
            note_recv.at[slot],
            (lax.div(other, 16), lax.rem(other, 16)),
        )

    def pair_copy(step, mine):
        other = lax.rem(at.f + step, 16)
        slot = at.f if mine else other
        return remote(
            pair_note, pair_in.at[slot], pair_send.at[step], pair_recv.at[slot], (at.x, other)
        )

    def part_copy(step, mine):
        other = lax.rem(at.f + step, 16)
        slot = at.f if mine else other
        return remote(
            part_rows.at[other],
            part_in.at[slot],
            part_send.at[step],
            part_recv.at[slot],
            (at.x, other),
        )

    pl.loop(1, 32)(lambda step: note_copy(step, True).start())
    pl.loop(1, 16)(lambda step: pair_copy(step, True).start())
    for job in range(ahead + 1):
        gather.start(job)
    local = []
    for chunk in range(chunk_count):
        column = pl.ds(aligned(chunk * chunk_cols + at.x * side_cols), ring_cols)
        copy = pltpu.make_async_copy(
            packed.at[:, column], held.at[at.cy, at.c, :, column], local_sem.at[chunk]
        )
        copy.start()
        local.append(copy)
    note_in[at.me] = first_note[at.f]
    pair_in[at.f] = pair_note[...]
    values = tokens[...].astype(f32)
    centred = values - jnp.mean(values, axis=-1, keepdims=True)
    spread = jnp.mean(centred * centred, axis=-1, keepdims=True)
    normed[...] = centred * lax.rsqrt(spread + epsilon)
    for copy in local:
        copy.wait()
    lead(0)

    @pl.loop(1, 32)
    def _(step):
        note_copy(step, False).wait_recv()

    for window in range(32):
        note_out[window : window + 1, :] = note_in[window]
    notes = note_out[...]
    kind = lax.broadcasted_iota(jnp.int32, (32, tables.shape[1]), 1).astype(f32)
    hit = (kind == notes[:, 48:49]) | (kind == notes[:, 49:50]) | (kind == notes[:, 50:51])
    pre = notes[:, 0:48] + dot_nt(hit.astype(f32).astype(b16), tables[...])
    pre_out[...] = jnp.zeros_like(pre_out)
    pre_out[:, 0:48] = pre
    group = pre_out[pl.ds(pl.multiple_of(at.x * 16, 16), 16), :][:, 0:48]
    cond = (group * (1.0 / (1.0 + jnp.exp(-group)))).astype(b16)
    partial_rows = dot_nn(cond, ada_shard[...])
    for row in range(16):
        part_rows[row] = partial_rows[row : row + 1, :]
    lead(1)

    @pl.loop(1, 16)
    def _(step):
        pair_copy(step, False).wait_recv()

    gathered = pair_in[...].reshape(256, 384)
    features = gathered[:, 0:128].astype(f32)
    features = features - jnp.mean(features, axis=0, keepdims=True)
    features = features * lax.rsqrt(jnp.mean(features * features, axis=0, keepdims=True) + epsilon)
    table = dot_tn(gathered[:, 128:256], features.astype(b16))[0:16, :].astype(b16)
    table_wide = table.astype(f32)
    edges[0] = jnp.broadcast_to(table_wide[:, 126:127], (16, 128))
    edges[1] = jnp.broadcast_to(table_wide[:, 0:1], (16, 128))
    edges[2] = jnp.broadcast_to(table_wide[:, 127:128], (16, 128))
    spots = dot_nt(table, class_map(128))
    for head in range(12):
        line = jnp.broadcast_to(spots[head : head + 1, :], (128, 512))
        bias[head] = pltpu.roll(line, 0, 1, stride=1, stride_axis=0)[:, 0:384]
    pl.loop(1, 16)(lambda step: part_copy(step, True).start())
    lead(2)

    breaks = jnp.sum(pair_in[:, :, 256:384].astype(f32), axis=0)
    break_row = jnp.concatenate([breaks[row : row + 1, :] for row in range(6)], axis=1)
    mark_row = rows[1:2, :].astype(b16)
    lead(3)

    @pl.loop(1, 16)
    def _(step):
        part_copy(step, False).wait_recv()

    part_in[at.f] = part_rows[at.f]
    adaptive = part_in[0]
    for row in range(1, 16):
        adaptive = adaptive + part_in[row]
    ada_out[...] = adaptive
    shift_one = adaptive[:, 0:768]
    scale_one = adaptive[:, 768:1536]
    gate_one = adaptive[:, 1536:2304]
    shift_two = adaptive[:, 2304:3072]
    scale_two = adaptive[:, 3072:3840]
    gate_two = adaptive[:, 3840:4608]
    lead(4)
    first = normed[...] * (1.0 + scale_one) + shift_one
    h_one[...] = (first + dot_tn(mark_row, break_row.astype(b16))).astype(b16)
    outgoing = []

    def emit(src, dst):
        copy = pltpu.make_async_copy(src, dst, out_sem.at[len(outgoing)])
        copy.start()
        outgoing.append(copy)

    emit(h_one, h_one_out)
    emit(pair_in, pair_out)
    for tau in range(1 + sum(ahead_plan), 15):
        gather.tick(tau)

    def weights(column, width):
        return held[:, :, :, column : column + width].reshape(768, width)

    def settle(chunk):
        gather.arrive(chunk)
        column = pl.ds(chunk * chunk_cols, chunk_cols)
        emit(held.at[:, :, :, column], held_out.at[:, :, :, column])

    settle(0)
    for piece in range(3):
        span = slice(piece * 768, piece * 768 + 768)
        qkv[:, span] = dot_nn(h_one[...], weights(piece * 768, 768)).astype(b16)
        if piece < 2:
            gather.tick(15 + piece)
    emit(qkv, qkv_out)
    chain_row = rows[0:1, :]
    pad_row = rows[2:3, :]
    first_size = 512.0 - jnp.sum(chain_row, axis=1, keepdims=True)
    low_lane = lax.broadcasted_iota(jnp.int32, (1, 128), 1) < 64
    line_number = lax.broadcasted_iota(jnp.int32, (128, 128), 0).astype(f32)

    def probs_copy(pair):
        slot = modulo(pair, 2)
        return pltpu.make_async_copy(
            probs.at[slot], probs_out.at[pl.ds(pair * 2, 2)], probs_sem.at[slot]
        )

    @pl.loop(0, 6)
    def _(pair):
        lane = pl.multiple_of(pair * 128, 128)
        slot = lax.rem(pair, 2)
        on(pair >= 2, lambda: probs_copy(pair - 2).wait())
        queries = qkv[:, pl.ds(lane, 128)] * jnp.asarray(0.125, b16)
        keys = qkv[:, pl.ds(768 + lane, 128)]
        content = qkv[:, pl.ds(1536 + lane, 128)]
        mixed = []
        for half in range(2):
            head = pair * 2 + half
            own = low_lane if half == 0 else jnp.logical_not(low_lane)
            raw = dot_nt(jnp.where(own, queries, jnp.zeros_like(queries)), keys)
            far_low = edges[0, pl.ds(head, 1), :]
            far_high = edges[1, pl.ds(head, 1), :]
            apart = edges[2, pl.ds(head, 1), :]
            for block in range(4):
                chain_here = (line_number + 128.0 * block >= first_size).astype(f32)
                tiles = []
                for other in range(4):
                    offset = block - other
                    if offset > 1:
                        near = far_low
                    elif offset < -1:
                        near = far_high
                    else:
                        near = bias[head, :, (1 - offset) * 128 : (2 - offset) * 128]
                    there = chain_row[:, other * 128 : other * 128 + 128]
                    near = jnp.where(chain_here == there, near, apart)
                    tiles.append(
                        raw[block * 128 : block * 128 + 128, other * 128 : other * 128 + 128]
                        + near
                        + pad_row[:, other * 128 : other * 128 + 128]
                    )
                scores = jnp.concatenate(tiles, axis=1)
                scores = jnp.exp(scores - jnp.max(scores, axis=1, keepdims=True))
                scores = scores * (1.0 / jnp.sum(scores, axis=1, keepdims=True))
                probs[slot, half, block * 128 : block * 128 + 128, :] = scores.astype(b16)
            mixed.append(dot_nn(probs[slot, half], content))
        attended[:, pl.ds(lane, 128)] = jnp.where(low_lane, mixed[0], mixed[1]).astype(b16)
        probs_copy(pair).start()
        spot = 17 + pair + lax.div(pair, 2)
        gather.tick(spot)
        on(lax.rem(pair, 2) == 1, lambda: gather.tick(spot + 1))

    emit(attended, attended_out)
    projected = dot_nn(attended[...], weights(2304, 768))
    proj[...] = projected.astype(b16)
    middle[...] = tokens[...].astype(f32) + gate_one * projected
    emit(proj, proj_out)
    emit(middle, middle_out)
    gather.tick(26)
    values = middle[...]
    centred = values - jnp.mean(values, axis=-1, keepdims=True)
    spread = jnp.mean(centred * centred, axis=-1, keepdims=True)
    second = centred * lax.rsqrt(spread + epsilon) * (1.0 + scale_two) + shift_two
    h_two[...] = second.astype(b16)
    emit(h_two, h_two_out)
    gather.tick(27)

    settle(1)

    def moving(column):
        return held[:, :, :, pl.ds(pl.multiple_of(column, 128), 768)].reshape(768, 768)

    @pl.loop(0, 4)
    def _(piece):
        span = pl.ds(pl.multiple_of(piece * 768, 128), 768)
        gate[:, span] = dot_nn(h_two[...], moving(3072 + piece * 768)).astype(b16)
        on(lax.rem(piece, 2) == 1, lambda: gather.tick(28 + lax.div(piece, 2)))

    emit(gate, gate_out)
    settle(2)

    @pl.loop(0, 4)
    def _(piece):
        span = pl.ds(pl.multiple_of(piece * 768, 128), 768)
        raised = dot_nn(h_two[...], moving(6144 + piece * 768))
        gated = gate[:, span].astype(f32)
        up[:, span] = raised.astype(b16)
        act[:, span] = (gated * (1.0 / (1.0 + jnp.exp(-gated))) * raised).astype(b16)
        on(piece < 3, lambda: gather.tick(30 + piece))

    emit(up, up_out)
    emit(act, act_out)
    settle(3)
    total[...] = dot_nt(act[...], weights(9216, 3072))
    fed = total[...]
    d_gate_two_out[...] = jnp.sum(cotangent[...].astype(f32) * fed, axis=0, keepdims=True)
    out_low[...] = (middle[...] + gate_two * fed).astype(b16)
    emit(out_low, output)

    probs_copy(4).wait()
    probs_copy(5).wait()
    gather.finish()
    for copy in outgoing:
        copy.wait()

    @pl.loop(1, 32)
    def _(step):
        note_copy(step, True).wait_send()

    @pl.loop(1, 16)
    def _(step):
        pair_copy(step, True).wait_send()
        part_copy(step, True).wait_send()


def run_forward(packed, tokens, cotangent, first_note, pair_note, ada_shard, tables, rows):
    anywhere = pl.BlockSpec(memory_space=pl.ANY)
    near = pl.BlockSpec(memory_space=pltpu.VMEM)
    shape = jax.ShapeDtypeStruct
    dma = pltpu.SemaphoreType.DMA
    vmem = pltpu.VMEM
    width = 768
    outs = [
        (shape((512, width), b16), anywhere),
        (shape((8, 2, 48, 12288), b16), anywhere),
        (shape((512, width), b16), anywhere),
        (shape((512, 3 * width), b16), anywhere),
        (shape((12, 512, 512), b16), anywhere),
        (shape((512, width), b16), anywhere),
        (shape((512, width), b16), anywhere),
        (shape((512, width), f32), anywhere),
        (shape((512, width), b16), anywhere),
        (shape((512, 3072), b16), anywhere),
        (shape((512, 3072), b16), anywhere),
        (shape((512, 3072), b16), anywhere),
        (shape((1, 4608), f32), near),
        (shape((1, width), f32), near),
        (shape((32, 128), f32), near),
        (shape((32, 128), f32), near),
        (shape((16, 16, 384), b16), anywhere),
    ]
    scratch = [
        vmem((8, 2, 48, 12288), b16),
        vmem((32, 1, 128), f32),
        vmem((16, 16, 384), b16),
        vmem((16, 1, 4608), f32),
        vmem((16, 1, 4608), f32),
        vmem((512, width), f32),
        vmem((512, width), b16),
        vmem((512, 3 * width), b16),
        vmem((12, 128, 384), f32),
        vmem((3, 16, 128), f32),
        vmem((2, 2, 512, 512), b16),
        vmem((512, width), b16),
        vmem((512, width), b16),
        vmem((512, width), f32),
        vmem((512, width), b16),
        vmem((512, 3072), b16),
        vmem((512, 3072), b16),
        vmem((512, 3072), b16),
        vmem((512, width), f32),
        vmem((512, width), b16),
        dma((job_count, 4, 2)),
        dma((job_count, 4, 2)),
        dma((8,)),
        dma((8,)),
        dma((8,)),
        dma((8,)),
        dma((32,)),
        dma((32,)),
        dma((16,)),
        dma((16,)),
        dma((16,)),
        dma((16,)),
        dma((4,)),
        dma((2,)),
        dma((24,)),
    ]
    return pl.pallas_call(
        forward_kernel,
        name="forward",
        out_shape=[one for one, _ in outs],
        in_specs=[anywhere] + [near] * 7,
        out_specs=[spec for _, spec in outs],
        scratch_shapes=scratch,
        compiler_params=pltpu.CompilerParams(
            collective_id=0, has_side_effects=True, vmem_limit_bytes=66_000_000
        ),
    )(packed, tokens, cotangent, first_note, pair_note, ada_shard, tables, rows)


side_jobs = 2
messages_in_job = 7


class Scatter:
    def __init__(self, at, grads, ring_in, core_in, side_in, last_in, summed, sems):
        self.at = at
        self.grads = grads
        self.ring_in = ring_in
        self.core_in = core_in
        self.side_in = side_in
        self.last_in = last_in
        self.summed = summed
        self.now = 0
        self.begun = []
        (
            self.ring_send,
            self.ring_recv,
            self.core_send,
            self.core_recv,
            self.side_send,
            self.side_recv,
            self.last_send,
            self.last_recv,
            self.credit,
        ) = sems

    def column(self, job, owner):
        inner = modulo(job, jobs_in_chunk)
        outer = quot(inner, 4)
        return aligned(inner * job_cols + side_cols + outer * (owner * ring_cols - ring_cols))

    def block(self, job, position):
        at = self.at
        buffer = modulo(quot(job, jobs_in_chunk), grad_buffers)
        span = pl.ds(self.column(job, at.x), job_cols)
        return self.grads.at[buffer, at.chip(position), at.c, :, span]

    def slot(self, job, step, way):
        return job * messages_in_job + (0 if step == 0 else 2 * step - 1 + way)

    def ring(self, job, step, way):
        at = self.at
        sign = 1 - 2 * way
        slot = self.slot(job, step, way)
        return remote(
            self.block(job, at.p + (4 - step) * sign),
            self.ring_in.at[slot],
            self.ring_send.at[slot],
            self.ring_recv.at[slot],
            at.ring_id(at.p + sign),
        )

    def absorb(self, job, step, way):
        self.ring(job, step, way).wait_recv()
        sign = 1 - 2 * way
        own = self.block(job, self.at.p + (3 - step) * sign)
        came = self.ring_in[self.slot(job, step, way)]
        own[...] = (own[...].astype(f32) + came.astype(f32)).astype(b16)

    def core(self, turn, piece):
        at = self.at
        span = pl.ds(aligned(piece * side_cols), side_cols)
        return remote(
            self.grads.at[turn % grad_buffers, :, 1 - at.c, :, span],
            self.core_in.at[turn % 2, piece],
            self.core_send.at[turn, piece],
            self.core_recv.at[turn, piece],
            at.core_id(),
        )

    def core_start(self, turn, piece):
        if turn >= 2:
            pl.semaphore_wait(self.credit.at[turn % 2, piece], 1)
        self.core(turn, piece).start()

    def core_add(self, turn, piece):
        at = self.at
        self.core(turn, piece).wait_recv()
        span = pl.ds(piece * side_cols, side_cols)

        @pl.loop(0, chip_count)
        def _(chip):
            own = self.grads.at[turn % grad_buffers, chip, at.c, :, span]
            came = self.core_in[turn % 2, piece, chip]
            own[...] = (own[...].astype(f32) + came.astype(f32)).astype(b16)

        if turn < 2:
            pl.semaphore_signal(
                self.credit.at[turn % 2, piece],
                inc=1,
                device_id=at.core_id(),
                device_id_type=mesh_ids,
            )

    def side(self, turn, half):
        at = self.at
        span = pl.ds(aligned((1 - at.x) * ring_cols + half * job_cols), job_cols)
        slot = turn * side_jobs + half
        return remote(
            self.grads.at[modulo(turn, grad_buffers), :, at.c, :, span],
            self.side_in.at[slot],
            self.side_send.at[slot],
            self.side_recv.at[slot],
            at.plane_id(),
        )

    def side_add(self, turn, half):
        at = self.at
        self.side(turn, half).wait_recv()
        span = pl.ds(aligned(at.x * ring_cols + half * job_cols), job_cols)

        @pl.loop(0, chip_count)
        def _(chip):
            own = self.grads.at[modulo(turn, grad_buffers), chip, at.c, :, span]
            came = self.side_in[turn * side_jobs + half, chip]
            own[...] = (own[...].astype(f32) + came.astype(f32)).astype(b16)

    def last(self, job):
        return remote(
            self.block(job, self.at.p),
            self.last_in.at[job],
            self.last_send.at[job],
            self.last_recv.at[job],
            self.at.plane_id(),
        )

    def store(self, job):
        at = self.at
        self.last(job).wait_recv()
        turn = quot(job, jobs_in_chunk)
        inner = modulo(job, jobs_in_chunk)
        if isinstance(job, int):
            chunk = (3, 1, 2, 0)[turn]
        else:
            chunk = turn + 3 * (1 - jnp.minimum(turn, 1)) - 3 * lax.div(turn, 3)
        base = chunk * chunk_cols
        mine = self.block(job, at.p)[...].astype(f32)
        other = self.last_in[job].astype(f32)

        def whole():
            span = pl.ds(aligned(base + self.column(job, at.x)), job_cols)
            self.summed[:, span] = mine + other

        def halves():
            span = pl.ds(aligned(base + self.column(job, at.x)), job_cols)
            self.summed[:, span] = mine
            span = pl.ds(aligned(base + self.column(job, 1 - at.x)), job_cols)
            self.summed[:, span] = other

        on(inner < 4, whole)
        on(inner >= 4, halves)

    def begin(self, turn, beside, wait=0):
        first = self.now + wait
        assert not self.begun or first >= self.begun[-1][0] + self.begun[-1][2]
        base = turn * jobs_in_chunk
        self.begun.append((first, base + 4, 2) if beside else (first, base, 4))

    def step(self, count=1):
        for _ in range(count):
            self.tick(self.now)
            self.now += 1

    def drain(self):
        last = self.begun[-1][0] + 2 + 4 * scatter_stride + 2
        pl.loop(self.now, last)(self.tick)
        self.now = last

    def tick(self, tau):
        def each(age, body):
            spot = tau - age
            if isinstance(spot, int):
                for first, base, count in self.begun:
                    if 0 <= spot - first < count:
                        body(base + spot - first)
                return
            job = jnp.int32(-1)
            for first, base, count in self.begun:
                inside = jnp.logical_and(spot >= first, spot < first + count)
                job = jnp.where(inside, spot - first + base, job)
            pl.when(job >= 0)(lambda: body(job))

        def two(step, body):
            def run(job):
                body(job, step, 0)
                body(job, step, 1)

            return run

        def start(job, step, way):
            self.ring(job, step, way).start()

        gap = scatter_stride
        each(4 * gap, two(3, self.absorb))
        each(3 * gap, two(2, self.absorb))
        each(2 * gap, two(1, self.absorb))
        each(gap, lambda job: self.absorb(job, 0, modulo(job, 2)))

        def beside(job):
            inner = modulo(job, jobs_in_chunk)
            turn = quot(job, jobs_in_chunk)
            on(inner == 4, lambda: self.side_add(turn, 0))
            on(inner == 5, lambda: self.side_add(turn, 1))

        each(0, beside)
        each(3 * gap, two(3, start))
        each(2 * gap, two(2, start))
        each(gap, two(1, start))
        each(0, lambda job: start(job, 0, modulo(job, 2)))
        each(4 * gap, lambda job: self.last(job).start())
        each(4 * gap + 2, self.store)

    def sent(self, turns):
        @pl.loop(turns[0] * jobs_in_chunk, turns[-1] * jobs_in_chunk + jobs_in_chunk)
        def _(job):
            self.ring(job, 0, lax.rem(job, 2)).wait_send()
            for step in range(1, 4):
                self.ring(job, step, 0).wait_send()
                self.ring(job, step, 1).wait_send()
            self.last(job).wait_send()

        for turn in turns:
            for piece in range(4):
                self.core(turn, piece).wait_send()
            for half in range(2):
                self.side(turn, half).wait_send()


def halves_of(values):
    high = values.astype(b16)
    return high, (values - high.astype(f32)).astype(b16)


def backward_kernel(
    held,
    probs_all,
    h_one_all,
    qkv_all,
    attended_all,
    proj_all,
    middle_all,
    h_two_all,
    gate_all,
    up_all,
    act_all,
    tokens_all,
    cotangent_all,
    adaptive,
    d_gate_two,
    pre_all,
    notes,
    pair_all,
    ada_shard,
    rows,
    d_tokens_out,
    summed,
    grad_ada,
    grad_tables,
    grad_pair,
    grad_proj,
    grad_break,
    grads,
    ring_in,
    core_in,
    side_in,
    last_in,
    piece_in,
    probs,
    d_scores,
    cot,
    act,
    gate,
    up,
    hidden,
    mid,
    d_mid,
    d_hid,
    proj,
    low,
    sums,
    lines,
    far,
    note_wide,
    note_low,
    vector_in,
    vector_wide,
    d_ada_all,
    pair_work,
    ring_send,
    ring_recv,
    core_send,
    core_recv,
    side_send,
    side_recv,
    last_send,
    last_recv,
    credit,
    load_sem,
    piece_sem,
    probs_sem,
    vector_send,
    vector_recv,
    share_send,
    share_recv,
):
    at = Place()
    scatter = Scatter(
        at,
        grads,
        ring_in,
        core_in,
        side_in,
        last_in,
        summed,
        (
            ring_send,
            ring_recv,
            core_send,
            core_recv,
            side_send,
            side_recv,
            last_send,
            last_recv,
            credit,
        ),
    )
    loads = []

    def load(src, dst):
        copy = pltpu.make_async_copy(src, dst, load_sem.at[len(loads)])
        copy.start()
        loads.append(copy)
        return copy

    cot_load = load(cotangent_all, cot)
    act_load = load(act_all, act)
    piece_order = [9216 + 768 * n for n in range(4)]
    for n in range(4):
        piece_order += [3072 + 768 * n, 6144 + 768 * n]
    piece_order += [2304, 0, 768, 1536]

    def piece_copy(index):
        if isinstance(index, int):
            column = pl.ds(piece_order[index], side_cols)
        else:
            inner = index - 4
            start = 3072 + 768 * lax.div(inner, 2) + 3072 * lax.rem(inner, 2)
            start = jnp.where(index < 4, 9216 + 768 * index, start)
            start = jnp.where(index == 12, 2304, start)
            start = jnp.where(index > 12, (index - 13) * 768, start)
            column = pl.ds(pl.multiple_of(start, 128), side_cols)
        index = modulo(index, 4)
        return pltpu.make_async_copy(
            held.at[:, :, :, column], piece_in.at[index], piece_sem.at[index]
        )

    def piece(index):
        piece_copy(index).wait()
        return piece_in[modulo(index, 4)].reshape(768, 768)

    def piece_used(index):
        on(index + 4 < len(piece_order), lambda: piece_copy(index + 4).start())

    for index in range(4):
        piece_copy(index).start()
    gate_load = load(gate_all, gate)
    up_load = load(up_all, up)
    hidden_load = load(h_two_all, hidden)
    mid_load = load(middle_all, mid)
    proj_load = load(proj_all, proj)

    def probs_copy(pair):
        slot = modulo(pair, 2)
        return pltpu.make_async_copy(
            probs_all.at[pl.ds(pair * 2, 2)], probs.at[slot], probs_sem.at[slot]
        )

    probs_copy(0).start()
    probs_copy(1).start()
    greet_all(at)
    scale_one = adaptive[:, 768:1536]
    gate_one = adaptive[:, 1536:2304]
    scale_two = adaptive[:, 3072:3840]
    gate_two = adaptive[:, 3840:4608]
    sums[...] = jnp.zeros_like(sums)

    def columns(part):
        return pl.ds(aligned(part * 768), 768)

    def put(turn, part, left, right):
        span = columns(part)
        grads[turn % grad_buffers, :, :, :, span] = (
            dot_tn(left, right).astype(b16).reshape(8, 2, 48, 768)
        )
        scatter.core_start(turn, part)

    def merge(turn):
        scatter.core_add(turn, 0)
        scatter.core_add(turn, 3)
        scatter.side(turn, 0).start()
        scatter.side(turn, 1).start()
        scatter.core_add(turn, 1)
        scatter.core_add(turn, 2)
        scatter.begin(turn, False)

    cot_load.wait()
    low[...] = (gate_two * cot[...].astype(f32)).astype(b16)
    act_load.wait()

    @pl.loop(0, 4)
    def _(index):
        part = lax.rem(3 * index, 4)
        put(0, part, low[...], act[:, columns(part)])

    qkv_load = load(qkv_all, act.at[:, 0:2304])
    attended_load = load(attended_all, act.at[:, 2304:3072])
    gate_load.wait()
    up_load.wait()

    def first_part():
        merge(0)

    @pl.loop(0, 4)
    def _(part):
        d_hid[...] = dot_nn(low[...], piece(part))
        piece_used(part)
        span = columns(part)

        @pl.loop(0, 8)
        def _(block):
            line = pl.ds(pl.multiple_of(block * 64, 64), 64)
            d_act = d_hid[line, :]
            gated = gate[line, span].astype(f32)
            raised = up[line, span].astype(f32)
            sigma = 1.0 / (1.0 + jnp.exp(-gated))
            scaled = d_act * sigma
            gate[line, span] = (scaled * raised * (1.0 + gated * (1.0 - sigma))).astype(b16)
            up[line, span] = (scaled * gated).astype(b16)

        on(part == 0, first_part)
        scatter.tick(scatter.now + part)

    scatter.now += 4
    hidden_load.wait()

    @pl.loop(0, 4)
    def _(index):
        part = lax.rem(3 * index, 4)
        put(1, part, hidden[...], gate[:, columns(part)])
        on(index == 1, lambda: scatter.tick(scatter.now))

    scatter.now += 1
    scatter.step(plan[1])

    def second_part():
        merge(1)
        scatter.begin(0, True, 4)
        scatter.tick(scatter.now)

    @pl.loop(0, 4)
    def _(index):
        part = lax.rem(3 * index, 4)
        put(2, part, hidden[...], up[:, columns(part)])
        on(index == 1, second_part)

    scatter.now += 1
    scatter.step(plan[2])
    h_one_load = load(h_one_all, hidden)
    d_hid[...] = jnp.zeros_like(d_hid)

    @pl.loop(0, 4)
    def _(part):
        span = columns(part)
        d_hid[...] += dot_nt(gate[:, span], piece(4 + 2 * part))
        piece_used(4 + 2 * part)
        d_hid[...] += dot_nt(up[:, span], piece(5 + 2 * part))
        piece_used(5 + 2 * part)
        scatter.tick(scatter.now + part)

    scatter.now += 4
    merge(2)
    scatter.begin(1, True, 4)
    scatter.begin(2, True, 12)
    mid_load.wait()
    proj_load.wait()

    @pl.loop(0, 8)
    def _(block):
        line = pl.ds(pl.multiple_of(block * 64, 64), 64)
        values = mid[line, :]
        centred = values - jnp.mean(values, axis=-1, keepdims=True)
        inverse = lax.rsqrt(jnp.mean(centred * centred, axis=-1, keepdims=True) + epsilon)
        centred = centred * inverse
        grad = d_hid[line, :]
        sums[0:1, :] += jnp.sum(grad, axis=0, keepdims=True)
        sums[1:2, :] += jnp.sum(grad * centred, axis=0, keepdims=True)
        grad = grad * (1.0 + scale_two)
        grad = grad - jnp.mean(grad, axis=-1, keepdims=True) - centred * jnp.mean(
            grad * centred, axis=-1, keepdims=True
        )
        grad = cot[line, :].astype(f32) + inverse * grad
        d_mid[line, :] = grad
        sums[2:3, :] += jnp.sum(grad * proj[line, :].astype(f32), axis=0, keepdims=True)
        low[line, :] = (gate_one * grad).astype(b16)

    tokens_load = load(tokens_all, proj)
    scatter.step(plan[4])
    cot[...] = dot_nt(low[...], piece(12)).astype(b16)
    piece_used(12)
    qkv_load.wait()
    attended_load.wait()
    scatter.step(plan[4])
    start_tick = scatter.now

    chain_row = rows[0:1, :]
    first_size = 512.0 - jnp.sum(chain_row, axis=1, keepdims=True)
    low_lane = lax.broadcasted_iota(jnp.int32, (1, 128), 1) < 64
    line_number = lax.broadcasted_iota(jnp.int32, (128, 128), 0).astype(f32)
    lines[...] = jnp.zeros_like(lines)
    far[...] = jnp.zeros_like(far)

    @pl.loop(0, 6)
    def _(pair):
        lane = pl.multiple_of(pair * 128, 128)
        slot = lax.rem(pair, 2)
        probs_copy(pair).wait()
        queries = act[:, pl.ds(lane, 128)] * jnp.asarray(0.125, b16)
        keys = act[:, pl.ds(768 + lane, 128)]
        content = act[:, pl.ds(1536 + lane, 128)]
        d_out = cot[:, pl.ds(lane, 128)]
        d_queries, d_keys, d_content = [], [], []
        for half in range(2):
            head = pair * 2 + half
            own = low_lane if half == 0 else jnp.logical_not(low_lane)
            d_own = jnp.where(own, d_out, jnp.zeros_like(d_out))
            d_probs = dot_nt(d_own, content)
            band = [None, None, None]
            low_sum = jnp.zeros((128, 128), f32)
            high_sum = jnp.zeros((128, 128), f32)
            apart = jnp.zeros((128, 128), f32)
            for block in range(4):
                line = slice(block * 128, block * 128 + 128)
                here = probs[slot, half, line, :].astype(f32)
                weighted = here * d_probs[line, :]
                weighted = weighted - here * jnp.sum(weighted, axis=1, keepdims=True)
                d_scores[line, :] = weighted.astype(b16)
                chain_here = (line_number + 128.0 * block >= first_size).astype(f32)
                for other in range(4):
                    tile = weighted[:, other * 128 : other * 128 + 128]
                    there = chain_row[:, other * 128 : other * 128 + 128]
                    same = jnp.where(chain_here == there, tile, jnp.zeros_like(tile))
                    apart = apart + (tile - same)
                    offset = block - other
                    if offset > 1:
                        low_sum = low_sum + same
                    elif offset < -1:
                        high_sum = high_sum + same
                    elif band[1 - offset] is None:
                        band[1 - offset] = same
                    else:
                        band[1 - offset] = band[1 - offset] + same
            far[0, pl.ds(head, 1), :] = jnp.sum(low_sum, axis=0, keepdims=True)
            far[1, pl.ds(head, 1), :] = jnp.sum(high_sum, axis=0, keepdims=True)
            far[2, pl.ds(head, 1), :] = jnp.sum(apart, axis=0, keepdims=True)
            folded = jnp.concatenate(band + [jnp.zeros((128, 128), f32)], axis=1)
            size = 64
            while size >= 1:
                folded = folded[0:size, :] + pltpu.roll(
                    folded[size : 2 * size, :], 512 - size, 1
                )
                size = size // 2
            lines[pl.ds(head, 1), :] = folded
            d_here = d_scores[...]
            d_queries.append(dot_nn(d_here, keys))
            masked = jnp.where(own, queries, jnp.zeros_like(queries))
            d_keys.append(dot_tn(d_here, masked))
            d_content.append(dot_tn(probs[slot, half], d_own))
            if half == 0:
                for extra in range(plan[5]):
                    scatter.tick(start_tick + (plan[5] + plan[6]) * pair + extra)
        gate[:, pl.ds(lane, 128)] = (
            jnp.where(low_lane, d_queries[0], d_queries[1]) * 0.125
        ).astype(b16)
        gate[:, pl.ds(768 + lane, 128)] = (d_keys[0] + d_keys[1]).astype(b16)
        gate[:, pl.ds(1536 + lane, 128)] = (d_content[0] + d_content[1]).astype(b16)
        on(pair < 4, lambda: probs_copy(pair + 2).start())
        for extra in range(plan[6]):
            scatter.tick(start_tick + (plan[5] + plan[6]) * pair + plan[5] + extra)

    scatter.now += 6 * (plan[5] + plan[6])
    if grad_buffers == 3:
        done = scatter.begun[2][0] + 2 + 4 * scatter_stride + 2
        assert scatter.now >= done and scatter.begun[2][1] == 4
        scatter.sent([0])
    put(3, 3, act[:, 2304:3072], low[...])
    h_one_load.wait()
    put(3, 0, hidden[...], gate[:, 0:768])
    scatter.step(plan[7])
    put(3, 1, hidden[...], gate[:, 768:1536])
    put(3, 2, hidden[...], gate[:, 1536:2304])
    for part in range(3):
        product = dot_nt(gate[:, part * 768 : part * 768 + 768], piece(13 + part))
        if part == 0:
            d_hid[...] = product
        else:
            d_hid[...] += product
        if part == 0:
            merge(3)
            scatter.begin(3, True, plan[10])
        scatter.step(plan[8])
    tokens_load.wait()

    @pl.loop(0, 8)
    def _(block):
        line = pl.ds(pl.multiple_of(block * 64, 64), 64)
        values = proj[line, :].astype(f32)
        centred = values - jnp.mean(values, axis=-1, keepdims=True)
        inverse = lax.rsqrt(jnp.mean(centred * centred, axis=-1, keepdims=True) + epsilon)
        centred = centred * inverse
        grad = d_hid[line, :]
        sums[3:4, :] += jnp.sum(grad, axis=0, keepdims=True)
        sums[4:5, :] += jnp.sum(grad * centred, axis=0, keepdims=True)
        cot[line, :] = grad.astype(b16)
        grad = grad * (1.0 + scale_one)
        grad = grad - jnp.mean(grad, axis=-1, keepdims=True) - centred * jnp.mean(
            grad * centred, axis=-1, keepdims=True
        )
        low[line, :] = (d_mid[line, :] + inverse * grad).astype(b16)

    tokens_store = load(low, d_tokens_out)
    break_sum = dot_nn(jnp.broadcast_to(rows[1:2, :], (8, 512)).astype(b16), cot[...])
    scatter.step(plan[9])

    scale = class_map(128)
    line_high, line_low = halves_of(lines[...])
    d_table = dot_nn(line_high, scale) + dot_nn(line_low, scale)
    kind = lax.broadcasted_iota(jnp.int32, (16, 128), 1)
    for index, label in ((0, 126), (1, 0), (2, 127)):
        total = jnp.sum(far[index], axis=1, keepdims=True)
        d_table = d_table + jnp.where(kind == label, total, jnp.zeros_like(d_table))
    vectors = [sums[3:4, :], sums[4:5, :], sums[2:3, :], sums[0:1, :], sums[1:2, :]]
    vectors.append(d_gate_two[...])
    for index in range(6):
        for part in range(6):
            note_wide[index * 6 + part : index * 6 + part + 1, :] = vectors[index][
                :, part * 128 : part * 128 + 128
            ]
    note_wide[36:48, :] = d_table[0:12, :]
    for part in range(6):
        note_wide[48 + part : 49 + part, :] = break_sum[0:1, part * 128 : part * 128 + 128]
    note_wide[54:64, :] = jnp.zeros((10, 128), f32)
    note_low[...] = note_wide[...].astype(b16)
    vector_in[at.x, at.cy, at.c] = note_low[...]
    scatter.step(plan[9])

    def vector_copy(step, mine):
        other = lax.rem(at.cy + step, 8)
        slot = at.cy if mine else other
        return remote(
            note_low,
            vector_in.at[at.x, slot, at.c],
            vector_send.at[step],
            vector_recv.at[slot],
            (at.x, other * 2 + at.c),
        )

    def plane_copy(plane):
        block = vector_in.at[plane, :, at.c]
        return remote(block, block, share_send.at[0], share_recv.at[0], at.plane_id())

    def pair_copy(core):
        block = vector_in.at[:, :, core]
        return remote(block, block, share_send.at[1], share_recv.at[1], at.core_id())

    for step in range(1, 8):
        vector_copy(step, True).start()
    scatter.step(plan[9])
    for step in range(1, 8):
        vector_copy(step, False).wait_recv()
    plane_copy(at.x).start()
    scatter.step(plan[9])
    plane_copy(1 - at.x).wait_recv()
    pair_copy(at.c).start()
    scatter.step(plan[9])
    pair_copy(1 - at.c).wait_recv()
    total = jnp.zeros((64, 128), f32)
    for plane in range(2):
        vector_wide[...] = vector_in[plane].reshape(1024, 128).astype(f32)
        for part in range(36):
            d_ada_all[plane * 16 : plane * 16 + 16, part * 128 : part * 128 + 128] = vector_wide[
                pl.ds(part, 16, stride=64), :
            ].astype(b16)
        for window in range(16):
            total = total + vector_wide[window * 64 : window * 64 + 64, :]
    note_wide[...] = total
    pre = pre_all[...]
    sigma = 1.0 / (1.0 + jnp.exp(-pre))
    grad_ada[...] = dot_tn((pre * sigma).astype(b16)[:, 0:48], d_ada_all[...])
    d_pre = dot_nt(d_ada_all[...], ada_shard[...])
    pre, sigma = pre[:, 0:48], sigma[:, 0:48]
    d_pre = d_pre * sigma * (1.0 + pre * (1.0 - sigma))
    scatter.step(plan[9])
    labels = notes[...]
    kind = lax.broadcasted_iota(jnp.int32, (32, grad_tables.shape[1]), 1).astype(f32)
    hit = (kind == labels[:, 48:49]) | (kind == labels[:, 49:50]) | (kind == labels[:, 50:51])
    hit = hit.astype(f32).astype(b16)
    high, rest = halves_of(d_pre)
    grad_tables[...] = dot_tn(high, hit) + dot_tn(rest, hit)
    scatter.step(plan[9])
    grad_break[...] = note_wide[48:56, :]
    d_table = note_wide[36:52, :]
    keep = lax.broadcasted_iota(jnp.int32, (16, 128), 0) < 12
    d_table = jnp.where(keep, d_table, jnp.zeros_like(d_table))
    gathered = pair_all[...].reshape(256, 384)
    features = gathered[:, 0:128].astype(f32)
    features = features - jnp.mean(features, axis=0, keepdims=True)
    inverse = lax.rsqrt(jnp.mean(features * features, axis=0, keepdims=True) + epsilon)
    features = features * inverse
    high, rest = halves_of(d_table)
    pair_low = features.astype(b16)
    pair_work[:, 0:16] = dot_nt(pair_low, high) + dot_nt(pair_low, rest)
    mine = pl.ds(pl.multiple_of(at.f * 16, 16), 16)
    grad_proj[...] = pair_work[mine, :]
    weights = gathered[:, 128:144]
    grad = dot_nn(weights, high) + dot_nn(weights, rest)
    grad = inverse * (
        grad
        - jnp.mean(grad, axis=0, keepdims=True)
        - features * jnp.mean(grad * features, axis=0, keepdims=True)
    )
    pair_work[...] = grad
    grad_pair[...] = pair_work[mine, :]
    scatter.drain()
    scatter.sent([1, 2, 3] if grad_buffers == 3 else [0, 1, 2, 3])
    tokens_store.wait()
    for step in range(1, 8):
        vector_copy(step, True).wait_send()
    plane_copy(at.x).wait_send()
    pair_copy(at.c).wait_send()


def run_backward(saved, tokens, cotangent, ada_shard, rows, table_rows):
    (
        held,
        h_one,
        qkv,
        probs,
        attended,
        proj,
        middle,
        h_two,
        gate,
        up,
        act,
        adaptive,
        d_gate_two,
        pre,
        notes,
        pair_all,
    ) = saved
    anywhere = pl.BlockSpec(memory_space=pl.ANY)
    near = pl.BlockSpec(memory_space=pltpu.VMEM)
    shape = jax.ShapeDtypeStruct
    dma = pltpu.SemaphoreType.DMA
    vmem = pltpu.VMEM
    width = 768
    outs = [
        (shape((512, width), b16), anywhere),
        (shape((48, 12288), f32), near),
        (shape((48, 4608), f32), near),
        (shape((48, table_rows), f32), near),
        (shape((16, 128), f32), near),
        (shape((16, 128), f32), near),
        (shape((8, 128), f32), near),
    ]
    ring_slots = job_count * messages_in_job
    scratch = [
        vmem((grad_buffers, 8, 2, 48, chunk_cols), b16),
        vmem((ring_slots, 48, job_cols), b16),
        vmem((2, 4, 8, 48, side_cols), b16),
        vmem((8, 8, 48, job_cols), b16),
        vmem((job_count, 48, job_cols), b16),
        vmem((4, 8, 2, 48, side_cols), b16),
        vmem((2, 2, 512, 512), b16),
        vmem((512, 512), b16),
        vmem((512, width), b16),
        vmem((512, 3072), b16),
        vmem((512, 3072), b16),
        vmem((512, 3072), b16),
        vmem((512, width), b16),
        vmem((512, width), f32),
        vmem((512, width), f32),
        vmem((512, width), f32),
        vmem((512, width), b16),
        vmem((512, width), b16),
        vmem((8, width), f32),
        vmem((16, 512), f32),
        vmem((3, 16, 128), f32),
        vmem((64, 128), f32),
        vmem((64, 128), b16),
        vmem((2, 8, 2, 64, 128), b16),
        vmem((1024, 128), f32),
        vmem((32, 4608), b16),
        vmem((256, 128), f32),
        dma((ring_slots,)),
        dma((ring_slots,)),
        dma((4, 4)),
        dma((4, 4)),
        dma((8,)),
        dma((8,)),
        dma((job_count,)),
        dma((job_count,)),
        pltpu.SemaphoreType.REGULAR((2, 4)),
        dma((16,)),
        dma((4,)),
        dma((2,)),
        dma((8,)),
        dma((8,)),
        dma((2,)),
        dma((2,)),
    ]
    return pl.pallas_call(
        backward_kernel,
        name="backward",
        out_shape=[one for one, _ in outs],
        in_specs=[anywhere] * 13 + [near] * 7,
        out_specs=[spec for _, spec in outs],
        scratch_shapes=scratch,
        compiler_params=pltpu.CompilerParams(
            collective_id=1, has_side_effects=True, vmem_limit_bytes=67_043_328
        ),
    )(
        held,
        probs,
        h_one,
        qkv,
        attended,
        proj,
        middle,
        h_two,
        gate,
        up,
        act,
        tokens,
        cotangent,
        adaptive,
        d_gate_two,
        pre,
        notes,
        pair_all,
        ada_shard,
        rows,
    )


def pack_kernel(
    time_embed,
    cath_class,
    cath_arch,
    cath_topo,
    res_counts,
    chain_ids,
    break_mask,
    w_qkv,
    w_out,
    w_gate,
    w_up,
    w_down,
    table_class,
    table_arch,
    table_topo,
    break_vec,
    pair_table,
    pair_proj,
    packed,
    first_note,
    pair_note,
    tables,
    rows,
):
    packed[:, 0:2304] = w_qkv[...]
    packed[:, 2304:3072] = w_out[...]
    packed[:, 3072:6144] = w_gate[...]
    packed[:, 6144:9216] = w_up[...]
    packed[:, 9216:12288] = w_down[...]
    lane = lax.broadcasted_iota(jnp.int32, (1, 128), 1)
    marks = jnp.zeros((1, 128), f32)
    for index, labels in enumerate((cath_class, cath_arch, cath_topo)):
        label = (labels[0] + 128 * index).astype(f32)
        marks = jnp.where(lane == 48 + index, label, marks)
    embed = time_embed[...].astype(f32)
    for owner in range(16):
        first_note[owner] = marks
        first_note[owner, :, 0:48] = embed[:, owner * 48 : owner * 48 + 48]
    shard = lax.axis_index("fsdp") * 48
    unit = lax.broadcasted_iota(jnp.int32, (128, 128), 0)
    unit = (unit == lax.broadcasted_iota(jnp.int32, (128, 128), 1)).astype(f32).astype(b16)
    pair_note[:, 0:128] = pair_table[...]
    pair_note[:, 128:256] = jnp.zeros((16, 128), b16)
    pair_note[:, 128:140] = pair_proj[...]
    spot = lax.broadcasted_iota(jnp.int32, (48, 2048), 1) - shard
    spot = (spot == lax.broadcasted_iota(jnp.int32, (48, 2048), 0)).astype(f32).astype(b16)
    placed = dot_nn(jnp.broadcast_to(break_vec[...].astype(f32), (16, 48)).astype(b16), spot)
    line = lax.broadcasted_iota(jnp.int32, (16, 128), 0)
    breaks = jnp.zeros((16, 128), f32)
    for row in range(16):
        breaks = jnp.where(line == row, placed[:, row * 128 : row * 128 + 128], breaks)
    pair_note[:, 256:384] = breaks.astype(b16)
    for index, lookup in enumerate((table_class, table_arch)):
        block = dot_tn(lookup[...], unit[0 : lookup.shape[0], :])
        tables[:, index * 128 : index * 128 + 128] = block.astype(b16)
    tables[:, 256:] = table_topo[...]
    rows[0:1, :] = chain_ids[...].astype(f32)
    rows[1:2, :] = break_mask[...].astype(f32)
    position = lax.broadcasted_iota(jnp.int32, (1, 512), 1)
    rows[2:3, :] = jnp.where(position < res_counts[0], 0.0, -1e30)
    rows[3:8, :] = jnp.zeros((5, 512), f32)


def forward_inputs(
    time_embed,
    cath_class,
    cath_arch,
    cath_topo,
    res_counts,
    chain_ids,
    break_mask,
    w_qkv,
    w_out,
    w_gate,
    w_up,
    w_down,
    table_class,
    table_arch,
    table_topo,
    break_vec,
    pair_table,
    pair_proj,
):
    near = pl.BlockSpec(memory_space=pltpu.VMEM)
    flat = pl.BlockSpec(memory_space=pltpu.SMEM)
    count = 256 + table_topo.shape[0]
    shape = jax.ShapeDtypeStruct
    return pl.pallas_call(
        pack_kernel,
        name="pack",
        out_shape=[
            shape((48, 12288), b16),
            shape((16, 1, 128), f32),
            shape((16, 384), b16),
            shape((48, count), b16),
            shape((8, 512), f32),
        ],
        in_specs=[near] + [flat] * 4 + [near] * 13,
        out_specs=[near] * 5,
    )(
        time_embed,
        cath_class,
        cath_arch,
        cath_topo,
        res_counts,
        chain_ids,
        break_mask,
        w_qkv,
        w_out,
        w_gate,
        w_up,
        w_down.T,
        table_class,
        table_arch,
        table_topo.T,
        break_vec[None, :],
        pair_table.T,
        pair_proj,
    )


def unpack_kernel(
    summed,
    ada_in,
    tables,
    pair_in,
    proj_in,
    break_in,
    grad_ada,
    grad_qkv,
    grad_out,
    grad_gate,
    grad_up,
    grad_down,
    grad_class,
    grad_arch,
    grad_topo,
    grad_break,
    grad_pair,
    grad_proj,
):
    grad_ada[...] = ada_in[...]
    grad_qkv[...] = summed[:, 0:2304]
    grad_out[...] = summed[:, 2304:3072]
    grad_gate[...] = summed[:, 3072:6144]
    grad_up[...] = summed[:, 6144:9216]
    grad_down[...] = summed[:, 9216:12288]
    grad_class[...] = tables[:, 0:128].T[0 : grad_class.shape[0], :]
    grad_arch[...] = tables[:, 128:256].T[0 : grad_arch.shape[0], :]
    grad_topo[...] = tables[:, 256:]
    shard = lax.axis_index("fsdp") * 48
    total = jnp.zeros((1, 48), f32)
    for owner in range(16):
        row, column = divmod(owner * 48, 128)
        width = min(48, 128 - column)
        piece = break_in[row : row + 1, column : column + width]
        if width < 48:
            piece = jnp.concatenate([piece, break_in[row + 1 : row + 2, 0 : 48 - width]], axis=1)
        total = jnp.where(shard == owner * 48, piece, total)
    grad_break[...] = total
    grad_pair[...] = pair_in[...]
    grad_proj[...] = proj_in[:, 0:12]


def run_unpack(summed, ada, tables, pair, proj, breaks, sizes):
    near = pl.BlockSpec(memory_space=pltpu.VMEM)
    shape = jax.ShapeDtypeStruct
    outs = [
        (48, 4608),
        (48, 2304),
        (48, 768),
        (48, 3072),
        (48, 3072),
        (48, 3072),
        (sizes[0], 48),
        (sizes[1], 48),
        (48, sizes[2]),
        (1, 48),
        (16, 128),
        (16, 12),
    ]
    return pl.pallas_call(
        unpack_kernel,
        name="unpack",
        out_shape=[shape(one, f32) for one in outs],
        in_specs=[near] * 6,
        out_specs=[near] * 12,
    )(summed, ada, tables, pair, proj, breaks)


def fast_shards(
    tokens,
    cotangent,
    time_embed,
    cath_class,
    cath_arch,
    cath_topo,
    res_counts,
    chain_ids,
    break_mask,
    w_ada,
    w_qkv,
    w_out,
    w_gate,
    w_up,
    w_down,
    table_class,
    table_arch,
    table_topo,
    break_vec,
    pair_table,
    pair_proj,
):
    packed, first_note, pair_note, tables, rows = forward_inputs(
        time_embed,
        cath_class,
        cath_arch,
        cath_topo,
        res_counts,
        chain_ids,
        break_mask,
        w_qkv,
        w_out,
        w_gate,
        w_up,
        w_down,
        table_class,
        table_arch,
        table_topo,
        break_vec,
        pair_table,
        pair_proj,
    )
    output, *saved = run_forward(
        packed, tokens[0], cotangent[0], first_note, pair_note, w_ada, tables, rows
    )
    d_tokens, summed, grad_ada, grad_tables, grad_pair, grad_proj, grad_break = run_backward(
        saved, tokens[0], cotangent[0], w_ada, rows, tables.shape[1]
    )
    sizes = (table_class.shape[0], table_arch.shape[0], table_topo.shape[0])
    grads = run_unpack(summed, grad_ada, grad_tables, grad_pair, grad_proj, grad_break, sizes)
    return (
        output[None],
        d_tokens[None],
        *grads[:5],
        grads[5].T,
        grads[6],
        grads[7],
        grads[8].T,
        grads[9][0],
        grads[10].T,
        grads[11],
    )


def solution(mesh):
    in_specs = (
        P(("dp", "fsdp"), None, None),
        P(("dp", "fsdp"), None, None),
        P(("dp", "fsdp"), None),
        P(("dp", "fsdp")),
        P(("dp", "fsdp")),
        P(("dp", "fsdp")),
        P(("dp", "fsdp")),
        P(("dp", "fsdp"), None),
        P(("dp", "fsdp"), None),
        P("fsdp", None),
        P("fsdp", None),
        P("fsdp", None),
        P("fsdp", None),
        P("fsdp", None),
        P(None, "fsdp"),
        P(None, "fsdp"),
        P(None, "fsdp"),
        P(None, "fsdp"),
        P("fsdp"),
        P(None, "fsdp"),
        P("fsdp", None),
    )
    out_specs = (
        P(("dp", "fsdp"), None, None),
        P(("dp", "fsdp"), None, None),
        P("fsdp", None),
        P("fsdp", None),
        P("fsdp", None),
        P("fsdp", None),
        P("fsdp", None),
        P(None, "fsdp"),
        P(None, "fsdp"),
        P(None, "fsdp"),
        P(None, "fsdp"),
        P("fsdp"),
        P(None, "fsdp"),
        P("fsdp", None),
    )
    sizes = dict(mesh.shape)
    body = fast_shards if (sizes["dp"], sizes["fsdp"]) == (2, 16) else shards
    return jax.shard_map(body, mesh=mesh, in_specs=in_specs, out_specs=out_specs, check_vma=False)
```

```python
from functools import partial

import jax
import jax.numpy as jnp
from jax import lax
from jax.experimental import pallas as pl
from jax.experimental.pallas import tpu as pltpu
from jax.sharding import PartitionSpec as P

epsilon = 1e-05
highest = lax.Precision.HIGHEST


def matmul(left, right):
    return jnp.dot(left, right, preferred_element_type=jnp.float32)


def matmul_t(left, right):
    return lax.dot_general(
        left, right, (((1,), (1,)), ((), ())), preferred_element_type=jnp.float32
    )


def matmul_tn(left, right):
    return lax.dot_general(
        left, right, (((0,), (0,)), ((), ())), preferred_element_type=jnp.float32
    )


def exact_tn(left, right):
    return lax.dot_general(
        left, right, (((0,), (0,)), ((), ())), precision=highest, preferred_element_type=jnp.float32
    )


def exact_nt(left, right):
    return lax.dot_general(
        left, right, (((1,), (1,)), ((), ())), precision=highest, preferred_element_type=jnp.float32
    )


def normalize(values):
    centred = values - jnp.mean(values, axis=-1, keepdims=True)
    inv_std = lax.rsqrt(jnp.mean(centred * centred, axis=-1, keepdims=True) + epsilon)
    return (centred * inv_std, inv_std)


def normalize_back(normed, inv_std, grad):
    return inv_std * (
        grad
        - jnp.mean(grad, axis=-1, keepdims=True)
        - normed * jnp.mean(grad * normed, axis=-1, keepdims=True)
    )


def pair_classes(chain_row, class_count):
    length = chain_row.shape[0]
    position = jnp.arange(length, dtype=jnp.int32)
    reach = class_count // 2 - 1
    offset = jnp.clip(position[:, None] - position[None, :], -reach, reach) + reach
    return jnp.where(chain_row[:, None] == chain_row[None, :], offset, class_count - 1)


def pair_bias(classes, bias_table):
    length = classes.shape[0]
    step_rows = min(length, 128)
    class_ids = jnp.arange(bias_table.shape[0], dtype=jnp.int32)

    def one_block(row_block):
        onehot = (row_block[:, :, None] == class_ids).astype(jnp.bfloat16)
        return jnp.einsum("ijc,ch->hij", onehot, bias_table, preferred_element_type=jnp.float32)

    pieces = lax.map(one_block, classes.reshape(length // step_rows, step_rows, length))
    return jnp.transpose(pieces, (1, 0, 2, 3)).reshape(bias_table.shape[1], length, length)


def pair_bias_back(classes, d_scores, class_count):
    head_count, length = (d_scores.shape[0], d_scores.shape[1])
    step_rows = min(length, 128)
    block_count = length // step_rows
    class_ids = jnp.arange(class_count, dtype=jnp.int32)
    grad_blocks = jnp.transpose(
        d_scores.reshape(head_count, block_count, step_rows, length), (1, 0, 2, 3)
    )

    def add_block(running, inputs):
        row_block, grad_block = inputs
        onehot = (row_block[:, :, None] == class_ids).astype(jnp.bfloat16)
        return (
            running
            + jnp.einsum("hij,ijc->ch", grad_block, onehot, preferred_element_type=jnp.float32),
            None,
        )

    start = jnp.zeros((class_count, head_count), jnp.float32)
    summed, unused = lax.scan(
        add_block, start, (classes.reshape(block_count, step_rows, length), grad_blocks)
    )
    return summed


def split_heads(qkv_win, head_count):
    length, triple = qkv_win.shape
    shaped = qkv_win.reshape(length, 3, head_count, triple // (3 * head_count))
    return (shaped[:, 0], shaped[:, 1], shaped[:, 2])


def window_scores(qkv_win, chain_row, count_win, bias_table):
    length = qkv_win.shape[0]
    queries, key_rows, value_rows = split_heads(qkv_win, bias_table.shape[1])
    classes = pair_classes(chain_row, bias_table.shape[0])
    score_scale = queries.shape[-1] ** (-0.5)
    scores = (
        jnp.einsum("qhd,khd->hqk", queries, key_rows, preferred_element_type=jnp.float32)
        * score_scale
    )
    scores = scores + pair_bias(classes, bias_table)
    live_keys = jnp.arange(length, dtype=jnp.int32) < count_win
    scores = jnp.where(live_keys[None, None, :], scores, -1e30)
    return (scores, queries, key_rows, value_rows, classes, score_scale)


def attend(inputs, bias_table):
    qkv_win, chain_row, count_win = inputs
    scores, queries, key_rows, value_rows, classes, score_scale = window_scores(
        qkv_win, chain_row, count_win, bias_table
    )
    highest_score = jnp.max(scores, axis=-1, keepdims=True)
    exponent = jnp.exp(scores - highest_score)
    row_total = jnp.sum(exponent, axis=-1, keepdims=True)
    attn_probs = (exponent / row_total).astype(jnp.bfloat16)
    attended = jnp.einsum(
        "hqk,khd->qhd", attn_probs, value_rows, preferred_element_type=jnp.float32
    )
    attended = attended.reshape(qkv_win.shape[0], -1).astype(jnp.bfloat16)
    return (attended, (highest_score + jnp.log(row_total))[:, :, 0])


def attend_back(inputs, bias_table):
    qkv_win, chain_row, count_win, log_total, d_attended = inputs
    scores, queries, key_rows, value_rows, classes, score_scale = window_scores(
        qkv_win, chain_row, count_win, bias_table
    )
    attn_probs = jnp.exp(scores - log_total[:, :, None])
    d_heads = d_attended.reshape(queries.shape)
    d_probs = jnp.einsum("qhd,khd->hqk", d_heads, value_rows, preferred_element_type=jnp.float32)
    d_scores = attn_probs * (d_probs - jnp.sum(attn_probs * d_probs, axis=-1, keepdims=True))
    d_scores = d_scores.astype(jnp.bfloat16)
    d_values = jnp.einsum(
        "hqk,qhd->khd", attn_probs.astype(jnp.bfloat16), d_heads, preferred_element_type=jnp.float32
    )
    d_queries = (
        jnp.einsum("hqk,khd->qhd", d_scores, key_rows, preferred_element_type=jnp.float32)
        * score_scale
    )
    d_keys = (
        jnp.einsum("hqk,qhd->khd", d_scores, queries, preferred_element_type=jnp.float32)
        * score_scale
    )
    d_qkv = (
        jnp.stack([d_queries, d_keys, d_values], axis=1)
        .reshape(qkv_win.shape[0], -1)
        .astype(jnp.bfloat16)
    )
    return (d_qkv, pair_bias_back(classes, d_scores, bias_table.shape[0]))


def forward(
    tokens,
    time_embed,
    cath_class,
    cath_arch,
    cath_topo,
    res_counts,
    chain_ids,
    break_mask,
    attn_set,
    mlp_set,
):
    ada_all, qkv_all, out_all, class_all, arch_all, topo_all, break_all, pair_all, proj_all = (
        attn_set
    )
    gate_all, up_all, down_all = mlp_set
    windows, length, model_width = tokens.shape
    row_count = windows * length
    pre_act = time_embed.astype(jnp.float32)
    onehots = []
    for labels, lookup in ((cath_class, class_all), (cath_arch, arch_all), (cath_topo, topo_all)):
        onehot = (labels[:, None] == jnp.arange(lookup.shape[0], dtype=jnp.int32)[None, :]).astype(
            jnp.bfloat16
        )
        pre_act = pre_act + matmul(onehot, lookup)
        onehots.append(onehot)
    cond_low = jax.nn.silu(pre_act).astype(jnp.bfloat16)
    ada_rows = matmul(cond_low, ada_all)
    shift_one, scale_one, gate_one, shift_two, scale_two, gate_two = [
        portion[:, None, :] for portion in jnp.split(ada_rows, 6, axis=1)
    ]
    resid_in = tokens.astype(jnp.float32)
    normed_one, inv_one = normalize(resid_in)
    break_rows = break_mask.astype(jnp.float32)[:, :, None]
    h_one_low = (
        normed_one * (1.0 + scale_one) + shift_one + break_rows * break_all.astype(jnp.float32)
    )
    h_one_low = h_one_low.astype(jnp.bfloat16).reshape(row_count, model_width)
    proj_qkv = (
        matmul(h_one_low, qkv_all).astype(jnp.bfloat16).reshape(windows, length, 3 * model_width)
    )
    pair_normed, pair_inv = normalize(pair_all.astype(jnp.float32))
    pair_low = pair_normed.astype(jnp.bfloat16)
    bias_table = matmul(pair_low, proj_all).astype(jnp.bfloat16)
    attended, log_total = lax.map(
        partial(attend, bias_table=bias_table), (proj_qkv, chain_ids, res_counts)
    )
    attended_rows = attended.reshape(row_count, model_width)
    attn_proj = matmul(attended_rows, out_all).reshape(windows, length, model_width)
    middle = resid_in + gate_one * attn_proj
    normed_two, inv_two = normalize(middle)
    h_two_low = (
        (normed_two * (1.0 + scale_two) + shift_two)
        .astype(jnp.bfloat16)
        .reshape(row_count, model_width)
    )
    gate_pre = matmul(h_two_low, gate_all)
    up_pre = matmul(h_two_low, up_all)
    activated = (jax.nn.silu(gate_pre) * up_pre).astype(jnp.bfloat16)
    ffn_out = matmul(activated, down_all).reshape(windows, length, model_width)
    output = middle + gate_two * ffn_out
    return {
        "output": output,
        "pre_act": pre_act,
        "onehots": onehots,
        "cond_low": cond_low,
        "scales": (scale_one, gate_one, scale_two, gate_two),
        "normed_one": normed_one,
        "inv_one": inv_one,
        "break_rows": break_rows,
        "h_one_low": h_one_low,
        "proj_qkv": proj_qkv,
        "pair_normed": pair_normed,
        "pair_inv": pair_inv,
        "pair_low": pair_low,
        "bias_table": bias_table,
        "log_total": log_total,
        "attended_rows": attended_rows,
        "attn_proj": attn_proj,
        "normed_two": normed_two,
        "inv_two": inv_two,
        "h_two_low": h_two_low,
        "gate_pre": gate_pre,
        "up_pre": up_pre,
        "activated": activated,
        "ffn_out": ffn_out,
    }


def shards(
    tokens,
    cotangent,
    time_embed,
    cath_class,
    cath_arch,
    cath_topo,
    res_counts,
    chain_ids,
    break_mask,
    w_ada,
    w_qkv,
    w_out,
    w_gate,
    w_up,
    w_down,
    table_class,
    table_arch,
    table_topo,
    break_vec,
    pair_table,
    pair_proj,
):
    attn_set = (
        lax.all_gather(w_ada, "fsdp", axis=0, tiled=True),
        lax.all_gather(w_qkv, "fsdp", axis=0, tiled=True),
        lax.all_gather(w_out, "fsdp", axis=0, tiled=True),
        lax.all_gather(table_class, "fsdp", axis=1, tiled=True),
        lax.all_gather(table_arch, "fsdp", axis=1, tiled=True),
        lax.all_gather(table_topo, "fsdp", axis=1, tiled=True),
        lax.all_gather(break_vec, "fsdp", axis=0, tiled=True),
        lax.all_gather(pair_table, "fsdp", axis=1, tiled=True),
        lax.all_gather(pair_proj, "fsdp", axis=0, tiled=True),
    )
    mlp_set = (
        lax.all_gather(w_gate, "fsdp", axis=0, tiled=True),
        lax.all_gather(w_up, "fsdp", axis=0, tiled=True),
        lax.all_gather(w_down, "fsdp", axis=1, tiled=True),
    )
    saved = forward(
        tokens,
        time_embed,
        cath_class,
        cath_arch,
        cath_topo,
        res_counts,
        chain_ids,
        break_mask,
        attn_set,
        mlp_set,
    )
    output = saved["output"].astype(jnp.bfloat16)
    attn_set = (
        lax.all_gather(w_ada, "fsdp", axis=0, tiled=True),
        lax.all_gather(w_qkv, "fsdp", axis=0, tiled=True),
        lax.all_gather(w_out, "fsdp", axis=0, tiled=True),
        lax.all_gather(table_class, "fsdp", axis=1, tiled=True),
        lax.all_gather(table_arch, "fsdp", axis=1, tiled=True),
        lax.all_gather(table_topo, "fsdp", axis=1, tiled=True),
        lax.all_gather(break_vec, "fsdp", axis=0, tiled=True),
        lax.all_gather(pair_table, "fsdp", axis=1, tiled=True),
        lax.all_gather(pair_proj, "fsdp", axis=0, tiled=True),
    )
    mlp_set = (
        lax.all_gather(w_gate, "fsdp", axis=0, tiled=True),
        lax.all_gather(w_up, "fsdp", axis=0, tiled=True),
        lax.all_gather(w_down, "fsdp", axis=1, tiled=True),
    )
    saved = forward(
        tokens,
        time_embed,
        cath_class,
        cath_arch,
        cath_topo,
        res_counts,
        chain_ids,
        break_mask,
        attn_set,
        mlp_set,
    )
    ada_all, qkv_all, out_all, class_all, arch_all, topo_all, break_all, pair_all, proj_all = (
        attn_set
    )
    gate_all, up_all, down_all = mlp_set
    windows, length, model_width = tokens.shape
    row_count = windows * length
    scale_one, gate_one, scale_two, gate_two = saved["scales"]
    grad_rows = cotangent.astype(jnp.float32)
    ffn_out = saved["ffn_out"]
    d_ffn = (gate_two * grad_rows).astype(jnp.bfloat16).reshape(row_count, model_width)
    d_gate_two = jnp.sum(grad_rows * ffn_out, axis=1)
    grad_down = matmul_tn(saved["activated"], d_ffn)
    d_act = matmul_t(d_ffn, down_all)
    gate_pre, up_pre = (saved["gate_pre"], saved["up_pre"])
    sigma = jax.nn.sigmoid(gate_pre)
    d_gate_pre = (d_act * up_pre * sigma * (1.0 + gate_pre * (1.0 - sigma))).astype(jnp.bfloat16)
    d_up_pre = (d_act * gate_pre * sigma).astype(jnp.bfloat16)
    h_two_low = saved["h_two_low"]
    grad_gate = matmul_tn(h_two_low, d_gate_pre)
    grad_up = matmul_tn(h_two_low, d_up_pre)
    d_h_two = (matmul_t(d_gate_pre, gate_all) + matmul_t(d_up_pre, up_all)).reshape(
        windows, length, model_width
    )
    normed_two = saved["normed_two"]
    d_scale_two = jnp.sum(d_h_two * normed_two, axis=1)
    d_shift_two = jnp.sum(d_h_two, axis=1)
    d_middle = grad_rows + normalize_back(normed_two, saved["inv_two"], d_h_two * (1.0 + scale_two))
    d_gate_one = jnp.sum(d_middle * saved["attn_proj"], axis=1)
    d_attn = (gate_one * d_middle).astype(jnp.bfloat16).reshape(row_count, model_width)
    grad_out = matmul_tn(saved["attended_rows"], d_attn)
    d_attended = (
        matmul_t(d_attn, out_all).astype(jnp.bfloat16).reshape(windows, length, model_width)
    )
    bias_table = saved["bias_table"]
    d_qkv, bias_grads = lax.map(
        partial(attend_back, bias_table=bias_table),
        (saved["proj_qkv"], chain_ids, res_counts, saved["log_total"], d_attended),
    )
    d_bias_table = jnp.sum(bias_grads, axis=0)
    d_qkv = d_qkv.reshape(row_count, 3 * model_width)
    h_one_low = saved["h_one_low"]
    grad_qkv = matmul_tn(h_one_low, d_qkv)
    d_h_one = matmul_t(d_qkv, qkv_all).reshape(windows, length, model_width)
    normed_one = saved["normed_one"]
    d_scale_one = jnp.sum(d_h_one * normed_one, axis=1)
    d_shift_one = jnp.sum(d_h_one, axis=1)
    grad_break = jnp.sum(d_h_one * saved["break_rows"], axis=(0, 1))
    d_tokens = d_middle + normalize_back(normed_one, saved["inv_one"], d_h_one * (1.0 + scale_one))
    d_ada = jnp.concatenate(
        [d_shift_one, d_scale_one, d_gate_one, d_shift_two, d_scale_two, d_gate_two], axis=1
    ).astype(jnp.bfloat16)
    grad_ada = matmul_tn(saved["cond_low"], d_ada)
    pre_act = saved["pre_act"]
    sigma_pre = jax.nn.sigmoid(pre_act)
    d_pre = matmul_t(d_ada, ada_all) * sigma_pre * (1.0 + pre_act * (1.0 - sigma_pre))
    onehots = saved["onehots"]
    grad_class = exact_tn(onehots[0].astype(jnp.float32), d_pre)
    grad_arch = exact_tn(onehots[1].astype(jnp.float32), d_pre)
    grad_topo = exact_tn(onehots[2].astype(jnp.float32), d_pre)
    grad_proj = exact_tn(saved["pair_low"].astype(jnp.float32), d_bias_table)
    d_pair_normed = exact_nt(d_bias_table, proj_all.astype(jnp.float32))
    grad_pair = normalize_back(saved["pair_normed"], saved["pair_inv"], d_pair_normed)
    attn_parts = (
        lax.psum_scatter(grad_ada, "fsdp", scatter_dimension=0, tiled=True),
        lax.psum_scatter(grad_qkv, "fsdp", scatter_dimension=0, tiled=True),
        lax.psum_scatter(grad_out, "fsdp", scatter_dimension=0, tiled=True),
        lax.psum_scatter(grad_class, "fsdp", scatter_dimension=1, tiled=True),
        lax.psum_scatter(grad_arch, "fsdp", scatter_dimension=1, tiled=True),
        lax.psum_scatter(grad_topo, "fsdp", scatter_dimension=1, tiled=True),
        lax.psum_scatter(grad_break, "fsdp", scatter_dimension=0, tiled=True),
        lax.psum_scatter(grad_pair, "fsdp", scatter_dimension=1, tiled=True),
        lax.psum_scatter(grad_proj, "fsdp", scatter_dimension=0, tiled=True),
    )
    mlp_parts = (
        lax.psum_scatter(grad_gate, "fsdp", scatter_dimension=0, tiled=True),
        lax.psum_scatter(grad_up, "fsdp", scatter_dimension=0, tiled=True),
        lax.psum_scatter(grad_down, "fsdp", scatter_dimension=1, tiled=True),
    )
    owned = (
        lax.psum(attn_parts[0].astype(jnp.bfloat16), "dp").astype(jnp.float32),
        lax.psum(attn_parts[1].astype(jnp.bfloat16), "dp").astype(jnp.float32),
        lax.psum(attn_parts[2].astype(jnp.bfloat16), "dp").astype(jnp.float32),
        lax.psum(mlp_parts[0].astype(jnp.bfloat16), "dp").astype(jnp.float32),
        lax.psum(mlp_parts[1].astype(jnp.bfloat16), "dp").astype(jnp.float32),
        lax.psum(mlp_parts[2].astype(jnp.bfloat16), "dp").astype(jnp.float32),
        lax.psum(attn_parts[3].astype(jnp.bfloat16), "dp").astype(jnp.float32),
        lax.psum(attn_parts[4].astype(jnp.bfloat16), "dp").astype(jnp.float32),
        lax.psum(attn_parts[5].astype(jnp.bfloat16), "dp").astype(jnp.float32),
        lax.psum(attn_parts[6].astype(jnp.bfloat16), "dp").astype(jnp.float32),
        lax.psum(attn_parts[7].astype(jnp.bfloat16), "dp").astype(jnp.float32),
        lax.psum(attn_parts[8].astype(jnp.bfloat16), "dp").astype(jnp.float32),
    )
    return (
        output,
        d_tokens.astype(jnp.bfloat16),
        owned[0],
        owned[1],
        owned[2],
        owned[3],
        owned[4],
        owned[5],
        owned[6],
        owned[7],
        owned[8],
        owned[9],
        owned[10],
        owned[11],
    )


mesh_ids = pl.DeviceIdType.MESH
f32 = jnp.float32
b16 = jnp.bfloat16
core_count = 2
chip_count = 8
shard_rows = 48
chunk_cols = 3072
chunk_count = 4
side_cols = 768
ring_cols = 2304
job_cols = 384
jobs_in_chunk = 6
job_count = 24
ahead = 3
gather_stride = 2
scatter_stride = 2
grad_buffers = 3
plan = (1, 1, 1, 1, 1, 1, 1, 1, 1, 1, 4)
ahead_plan = (2, 2, 2, 2, 2)


def dot_nn(left, right):
    return jnp.dot(left, right, preferred_element_type=f32)


def dot_nt(left, right):
    return lax.dot_general(left, right, (((1,), (1,)), ((), ())), preferred_element_type=f32)


def dot_tn(left, right):
    return lax.dot_general(left, right, (((0,), (0,)), ((), ())), preferred_element_type=f32)


def on(condition, body):
    if isinstance(condition, bool):
        if condition:
            body()
    else:
        pl.when(condition)(body)


def both(first, second):
    if isinstance(first, bool) and isinstance(second, bool):
        return first and second
    return jnp.logical_and(first, second)


def quot(value, by):
    return value // by if isinstance(value, int) else lax.div(value, by)


def modulo(value, by):
    return value % by if isinstance(value, int) else lax.rem(value, by)


def aligned(value, by=128):
    return value if isinstance(value, int) else pl.multiple_of(value, by)


class Place:
    def __init__(self):
        self.x = lax.axis_index("dp")
        self.f = lax.axis_index("fsdp")
        self.me = self.x * 16 + self.f
        self.c = lax.rem(self.f, 2)
        self.cy = lax.div(self.f, 2)
        y = lax.rem(self.cy, 2)
        z = lax.div(self.cy, 2)
        self.p = z * (1 - y) + (7 - z) * y

    def chip(self, position):
        position = lax.rem(position + 16, 8)
        half = lax.div(position, 4)
        return 2 * position * (1 - half) + (15 - 2 * position) * half

    def ring_id(self, position):
        return (self.x, self.chip(position) * 2 + self.c)

    def plane_id(self):
        return (1 - self.x, self.f)

    def core_id(self):
        return (self.x, self.cy * 2 + 1 - self.c)


def greet_all(at):
    barrier = pltpu.get_barrier_semaphore()

    @pl.loop(1, 32)
    def _(step):
        other = lax.rem(at.me + step, 32)
        pl.semaphore_signal(
            barrier,
            inc=1,
            device_id=(lax.div(other, 16), lax.rem(other, 16)),
            device_id_type=mesh_ids,
        )

    pl.semaphore_wait(barrier, 31)


def remote(src, dst, send_sem, recv_sem, device_id):
    return pltpu.make_async_remote_copy(
        src_ref=src,
        dst_ref=dst,
        send_sem=send_sem,
        recv_sem=recv_sem,
        device_id=device_id,
        device_id_type=mesh_ids,
    )


def job_column(at, job):
    chunk = quot(job, jobs_in_chunk)
    inner = modulo(job, jobs_in_chunk)
    base = chunk * chunk_cols + inner * job_cols
    if isinstance(job, int):
        return aligned(base + (at.x * ring_cols if inner < 2 else 0))
    side = 1 - jnp.minimum(lax.div(inner, 2), 1)
    return aligned(base + side * at.x * ring_cols)


class Gather:
    def __init__(self, at, packed, held, sems):
        self.at = at
        self.packed = packed
        self.held = held
        (
            self.ring_send,
            self.ring_recv,
            self.side_send,
            self.side_recv,
            self.core_send,
            self.core_recv,
        ) = sems

    def ring(self, job, step, way, hop):
        at = self.at
        sign = 1 - 2 * way
        column = pl.ds(job_column(at, job), job_cols)
        block = self.held.at[at.chip(at.p - (step + hop) * sign), at.c, :, column]
        src = self.packed.at[:, column] if step == 0 and hop == 0 else block
        return remote(
            src,
            block,
            self.ring_send.at[job, step, way],
            self.ring_recv.at[job, step, way],
            at.ring_id(at.p + sign),
        )

    def relay(self, job, step, way):
        at = self.at
        sign = 1 - 2 * way
        column = pl.ds(job_column(at, job), job_cols)
        block = self.held.at[at.chip(at.p - (step + 1) * sign), at.c, :, column]
        self.pass_on(block, block, job)

    def pass_on(self, src, dst, job):
        at = self.at
        chunk = quot(job, jobs_in_chunk)
        inner = modulo(job, jobs_in_chunk)
        slot = chunk * 2
        remote(
            src, dst, self.core_send.at[slot], self.core_recv.at[slot], at.core_id()
        ).start()

        def across():
            spot = chunk * 2 + inner
            remote(
                src, dst, self.side_send.at[spot], self.side_recv.at[spot], at.plane_id()
            ).start()

        on(inner < 2, across)

    def side(self, job, mine):
        at = self.at
        chunk = quot(job, jobs_in_chunk)
        inner = modulo(job, jobs_in_chunk)
        owner = at.x if mine else 1 - at.x
        column = aligned(chunk * chunk_cols + inner * job_cols + owner * ring_cols)
        block = self.held.at[:, at.c, :, pl.ds(column, job_cols)]
        slot = chunk * 2 + inner
        return remote(
            block, block, self.side_send.at[slot], self.side_recv.at[slot], at.plane_id()
        )

    def core(self, chunk, part, mine):
        at = self.at
        if part == 0:
            column, width = chunk * chunk_cols + at.x * side_cols, ring_cols
        else:
            column, width = chunk * chunk_cols + (1 - at.x) * ring_cols, side_cols
        row = at.c if mine else 1 - at.c
        block = self.held.at[:, row, :, pl.ds(aligned(column), width)]
        slot = chunk * 2 + part
        return remote(block, block, self.core_send.at[slot], self.core_recv.at[slot], at.core_id())

    def start(self, job):
        self.ring(job, 0, 0, 0).start()
        self.ring(job, 0, 1, 0).start()
        at = self.at
        column = pl.ds(job_column(at, job), job_cols)
        self.pass_on(self.packed.at[:, column], self.held.at[at.cy, at.c, :, column], job)

    def tick(self, tau):
        def valid(job):
            return both(job >= 0, job < job_count)

        for step in (4, 3, 2, 1):
            job = tau - step * gather_stride

            def advance(job=job, step=step):
                if step < 4:
                    ways = (0, 1)
                else:
                    ways = (modulo(job, 2),)
                for way in ways:
                    self.ring(job, step - 1, way, 1).wait_recv()
                if step < 3:
                    self.ring(job, step, 0, 0).start()
                    self.ring(job, step, 1, 0).start()
                elif step == 3:
                    self.ring(job, 3, modulo(job, 2), 0).start()
                for way in ways:
                    self.relay(job, step - 1, way)

            on(valid(job), advance)
        on(valid(tau + ahead), lambda: self.start(tau + ahead))

        late = tau - 4 * gather_stride - jobs_in_chunk

        def side_done():
            chunk = quot(late, jobs_in_chunk)
            self.side(chunk * jobs_in_chunk, False).wait_recv()
            self.side(chunk * jobs_in_chunk + 1, False).wait_recv()
            self.core(chunk, 1, True).start()

        on(both(valid(late), modulo(late + 60, jobs_in_chunk) == 0), side_done)

    def arrive(self, chunk):
        self.core(chunk, 0, False).wait_recv()
        self.core(chunk, 1, False).wait_recv()

    def finish(self):
        @pl.loop(0, job_count)
        def _(job):
            for step in range(3):
                self.ring(job, step, 0, 0).wait_send()
                self.ring(job, step, 1, 0).wait_send()
            self.ring(job, 3, lax.rem(job, 2), 0).wait_send()

        for chunk in range(chunk_count):
            for inner in range(2):
                self.side(chunk * jobs_in_chunk + inner, True).wait_send()
                self.core(chunk, inner, True).wait_send()


def class_map(class_count):
    spot = lax.broadcasted_iota(jnp.int32, (512, class_count), 0)
    spot = jnp.where(spot < 384, spot, spot - 512)
    reach = class_count // 2 - 1
    label = jnp.clip(128 - spot, -reach, reach) + reach
    kind = lax.broadcasted_iota(jnp.int32, (512, class_count), 1)
    return (label == kind).astype(f32).astype(b16)


def forward_kernel(
    packed,
    tokens,
    cotangent,
    first_note,
    pair_note,
    ada_shard,
    tables,
    rows,
    output,
    held_out,
    h_one_out,
    qkv_out,
    probs_out,
    attended_out,
    proj_out,
    middle_out,
    h_two_out,
    gate_out,
    up_out,
    act_out,
    ada_out,
    d_gate_two_out,
    pre_out,
    note_out,
    pair_out,
    held,
    note_in,
    pair_in,
    part_rows,
    part_in,
    normed,
    h_one,
    qkv,
    bias,
    edges,
    probs,
    attended,
    proj,
    middle,
    h_two,
    gate,
    up,
    act,
    total,
    out_low,
    ring_send,
    ring_recv,
    side_send,
    side_recv,
    core_send,
    core_recv,
    note_send,
    note_recv,
    pair_send,
    pair_recv,
    part_send,
    part_recv,
    local_sem,
    probs_sem,
    out_sem,
):
    at = Place()
    gather = Gather(
        at, packed, held, (ring_send, ring_recv, side_send, side_recv, core_send, core_recv)
    )
    greet_all(at)

    def lead(index):
        for tau in range(sum(ahead_plan[:index]), sum(ahead_plan[: index + 1])):
            gather.tick(1 + tau)

    def note_copy(step, mine):
        other = lax.rem(at.me + step, 32)
        slot = at.me if mine else other
        return remote(
            first_note.at[lax.rem(other, 16)],
            note_in.at[slot],
            note_send.at[step],
            note_recv.at[slot],
            (lax.div(other, 16), lax.rem(other, 16)),
        )

    def pair_copy(step, mine):
        other = lax.rem(at.f + step, 16)
        slot = at.f if mine else other
        return remote(
            pair_note, pair_in.at[slot], pair_send.at[step], pair_recv.at[slot], (at.x, other)
        )

    def part_copy(step, mine):
        other = lax.rem(at.f + step, 16)
        slot = at.f if mine else other
        return remote(
            part_rows.at[other],
            part_in.at[slot],
            part_send.at[step],
            part_recv.at[slot],
            (at.x, other),
        )

    pl.loop(1, 32)(lambda step: note_copy(step, True).start())
    pl.loop(1, 16)(lambda step: pair_copy(step, True).start())
    for job in range(ahead + 1):
        gather.start(job)
    local = []
    for chunk in range(chunk_count):
        column = pl.ds(aligned(chunk * chunk_cols + at.x * side_cols), ring_cols)
        copy = pltpu.make_async_copy(
            packed.at[:, column], held.at[at.cy, at.c, :, column], local_sem.at[chunk]
        )
        copy.start()
        local.append(copy)
    note_in[at.me] = first_note[at.f]
    pair_in[at.f] = pair_note[...]
    values = tokens[...].astype(f32)
    centred = values - jnp.mean(values, axis=-1, keepdims=True)
    spread = jnp.mean(centred * centred, axis=-1, keepdims=True)
    normed[...] = centred * lax.rsqrt(spread + epsilon)
    for copy in local:
        copy.wait()
    lead(0)

    @pl.loop(1, 32)
    def _(step):
        note_copy(step, False).wait_recv()

    for window in range(32):
        note_out[window : window + 1, :] = note_in[window]
    notes = note_out[...]
    kind = lax.broadcasted_iota(jnp.int32, (32, tables.shape[1]), 1).astype(f32)
    hit = (kind == notes[:, 48:49]) | (kind == notes[:, 49:50]) | (kind == notes[:, 50:51])
    pre = notes[:, 0:48] + dot_nt(hit.astype(f32).astype(b16), tables[...])
    pre_out[...] = jnp.zeros_like(pre_out)
    pre_out[:, 0:48] = pre
    group = pre_out[pl.ds(pl.multiple_of(at.x * 16, 16), 16), :][:, 0:48]
    cond = (group * (1.0 / (1.0 + jnp.exp(-group)))).astype(b16)
    partial_rows = dot_nn(cond, ada_shard[...])
    for row in range(16):
        part_rows[row] = partial_rows[row : row + 1, :]
    lead(1)

    @pl.loop(1, 16)
    def _(step):
        pair_copy(step, False).wait_recv()

    gathered = pair_in[...].reshape(256, 384)
    features = gathered[:, 0:128].astype(f32)
    features = features - jnp.mean(features, axis=0, keepdims=True)
    features = features * lax.rsqrt(jnp.mean(features * features, axis=0, keepdims=True) + epsilon)
    table = dot_tn(gathered[:, 128:256], features.astype(b16))[0:16, :].astype(b16)
    table_wide = table.astype(f32)
    edges[0] = jnp.broadcast_to(table_wide[:, 126:127], (16, 128))
    edges[1] = jnp.broadcast_to(table_wide[:, 0:1], (16, 128))
    edges[2] = jnp.broadcast_to(table_wide[:, 127:128], (16, 128))
    spots = dot_nt(table, class_map(128))
    for head in range(12):
        line = jnp.broadcast_to(spots[head : head + 1, :], (128, 512))
        bias[head] = pltpu.roll(line, 0, 1, stride=1, stride_axis=0)[:, 0:384]
    pl.loop(1, 16)(lambda step: part_copy(step, True).start())
    lead(2)

    breaks = jnp.sum(pair_in[:, :, 256:384].astype(f32), axis=0)
    break_row = jnp.concatenate([breaks[row : row + 1, :] for row in range(6)], axis=1)
    mark_row = rows[1:2, :].astype(b16)
    lead(3)

    @pl.loop(1, 16)
    def _(step):
        part_copy(step, False).wait_recv()

    part_in[at.f] = part_rows[at.f]
    adaptive = part_in[0]
    for row in range(1, 16):
        adaptive = adaptive + part_in[row]
    ada_out[...] = adaptive
    shift_one = adaptive[:, 0:768]
    scale_one = adaptive[:, 768:1536]
    gate_one = adaptive[:, 1536:2304]
    shift_two = adaptive[:, 2304:3072]
    scale_two = adaptive[:, 3072:3840]
    gate_two = adaptive[:, 3840:4608]
    lead(4)
    first = normed[...] * (1.0 + scale_one) + shift_one
    h_one[...] = (first + dot_tn(mark_row, break_row.astype(b16))).astype(b16)
    outgoing = []

    def emit(src, dst):
        copy = pltpu.make_async_copy(src, dst, out_sem.at[len(outgoing)])
        copy.start()
        outgoing.append(copy)

    emit(h_one, h_one_out)
    emit(pair_in, pair_out)
    for tau in range(1 + sum(ahead_plan), 15):
        gather.tick(tau)

    def weights(column, width):
        return held[:, :, :, column : column + width].reshape(768, width)

    def settle(chunk):
        gather.arrive(chunk)
        column = pl.ds(chunk * chunk_cols, chunk_cols)
        emit(held.at[:, :, :, column], held_out.at[:, :, :, column])

    settle(0)
    for piece in range(3):
        span = slice(piece * 768, piece * 768 + 768)
        qkv[:, span] = dot_nn(h_one[...], weights(piece * 768, 768)).astype(b16)
        if piece < 2:
            gather.tick(15 + piece)
    emit(qkv, qkv_out)
    chain_row = rows[0:1, :]
    pad_row = rows[2:3, :]
    first_size = 512.0 - jnp.sum(chain_row, axis=1, keepdims=True)
    low_lane = lax.broadcasted_iota(jnp.int32, (1, 128), 1) < 64
    line_number = lax.broadcasted_iota(jnp.int32, (128, 128), 0).astype(f32)

    def probs_copy(pair):
        slot = modulo(pair, 2)
        return pltpu.make_async_copy(
            probs.at[slot], probs_out.at[pl.ds(pair * 2, 2)], probs_sem.at[slot]
        )

    @pl.loop(0, 6)
    def _(pair):
        lane = pl.multiple_of(pair * 128, 128)
        slot = lax.rem(pair, 2)
        on(pair >= 2, lambda: probs_copy(pair - 2).wait())
        queries = qkv[:, pl.ds(lane, 128)] * jnp.asarray(0.125, b16)
        keys = qkv[:, pl.ds(768 + lane, 128)]
        content = qkv[:, pl.ds(1536 + lane, 128)]
        mixed = []
        for half in range(2):
            head = pair * 2 + half
            own = low_lane if half == 0 else jnp.logical_not(low_lane)
            raw = dot_nt(jnp.where(own, queries, jnp.zeros_like(queries)), keys)
            far_low = edges[0, pl.ds(head, 1), :]
            far_high = edges[1, pl.ds(head, 1), :]
            apart = edges[2, pl.ds(head, 1), :]
            for block in range(4):
                chain_here = (line_number + 128.0 * block >= first_size).astype(f32)
                tiles = []
                for other in range(4):
                    offset = block - other
                    if offset > 1:
                        near = far_low
                    elif offset < -1:
                        near = far_high
                    else:
                        near = bias[head, :, (1 - offset) * 128 : (2 - offset) * 128]
                    there = chain_row[:, other * 128 : other * 128 + 128]
                    near = jnp.where(chain_here == there, near, apart)
                    tiles.append(
                        raw[block * 128 : block * 128 + 128, other * 128 : other * 128 + 128]
                        + near
                        + pad_row[:, other * 128 : other * 128 + 128]
                    )
                scores = jnp.concatenate(tiles, axis=1)
                scores = jnp.exp(scores - jnp.max(scores, axis=1, keepdims=True))
                scores = scores * (1.0 / jnp.sum(scores, axis=1, keepdims=True))
                probs[slot, half, block * 128 : block * 128 + 128, :] = scores.astype(b16)
            mixed.append(dot_nn(probs[slot, half], content))
        attended[:, pl.ds(lane, 128)] = jnp.where(low_lane, mixed[0], mixed[1]).astype(b16)
        probs_copy(pair).start()
        spot = 17 + pair + lax.div(pair, 2)
        gather.tick(spot)
        on(lax.rem(pair, 2) == 1, lambda: gather.tick(spot + 1))

    emit(attended, attended_out)
    projected = dot_nn(attended[...], weights(2304, 768))
    proj[...] = projected.astype(b16)
    middle[...] = tokens[...].astype(f32) + gate_one * projected
    emit(proj, proj_out)
    emit(middle, middle_out)
    gather.tick(26)
    values = middle[...]
    centred = values - jnp.mean(values, axis=-1, keepdims=True)
    spread = jnp.mean(centred * centred, axis=-1, keepdims=True)
    second = centred * lax.rsqrt(spread + epsilon) * (1.0 + scale_two) + shift_two
    h_two[...] = second.astype(b16)
    emit(h_two, h_two_out)
    gather.tick(27)

    settle(1)

    def moving(column):
        return held[:, :, :, pl.ds(pl.multiple_of(column, 128), 768)].reshape(768, 768)

    @pl.loop(0, 4)
    def _(piece):
        span = pl.ds(pl.multiple_of(piece * 768, 128), 768)
        gate[:, span] = dot_nn(h_two[...], moving(3072 + piece * 768)).astype(b16)
        on(lax.rem(piece, 2) == 1, lambda: gather.tick(28 + lax.div(piece, 2)))

    emit(gate, gate_out)
    settle(2)

    @pl.loop(0, 4)
    def _(piece):
        span = pl.ds(pl.multiple_of(piece * 768, 128), 768)
        raised = dot_nn(h_two[...], moving(6144 + piece * 768))
        gated = gate[:, span].astype(f32)
        up[:, span] = raised.astype(b16)
        act[:, span] = (gated * (1.0 / (1.0 + jnp.exp(-gated))) * raised).astype(b16)
        on(piece < 3, lambda: gather.tick(30 + piece))

    emit(up, up_out)
    emit(act, act_out)
    settle(3)
    total[...] = dot_nt(act[...], weights(9216, 3072))
    fed = total[...]
    d_gate_two_out[...] = jnp.sum(cotangent[...].astype(f32) * fed, axis=0, keepdims=True)
    out_low[...] = (middle[...] + gate_two * fed).astype(b16)
    emit(out_low, output)

    probs_copy(4).wait()
    probs_copy(5).wait()
    gather.finish()
    for copy in outgoing:
        copy.wait()

    @pl.loop(1, 32)
    def _(step):
        note_copy(step, True).wait_send()

    @pl.loop(1, 16)
    def _(step):
        pair_copy(step, True).wait_send()
        part_copy(step, True).wait_send()


def run_forward(packed, tokens, cotangent, first_note, pair_note, ada_shard, tables, rows):
    anywhere = pl.BlockSpec(memory_space=pl.ANY)
    near = pl.BlockSpec(memory_space=pltpu.VMEM)
    shape = jax.ShapeDtypeStruct
    dma = pltpu.SemaphoreType.DMA
    vmem = pltpu.VMEM
    width = 768
    outs = [
        (shape((512, width), b16), anywhere),
        (shape((8, 2, 48, 12288), b16), anywhere),
        (shape((512, width), b16), anywhere),
        (shape((512, 3 * width), b16), anywhere),
        (shape((12, 512, 512), b16), anywhere),
        (shape((512, width), b16), anywhere),
        (shape((512, width), b16), anywhere),
        (shape((512, width), f32), anywhere),
        (shape((512, width), b16), anywhere),
        (shape((512, 3072), b16), anywhere),
        (shape((512, 3072), b16), anywhere),
        (shape((512, 3072), b16), anywhere),
        (shape((1, 4608), f32), near),
        (shape((1, width), f32), near),
        (shape((32, 128), f32), near),
        (shape((32, 128), f32), near),
        (shape((16, 16, 384), b16), anywhere),
    ]
    scratch = [
        vmem((8, 2, 48, 12288), b16),
        vmem((32, 1, 128), f32),
        vmem((16, 16, 384), b16),
        vmem((16, 1, 4608), f32),
        vmem((16, 1, 4608), f32),
        vmem((512, width), f32),
        vmem((512, width), b16),
        vmem((512, 3 * width), b16),
        vmem((12, 128, 384), f32),
        vmem((3, 16, 128), f32),
        vmem((2, 2, 512, 512), b16),
        vmem((512, width), b16),
        vmem((512, width), b16),
        vmem((512, width), f32),
        vmem((512, width), b16),
        vmem((512, 3072), b16),
        vmem((512, 3072), b16),
        vmem((512, 3072), b16),
        vmem((512, width), f32),
        vmem((512, width), b16),
        dma((job_count, 4, 2)),
        dma((job_count, 4, 2)),
        dma((8,)),
        dma((8,)),
        dma((8,)),
        dma((8,)),
        dma((32,)),
        dma((32,)),
        dma((16,)),
        dma((16,)),
        dma((16,)),
        dma((16,)),
        dma((4,)),
        dma((2,)),
        dma((24,)),
    ]
    return pl.pallas_call(
        forward_kernel,
        name="forward",
        out_shape=[one for one, _ in outs],
        in_specs=[anywhere] + [near] * 7,
        out_specs=[spec for _, spec in outs],
        scratch_shapes=scratch,
        compiler_params=pltpu.CompilerParams(
            collective_id=0, has_side_effects=True, vmem_limit_bytes=66_000_000
        ),
    )(packed, tokens, cotangent, first_note, pair_note, ada_shard, tables, rows)


side_jobs = 2
messages_in_job = 7


class Scatter:
    def __init__(self, at, grads, ring_in, core_in, side_in, last_in, summed, sems):
        self.at = at
        self.grads = grads
        self.ring_in = ring_in
        self.core_in = core_in
        self.side_in = side_in
        self.last_in = last_in
        self.summed = summed
        self.now = 0
        self.begun = []
        (
            self.ring_send,
            self.ring_recv,
            self.core_send,
            self.core_recv,
            self.side_send,
            self.side_recv,
            self.last_send,
            self.last_recv,
            self.credit,
        ) = sems

    def column(self, job, owner):
        inner = modulo(job, jobs_in_chunk)
        outer = quot(inner, 4)
        return aligned(inner * job_cols + side_cols + outer * (owner * ring_cols - ring_cols))

    def block(self, job, position):
        at = self.at
        buffer = modulo(quot(job, jobs_in_chunk), grad_buffers)
        span = pl.ds(self.column(job, at.x), job_cols)
        return self.grads.at[buffer, at.chip(position), at.c, :, span]

    def slot(self, job, step, way):
        return job * messages_in_job + (0 if step == 0 else 2 * step - 1 + way)

    def ring(self, job, step, way):
        at = self.at
        sign = 1 - 2 * way
        slot = self.slot(job, step, way)
        return remote(
            self.block(job, at.p + (4 - step) * sign),
            self.ring_in.at[slot],
            self.ring_send.at[slot],
            self.ring_recv.at[slot],
            at.ring_id(at.p + sign),
        )

    def absorb(self, job, step, way):
        self.ring(job, step, way).wait_recv()
        sign = 1 - 2 * way
        own = self.block(job, self.at.p + (3 - step) * sign)
        came = self.ring_in[self.slot(job, step, way)]
        own[...] = (own[...].astype(f32) + came.astype(f32)).astype(b16)

    def core(self, turn, piece):
        at = self.at
        span = pl.ds(aligned(piece * side_cols), side_cols)
        return remote(
            self.grads.at[turn % grad_buffers, :, 1 - at.c, :, span],
            self.core_in.at[turn % 2, piece],
            self.core_send.at[turn, piece],
            self.core_recv.at[turn, piece],
            at.core_id(),
        )

    def core_start(self, turn, piece):
        if turn >= 2:
            pl.semaphore_wait(self.credit.at[turn % 2, piece], 1)
        self.core(turn, piece).start()

    def core_add(self, turn, piece):
        at = self.at
        self.core(turn, piece).wait_recv()
        span = pl.ds(piece * side_cols, side_cols)

        @pl.loop(0, chip_count)
        def _(chip):
            own = self.grads.at[turn % grad_buffers, chip, at.c, :, span]
            came = self.core_in[turn % 2, piece, chip]
            own[...] = (own[...].astype(f32) + came.astype(f32)).astype(b16)

        if turn < 2:
            pl.semaphore_signal(
                self.credit.at[turn % 2, piece],
                inc=1,
                device_id=at.core_id(),
                device_id_type=mesh_ids,
            )

    def side(self, turn, half):
        at = self.at
        span = pl.ds(aligned((1 - at.x) * ring_cols + half * job_cols), job_cols)
        slot = turn * side_jobs + half
        return remote(
            self.grads.at[modulo(turn, grad_buffers), :, at.c, :, span],
            self.side_in.at[slot],
            self.side_send.at[slot],
            self.side_recv.at[slot],
            at.plane_id(),
        )

    def side_add(self, turn, half):
        at = self.at
        self.side(turn, half).wait_recv()
        span = pl.ds(aligned(at.x * ring_cols + half * job_cols), job_cols)

        @pl.loop(0, chip_count)
        def _(chip):
            own = self.grads.at[modulo(turn, grad_buffers), chip, at.c, :, span]
            came = self.side_in[turn * side_jobs + half, chip]
            own[...] = (own[...].astype(f32) + came.astype(f32)).astype(b16)

    def last(self, job):
        return remote(
            self.block(job, self.at.p),
            self.last_in.at[job],
            self.last_send.at[job],
            self.last_recv.at[job],
            self.at.plane_id(),
        )

    def store(self, job):
        at = self.at
        self.last(job).wait_recv()
        turn = quot(job, jobs_in_chunk)
        inner = modulo(job, jobs_in_chunk)
        if isinstance(job, int):
            chunk = (3, 1, 2, 0)[turn]
        else:
            chunk = turn + 3 * (1 - jnp.minimum(turn, 1)) - 3 * lax.div(turn, 3)
        base = chunk * chunk_cols
        mine = self.block(job, at.p)[...].astype(f32)
        other = self.last_in[job].astype(f32)

        def whole():
            span = pl.ds(aligned(base + self.column(job, at.x)), job_cols)
            self.summed[:, span] = mine + other

        def halves():
            span = pl.ds(aligned(base + self.column(job, at.x)), job_cols)
            self.summed[:, span] = mine
            span = pl.ds(aligned(base + self.column(job, 1 - at.x)), job_cols)
            self.summed[:, span] = other

        on(inner < 4, whole)
        on(inner >= 4, halves)

    def begin(self, turn, beside, wait=0):
        first = self.now + wait
        assert not self.begun or first >= self.begun[-1][0] + self.begun[-1][2]
        base = turn * jobs_in_chunk
        self.begun.append((first, base + 4, 2) if beside else (first, base, 4))

    def step(self, count=1):
        for _ in range(count):
            self.tick(self.now)
            self.now += 1

    def drain(self):
        last = self.begun[-1][0] + 2 + 4 * scatter_stride + 2
        pl.loop(self.now, last)(self.tick)
        self.now = last

    def tick(self, tau):
        def each(age, body):
            spot = tau - age
            if isinstance(spot, int):
                for first, base, count in self.begun:
                    if 0 <= spot - first < count:
                        body(base + spot - first)
                return
            job = jnp.int32(-1)
            for first, base, count in self.begun:
                inside = jnp.logical_and(spot >= first, spot < first + count)
                job = jnp.where(inside, spot - first + base, job)
            pl.when(job >= 0)(lambda: body(job))

        def two(step, body):
            def run(job):
                body(job, step, 0)
                body(job, step, 1)

            return run

        def start(job, step, way):
            self.ring(job, step, way).start()

        gap = scatter_stride
        each(4 * gap, two(3, self.absorb))
        each(3 * gap, two(2, self.absorb))
        each(2 * gap, two(1, self.absorb))
        each(gap, lambda job: self.absorb(job, 0, modulo(job, 2)))

        def beside(job):
            inner = modulo(job, jobs_in_chunk)
            turn = quot(job, jobs_in_chunk)
            on(inner == 4, lambda: self.side_add(turn, 0))
            on(inner == 5, lambda: self.side_add(turn, 1))

        each(0, beside)
        each(3 * gap, two(3, start))
        each(2 * gap, two(2, start))
        each(gap, two(1, start))
        each(0, lambda job: start(job, 0, modulo(job, 2)))
        each(4 * gap, lambda job: self.last(job).start())
        each(4 * gap + 2, self.store)

    def sent(self, turns):
        @pl.loop(turns[0] * jobs_in_chunk, turns[-1] * jobs_in_chunk + jobs_in_chunk)
        def _(job):
            self.ring(job, 0, lax.rem(job, 2)).wait_send()
            for step in range(1, 4):
                self.ring(job, step, 0).wait_send()
                self.ring(job, step, 1).wait_send()
            self.last(job).wait_send()

        for turn in turns:
            for piece in range(4):
                self.core(turn, piece).wait_send()
            for half in range(2):
                self.side(turn, half).wait_send()


def halves_of(values):
    high = values.astype(b16)
    return high, (values - high.astype(f32)).astype(b16)


def backward_kernel(
    held,
    probs_all,
    h_one_all,
    qkv_all,
    attended_all,
    proj_all,
    middle_all,
    h_two_all,
    gate_all,
    up_all,
    act_all,
    tokens_all,
    cotangent_all,
    adaptive,
    d_gate_two,
    pre_all,
    notes,
    pair_all,
    ada_shard,
    rows,
    d_tokens_out,
    summed,
    grad_ada,
    grad_tables,
    grad_pair,
    grad_proj,
    grad_break,
    grads,
    ring_in,
    core_in,
    side_in,
    last_in,
    piece_in,
    probs,
    d_scores,
    cot,
    act,
    gate,
    up,
    hidden,
    mid,
    d_mid,
    d_hid,
    proj,
    low,
    sums,
    lines,
    far,
    note_wide,
    note_low,
    vector_in,
    vector_wide,
    d_ada_all,
    pair_work,
    ring_send,
    ring_recv,
    core_send,
    core_recv,
    side_send,
    side_recv,
    last_send,
    last_recv,
    credit,
    load_sem,
    piece_sem,
    probs_sem,
    vector_send,
    vector_recv,
    share_send,
    share_recv,
):
    at = Place()
    scatter = Scatter(
        at,
        grads,
        ring_in,
        core_in,
        side_in,
        last_in,
        summed,
        (
            ring_send,
            ring_recv,
            core_send,
            core_recv,
            side_send,
            side_recv,
            last_send,
            last_recv,
            credit,
        ),
    )
    loads = []

    def load(src, dst):
        copy = pltpu.make_async_copy(src, dst, load_sem.at[len(loads)])
        copy.start()
        loads.append(copy)
        return copy

    cot_load = load(cotangent_all, cot)
    act_load = load(act_all, act)
    piece_order = [9216 + 768 * n for n in range(4)]
    for n in range(4):
        piece_order += [3072 + 768 * n, 6144 + 768 * n]
    piece_order += [2304, 0, 768, 1536]

    def piece_copy(index):
        if isinstance(index, int):
            column = pl.ds(piece_order[index], side_cols)
        else:
            inner = index - 4
            start = 3072 + 768 * lax.div(inner, 2) + 3072 * lax.rem(inner, 2)
            start = jnp.where(index < 4, 9216 + 768 * index, start)
            start = jnp.where(index == 12, 2304, start)
            start = jnp.where(index > 12, (index - 13) * 768, start)
            column = pl.ds(pl.multiple_of(start, 128), side_cols)
        index = modulo(index, 4)
        return pltpu.make_async_copy(
            held.at[:, :, :, column], piece_in.at[index], piece_sem.at[index]
        )

    def piece(index):
        piece_copy(index).wait()
        return piece_in[modulo(index, 4)].reshape(768, 768)

    def piece_used(index):
        on(index + 4 < len(piece_order), lambda: piece_copy(index + 4).start())

    for index in range(4):
        piece_copy(index).start()
    gate_load = load(gate_all, gate)
    up_load = load(up_all, up)
    hidden_load = load(h_two_all, hidden)
    mid_load = load(middle_all, mid)
    proj_load = load(proj_all, proj)

    def probs_copy(pair):
        slot = modulo(pair, 2)
        return pltpu.make_async_copy(
            probs_all.at[pl.ds(pair * 2, 2)], probs.at[slot], probs_sem.at[slot]
        )

    probs_copy(0).start()
    probs_copy(1).start()
    greet_all(at)
    scale_one = adaptive[:, 768:1536]
    gate_one = adaptive[:, 1536:2304]
    scale_two = adaptive[:, 3072:3840]
    gate_two = adaptive[:, 3840:4608]
    sums[...] = jnp.zeros_like(sums)

    def columns(part):
        return pl.ds(aligned(part * 768), 768)

    def put(turn, part, left, right):
        span = columns(part)
        grads[turn % grad_buffers, :, :, :, span] = (
            dot_tn(left, right).astype(b16).reshape(8, 2, 48, 768)
        )
        scatter.core_start(turn, part)

    def merge_sides(turn):
        scatter.core_add(turn, 0)
        scatter.core_add(turn, 3)
        scatter.side(turn, 0).start()
        scatter.side(turn, 1).start()

    def merge(turn, sides=True):
        if sides:
            merge_sides(turn)
        scatter.core_add(turn, 1)
        scatter.core_add(turn, 2)
        scatter.begin(turn, False)

    cot_load.wait()
    low[...] = (gate_two * cot[...].astype(f32)).astype(b16)
    act_load.wait()

    @pl.loop(0, 4)
    def _(index):
        part = lax.rem(3 * index, 4)
        put(0, part, low[...], act[:, columns(part)])

    qkv_load = load(qkv_all, act.at[:, 0:2304])
    attended_load = load(attended_all, act.at[:, 2304:3072])
    gate_load.wait()
    up_load.wait()

    def first_part():
        merge(0)

    @pl.loop(0, 4)
    def _(part):
        d_hid[...] = dot_nn(low[...], piece(part))
        piece_used(part)
        span = columns(part)

        @pl.loop(0, 8)
        def _(block):
            line = pl.ds(pl.multiple_of(block * 64, 64), 64)
            d_act = d_hid[line, :]
            gated = gate[line, span].astype(f32)
            raised = up[line, span].astype(f32)
            sigma = 1.0 / (1.0 + jnp.exp(-gated))
            scaled = d_act * sigma
            gate[line, span] = (scaled * raised * (1.0 + gated * (1.0 - sigma))).astype(b16)
            up[line, span] = (scaled * gated).astype(b16)

        on(part == 0, first_part)
        scatter.tick(scatter.now + part)

    scatter.now += 4
    hidden_load.wait()

    @pl.loop(0, 4)
    def _(index):
        part = lax.rem(3 * index, 4)
        put(1, part, hidden[...], gate[:, columns(part)])
        on(index == 1, lambda: scatter.tick(scatter.now))

    scatter.now += 1
    scatter.step(plan[1])

    def second_part():
        merge(1)
        scatter.begin(0, True, 4)
        scatter.tick(scatter.now)

    @pl.loop(0, 4)
    def _(index):
        part = lax.rem(3 * index, 4)
        put(2, part, hidden[...], up[:, columns(part)])
        on(index == 1, second_part)

    scatter.now += 1
    scatter.step(plan[2])
    h_one_load = load(h_one_all, hidden)
    d_hid[...] = jnp.zeros_like(d_hid)

    @pl.loop(0, 4)
    def _(part):
        span = columns(part)
        d_hid[...] += dot_nt(gate[:, span], piece(4 + 2 * part))
        piece_used(4 + 2 * part)
        d_hid[...] += dot_nt(up[:, span], piece(5 + 2 * part))
        piece_used(5 + 2 * part)
        scatter.tick(scatter.now + part)

    scatter.now += 4
    merge(2)
    scatter.begin(1, True, 4)
    scatter.begin(2, True, 12)
    mid_load.wait()
    proj_load.wait()

    @pl.loop(0, 8)
    def _(block):
        line = pl.ds(pl.multiple_of(block * 64, 64), 64)
        values = mid[line, :]
        centred = values - jnp.mean(values, axis=-1, keepdims=True)
        inverse = lax.rsqrt(jnp.mean(centred * centred, axis=-1, keepdims=True) + epsilon)
        centred = centred * inverse
        grad = d_hid[line, :]
        sums[0:1, :] += jnp.sum(grad, axis=0, keepdims=True)
        sums[1:2, :] += jnp.sum(grad * centred, axis=0, keepdims=True)
        grad = grad * (1.0 + scale_two)
        grad = grad - jnp.mean(grad, axis=-1, keepdims=True) - centred * jnp.mean(
            grad * centred, axis=-1, keepdims=True
        )
        grad = cot[line, :].astype(f32) + inverse * grad
        d_mid[line, :] = grad
        sums[2:3, :] += jnp.sum(grad * proj[line, :].astype(f32), axis=0, keepdims=True)
        low[line, :] = (gate_one * grad).astype(b16)

    tokens_load = load(tokens_all, proj)
    scatter.step(plan[4])
    cot[...] = dot_nt(low[...], piece(12)).astype(b16)
    piece_used(12)
    qkv_load.wait()
    attended_load.wait()
    scatter.step(plan[4])
    start_tick = scatter.now

    chain_row = rows[0:1, :]
    first_size = 512.0 - jnp.sum(chain_row, axis=1, keepdims=True)
    low_lane = lax.broadcasted_iota(jnp.int32, (1, 128), 1) < 64
    line_number = lax.broadcasted_iota(jnp.int32, (128, 128), 0).astype(f32)
    lines[...] = jnp.zeros_like(lines)
    far[...] = jnp.zeros_like(far)

    @pl.loop(0, 6)
    def _(pair):
        lane = pl.multiple_of(pair * 128, 128)
        slot = lax.rem(pair, 2)
        probs_copy(pair).wait()
        queries = act[:, pl.ds(lane, 128)] * jnp.asarray(0.125, b16)
        keys = act[:, pl.ds(768 + lane, 128)]
        content = act[:, pl.ds(1536 + lane, 128)]
        d_out = cot[:, pl.ds(lane, 128)]
        d_queries, d_keys, d_content = [], [], []
        for half in range(2):
            head = pair * 2 + half
            own = low_lane if half == 0 else jnp.logical_not(low_lane)
            d_own = jnp.where(own, d_out, jnp.zeros_like(d_out))
            d_probs = dot_nt(d_own, content)
            band = [None, None, None]
            low_sum = jnp.zeros((128, 128), f32)
            high_sum = jnp.zeros((128, 128), f32)
            apart = jnp.zeros((128, 128), f32)
            for block in range(4):
                line = slice(block * 128, block * 128 + 128)
                here = probs[slot, half, line, :].astype(f32)
                weighted = here * d_probs[line, :]
                weighted = weighted - here * jnp.sum(weighted, axis=1, keepdims=True)
                d_scores[line, :] = weighted.astype(b16)
                chain_here = (line_number + 128.0 * block >= first_size).astype(f32)
                for other in range(4):
                    tile = weighted[:, other * 128 : other * 128 + 128]
                    there = chain_row[:, other * 128 : other * 128 + 128]
                    same = jnp.where(chain_here == there, tile, jnp.zeros_like(tile))
                    apart = apart + (tile - same)
                    offset = block - other
                    if offset > 1:
                        low_sum = low_sum + same
                    elif offset < -1:
                        high_sum = high_sum + same
                    elif band[1 - offset] is None:
                        band[1 - offset] = same
                    else:
                        band[1 - offset] = band[1 - offset] + same
            far[0, pl.ds(head, 1), :] = jnp.sum(low_sum, axis=0, keepdims=True)
            far[1, pl.ds(head, 1), :] = jnp.sum(high_sum, axis=0, keepdims=True)
            far[2, pl.ds(head, 1), :] = jnp.sum(apart, axis=0, keepdims=True)
            folded = jnp.concatenate(band + [jnp.zeros((128, 128), f32)], axis=1)
            size = 64
            while size >= 1:
                folded = folded[0:size, :] + pltpu.roll(
                    folded[size : 2 * size, :], 512 - size, 1
                )
                size = size // 2
            lines[pl.ds(head, 1), :] = folded
            d_here = d_scores[...]
            d_queries.append(dot_nn(d_here, keys))
            masked = jnp.where(own, queries, jnp.zeros_like(queries))
            d_keys.append(dot_tn(d_here, masked))
            d_content.append(dot_tn(probs[slot, half], d_own))
            if half == 0:
                for extra in range(plan[5]):
                    scatter.tick(start_tick + (plan[5] + plan[6]) * pair + extra)
        gate[:, pl.ds(lane, 128)] = (
            jnp.where(low_lane, d_queries[0], d_queries[1]) * 0.125
        ).astype(b16)
        gate[:, pl.ds(768 + lane, 128)] = (d_keys[0] + d_keys[1]).astype(b16)
        gate[:, pl.ds(1536 + lane, 128)] = (d_content[0] + d_content[1]).astype(b16)
        on(pair < 4, lambda: probs_copy(pair + 2).start())
        for extra in range(plan[6]):
            scatter.tick(start_tick + (plan[5] + plan[6]) * pair + plan[5] + extra)

    scatter.now += 6 * (plan[5] + plan[6])
    if grad_buffers == 3:
        done = scatter.begun[2][0] + 2 + 4 * scatter_stride + 2
        assert scatter.now >= done and scatter.begun[2][1] == 4
        scatter.sent([0])
    put(3, 3, act[:, 2304:3072], low[...])
    h_one_load.wait()
    put(3, 0, hidden[...], gate[:, 0:768])
    scatter.step(plan[7])
    put(3, 1, hidden[...], gate[:, 768:1536])
    merge_sides(3)
    put(3, 2, hidden[...], gate[:, 1536:2304])
    for part in range(3):
        product = dot_nt(gate[:, part * 768 : part * 768 + 768], piece(13 + part))
        if part == 0:
            d_hid[...] = product
        else:
            d_hid[...] += product
        if part == 0:
            merge(3, False)
            scatter.begin(3, True, plan[10])
        scatter.step(plan[8])
    tokens_load.wait()

    @pl.loop(0, 8)
    def _(block):
        line = pl.ds(pl.multiple_of(block * 64, 64), 64)
        values = proj[line, :].astype(f32)
        centred = values - jnp.mean(values, axis=-1, keepdims=True)
        inverse = lax.rsqrt(jnp.mean(centred * centred, axis=-1, keepdims=True) + epsilon)
        centred = centred * inverse
        grad = d_hid[line, :]
        sums[3:4, :] += jnp.sum(grad, axis=0, keepdims=True)
        sums[4:5, :] += jnp.sum(grad * centred, axis=0, keepdims=True)
        cot[line, :] = grad.astype(b16)
        grad = grad * (1.0 + scale_one)
        grad = grad - jnp.mean(grad, axis=-1, keepdims=True) - centred * jnp.mean(
            grad * centred, axis=-1, keepdims=True
        )
        low[line, :] = (d_mid[line, :] + inverse * grad).astype(b16)

    tokens_store = load(low, d_tokens_out)
    break_sum = dot_nn(jnp.broadcast_to(rows[1:2, :], (8, 512)).astype(b16), cot[...])
    scatter.step(plan[9])

    scale = class_map(128)
    line_high, line_low = halves_of(lines[...])
    d_table = dot_nn(line_high, scale) + dot_nn(line_low, scale)
    kind = lax.broadcasted_iota(jnp.int32, (16, 128), 1)
    for index, label in ((0, 126), (1, 0), (2, 127)):
        total = jnp.sum(far[index], axis=1, keepdims=True)
        d_table = d_table + jnp.where(kind == label, total, jnp.zeros_like(d_table))
    vectors = [sums[3:4, :], sums[4:5, :], sums[2:3, :], sums[0:1, :], sums[1:2, :]]
    vectors.append(d_gate_two[...])
    for index in range(6):
        for part in range(6):
            note_wide[index * 6 + part : index * 6 + part + 1, :] = vectors[index][
                :, part * 128 : part * 128 + 128
            ]
    note_wide[36:48, :] = d_table[0:12, :]
    for part in range(6):
        note_wide[48 + part : 49 + part, :] = break_sum[0:1, part * 128 : part * 128 + 128]
    note_wide[54:64, :] = jnp.zeros((10, 128), f32)
    note_low[...] = note_wide[...].astype(b16)
    vector_in[at.x, at.cy, at.c] = note_low[...]
    scatter.step(plan[9])

    def vector_copy(step, mine):
        other = lax.rem(at.cy + step, 8)
        slot = at.cy if mine else other
        return remote(
            note_low,
            vector_in.at[at.x, slot, at.c],
            vector_send.at[step],
            vector_recv.at[slot],
            (at.x, other * 2 + at.c),
        )

    def plane_copy(plane):
        block = vector_in.at[plane, :, at.c]
        return remote(block, block, share_send.at[0], share_recv.at[0], at.plane_id())

    def pair_copy(core):
        block = vector_in.at[:, :, core]
        return remote(block, block, share_send.at[1], share_recv.at[1], at.core_id())

    for step in range(1, 8):
        vector_copy(step, True).start()
    scatter.step(plan[9])
    for step in range(1, 8):
        vector_copy(step, False).wait_recv()
    plane_copy(at.x).start()
    scatter.step(plan[9])
    plane_copy(1 - at.x).wait_recv()
    pair_copy(at.c).start()
    scatter.step(plan[9])
    pair_copy(1 - at.c).wait_recv()
    total = jnp.zeros((64, 128), f32)
    for plane in range(2):
        vector_wide[...] = vector_in[plane].reshape(1024, 128).astype(f32)
        for part in range(36):
            d_ada_all[plane * 16 : plane * 16 + 16, part * 128 : part * 128 + 128] = vector_wide[
                pl.ds(part, 16, stride=64), :
            ].astype(b16)
        for window in range(16):
            total = total + vector_wide[window * 64 : window * 64 + 64, :]
    note_wide[...] = total
    pre = pre_all[...]
    sigma = 1.0 / (1.0 + jnp.exp(-pre))
    grad_ada[...] = dot_tn((pre * sigma).astype(b16)[:, 0:48], d_ada_all[...])
    d_pre = dot_nt(d_ada_all[...], ada_shard[...])
    pre, sigma = pre[:, 0:48], sigma[:, 0:48]
    d_pre = d_pre * sigma * (1.0 + pre * (1.0 - sigma))
    scatter.step(plan[9])
    labels = notes[...]
    kind = lax.broadcasted_iota(jnp.int32, (32, grad_tables.shape[1]), 1).astype(f32)
    hit = (kind == labels[:, 48:49]) | (kind == labels[:, 49:50]) | (kind == labels[:, 50:51])
    hit = hit.astype(f32).astype(b16)
    high, rest = halves_of(d_pre)
    grad_tables[...] = dot_tn(high, hit) + dot_tn(rest, hit)
    scatter.step(plan[9])
    grad_break[...] = note_wide[48:56, :]
    d_table = note_wide[36:52, :]
    keep = lax.broadcasted_iota(jnp.int32, (16, 128), 0) < 12
    d_table = jnp.where(keep, d_table, jnp.zeros_like(d_table))
    gathered = pair_all[...].reshape(256, 384)
    features = gathered[:, 0:128].astype(f32)
    features = features - jnp.mean(features, axis=0, keepdims=True)
    inverse = lax.rsqrt(jnp.mean(features * features, axis=0, keepdims=True) + epsilon)
    features = features * inverse
    high, rest = halves_of(d_table)
    pair_low = features.astype(b16)
    pair_work[:, 0:16] = dot_nt(pair_low, high) + dot_nt(pair_low, rest)
    mine = pl.ds(pl.multiple_of(at.f * 16, 16), 16)
    grad_proj[...] = pair_work[mine, :]
    weights = gathered[:, 128:144]
    grad = dot_nn(weights, high) + dot_nn(weights, rest)
    grad = inverse * (
        grad
        - jnp.mean(grad, axis=0, keepdims=True)
        - features * jnp.mean(grad * features, axis=0, keepdims=True)
    )
    pair_work[...] = grad
    grad_pair[...] = pair_work[mine, :]
    scatter.drain()
    scatter.sent([1, 2, 3] if grad_buffers == 3 else [0, 1, 2, 3])
    tokens_store.wait()
    for step in range(1, 8):
        vector_copy(step, True).wait_send()
    plane_copy(at.x).wait_send()
    pair_copy(at.c).wait_send()


def run_backward(saved, tokens, cotangent, ada_shard, rows, table_rows):
    (
        held,
        h_one,
        qkv,
        probs,
        attended,
        proj,
        middle,
        h_two,
        gate,
        up,
        act,
        adaptive,
        d_gate_two,
        pre,
        notes,
        pair_all,
    ) = saved
    anywhere = pl.BlockSpec(memory_space=pl.ANY)
    near = pl.BlockSpec(memory_space=pltpu.VMEM)
    shape = jax.ShapeDtypeStruct
    dma = pltpu.SemaphoreType.DMA
    vmem = pltpu.VMEM
    width = 768
    outs = [
        (shape((512, width), b16), anywhere),
        (shape((48, 12288), f32), near),
        (shape((48, 4608), f32), near),
        (shape((48, table_rows), f32), near),
        (shape((16, 128), f32), near),
        (shape((16, 128), f32), near),
        (shape((8, 128), f32), near),
    ]
    ring_slots = job_count * messages_in_job
    scratch = [
        vmem((grad_buffers, 8, 2, 48, chunk_cols), b16),
        vmem((ring_slots, 48, job_cols), b16),
        vmem((2, 4, 8, 48, side_cols), b16),
        vmem((8, 8, 48, job_cols), b16),
        vmem((job_count, 48, job_cols), b16),
        vmem((4, 8, 2, 48, side_cols), b16),
        vmem((2, 2, 512, 512), b16),
        vmem((512, 512), b16),
        vmem((512, width), b16),
        vmem((512, 3072), b16),
        vmem((512, 3072), b16),
        vmem((512, 3072), b16),
        vmem((512, width), b16),
        vmem((512, width), f32),
        vmem((512, width), f32),
        vmem((512, width), f32),
        vmem((512, width), b16),
        vmem((512, width), b16),
        vmem((8, width), f32),
        vmem((16, 512), f32),
        vmem((3, 16, 128), f32),
        vmem((64, 128), f32),
        vmem((64, 128), b16),
        vmem((2, 8, 2, 64, 128), b16),
        vmem((1024, 128), f32),
        vmem((32, 4608), b16),
        vmem((256, 128), f32),
        dma((ring_slots,)),
        dma((ring_slots,)),
        dma((4, 4)),
        dma((4, 4)),
        dma((8,)),
        dma((8,)),
        dma((job_count,)),
        dma((job_count,)),
        pltpu.SemaphoreType.REGULAR((2, 4)),
        dma((16,)),
        dma((4,)),
        dma((2,)),
        dma((8,)),
        dma((8,)),
        dma((2,)),
        dma((2,)),
    ]
    return pl.pallas_call(
        backward_kernel,
        name="backward",
        out_shape=[one for one, _ in outs],
        in_specs=[anywhere] * 13 + [near] * 7,
        out_specs=[spec for _, spec in outs],
        scratch_shapes=scratch,
        compiler_params=pltpu.CompilerParams(
            collective_id=1, has_side_effects=True, vmem_limit_bytes=67_043_328
        ),
    )(
        held,
        probs,
        h_one,
        qkv,
        attended,
        proj,
        middle,
        h_two,
        gate,
        up,
        act,
        tokens,
        cotangent,
        adaptive,
        d_gate_two,
        pre,
        notes,
        pair_all,
        ada_shard,
        rows,
    )


def pack_kernel(
    time_embed,
    cath_class,
    cath_arch,
    cath_topo,
    res_counts,
    chain_ids,
    break_mask,
    w_qkv,
    w_out,
    w_gate,
    w_up,
    w_down,
    table_class,
    table_arch,
    table_topo,
    break_vec,
    pair_table,
    pair_proj,
    packed,
    first_note,
    pair_note,
    tables,
    rows,
):
    packed[:, 0:2304] = w_qkv[...]
    packed[:, 2304:3072] = w_out[...]
    packed[:, 3072:6144] = w_gate[...]
    packed[:, 6144:9216] = w_up[...]
    packed[:, 9216:12288] = w_down[...]
    lane = lax.broadcasted_iota(jnp.int32, (1, 128), 1)
    marks = jnp.zeros((1, 128), f32)
    for index, labels in enumerate((cath_class, cath_arch, cath_topo)):
        label = (labels[0] + 128 * index).astype(f32)
        marks = jnp.where(lane == 48 + index, label, marks)
    embed = time_embed[...].astype(f32)
    for owner in range(16):
        first_note[owner] = marks
        first_note[owner, :, 0:48] = embed[:, owner * 48 : owner * 48 + 48]
    shard = lax.axis_index("fsdp") * 48
    unit = lax.broadcasted_iota(jnp.int32, (128, 128), 0)
    unit = (unit == lax.broadcasted_iota(jnp.int32, (128, 128), 1)).astype(f32).astype(b16)
    pair_note[:, 0:128] = pair_table[...]
    pair_note[:, 128:256] = jnp.zeros((16, 128), b16)
    pair_note[:, 128:140] = pair_proj[...]
    spot = lax.broadcasted_iota(jnp.int32, (48, 2048), 1) - shard
    spot = (spot == lax.broadcasted_iota(jnp.int32, (48, 2048), 0)).astype(f32).astype(b16)
    placed = dot_nn(jnp.broadcast_to(break_vec[...].astype(f32), (16, 48)).astype(b16), spot)
    line = lax.broadcasted_iota(jnp.int32, (16, 128), 0)
    breaks = jnp.zeros((16, 128), f32)
    for row in range(16):
        breaks = jnp.where(line == row, placed[:, row * 128 : row * 128 + 128], breaks)
    pair_note[:, 256:384] = breaks.astype(b16)
    for index, lookup in enumerate((table_class, table_arch)):
        block = dot_tn(lookup[...], unit[0 : lookup.shape[0], :])
        tables[:, index * 128 : index * 128 + 128] = block.astype(b16)
    tables[:, 256:] = table_topo[...]
    rows[0:1, :] = chain_ids[...].astype(f32)
    rows[1:2, :] = break_mask[...].astype(f32)
    position = lax.broadcasted_iota(jnp.int32, (1, 512), 1)
    rows[2:3, :] = jnp.where(position < res_counts[0], 0.0, -1e30)
    rows[3:8, :] = jnp.zeros((5, 512), f32)


def forward_inputs(
    time_embed,
    cath_class,
    cath_arch,
    cath_topo,
    res_counts,
    chain_ids,
    break_mask,
    w_qkv,
    w_out,
    w_gate,
    w_up,
    w_down,
    table_class,
    table_arch,
    table_topo,
    break_vec,
    pair_table,
    pair_proj,
):
    near = pl.BlockSpec(memory_space=pltpu.VMEM)
    flat = pl.BlockSpec(memory_space=pltpu.SMEM)
    count = 256 + table_topo.shape[0]
    shape = jax.ShapeDtypeStruct
    return pl.pallas_call(
        pack_kernel,
        name="pack",
        out_shape=[
            shape((48, 12288), b16),
            shape((16, 1, 128), f32),
            shape((16, 384), b16),
            shape((48, count), b16),
            shape((8, 512), f32),
        ],
        in_specs=[near] + [flat] * 4 + [near] * 13,
        out_specs=[near] * 5,
    )(
        time_embed,
        cath_class,
        cath_arch,
        cath_topo,
        res_counts,
        chain_ids,
        break_mask,
        w_qkv,
        w_out,
        w_gate,
        w_up,
        w_down.T,
        table_class,
        table_arch,
        table_topo.T,
        break_vec[None, :],
        pair_table.T,
        pair_proj,
    )


def unpack_kernel(
    summed,
    ada_in,
    tables,
    pair_in,
    proj_in,
    break_in,
    grad_ada,
    grad_qkv,
    grad_out,
    grad_gate,
    grad_up,
    grad_down,
    grad_class,
    grad_arch,
    grad_topo,
    grad_break,
    grad_pair,
    grad_proj,
):
    grad_ada[...] = ada_in[...]
    grad_qkv[...] = summed[:, 0:2304]
    grad_out[...] = summed[:, 2304:3072]
    grad_gate[...] = summed[:, 3072:6144]
    grad_up[...] = summed[:, 6144:9216]
    grad_down[...] = summed[:, 9216:12288]
    grad_class[...] = tables[:, 0:128].T[0 : grad_class.shape[0], :]
    grad_arch[...] = tables[:, 128:256].T[0 : grad_arch.shape[0], :]
    grad_topo[...] = tables[:, 256:]
    shard = lax.axis_index("fsdp") * 48
    total = jnp.zeros((1, 48), f32)
    for owner in range(16):
        row, column = divmod(owner * 48, 128)
        width = min(48, 128 - column)
        piece = break_in[row : row + 1, column : column + width]
        if width < 48:
            piece = jnp.concatenate([piece, break_in[row + 1 : row + 2, 0 : 48 - width]], axis=1)
        total = jnp.where(shard == owner * 48, piece, total)
    grad_break[...] = total
    grad_pair[...] = pair_in[...]
    grad_proj[...] = proj_in[:, 0:12]


def run_unpack(summed, ada, tables, pair, proj, breaks, sizes):
    near = pl.BlockSpec(memory_space=pltpu.VMEM)
    shape = jax.ShapeDtypeStruct
    outs = [
        (48, 4608),
        (48, 2304),
        (48, 768),
        (48, 3072),
        (48, 3072),
        (48, 3072),
        (sizes[0], 48),
        (sizes[1], 48),
        (48, sizes[2]),
        (1, 48),
        (16, 128),
        (16, 12),
    ]
    return pl.pallas_call(
        unpack_kernel,
        name="unpack",
        out_shape=[shape(one, f32) for one in outs],
        in_specs=[near] * 6,
        out_specs=[near] * 12,
    )(summed, ada, tables, pair, proj, breaks)


def fast_shards(
    tokens,
    cotangent,
    time_embed,
    cath_class,
    cath_arch,
    cath_topo,
    res_counts,
    chain_ids,
    break_mask,
    w_ada,
    w_qkv,
    w_out,
    w_gate,
    w_up,
    w_down,
    table_class,
    table_arch,
    table_topo,
    break_vec,
    pair_table,
    pair_proj,
):
    packed, first_note, pair_note, tables, rows = forward_inputs(
        time_embed,
        cath_class,
        cath_arch,
        cath_topo,
        res_counts,
        chain_ids,
        break_mask,
        w_qkv,
        w_out,
        w_gate,
        w_up,
        w_down,
        table_class,
        table_arch,
        table_topo,
        break_vec,
        pair_table,
        pair_proj,
    )
    output, *saved = run_forward(
        packed, tokens[0], cotangent[0], first_note, pair_note, w_ada, tables, rows
    )
    d_tokens, summed, grad_ada, grad_tables, grad_pair, grad_proj, grad_break = run_backward(
        saved, tokens[0], cotangent[0], w_ada, rows, tables.shape[1]
    )
    sizes = (table_class.shape[0], table_arch.shape[0], table_topo.shape[0])
    grads = run_unpack(summed, grad_ada, grad_tables, grad_pair, grad_proj, grad_break, sizes)
    return (
        output[None],
        d_tokens[None],
        *grads[:5],
        grads[5].T,
        grads[6],
        grads[7],
        grads[8].T,
        grads[9][0],
        grads[10].T,
        grads[11],
    )


def solution(mesh):
    in_specs = (
        P(("dp", "fsdp"), None, None),
        P(("dp", "fsdp"), None, None),
        P(("dp", "fsdp"), None),
        P(("dp", "fsdp")),
        P(("dp", "fsdp")),
        P(("dp", "fsdp")),
        P(("dp", "fsdp")),
        P(("dp", "fsdp"), None),
        P(("dp", "fsdp"), None),
        P("fsdp", None),
        P("fsdp", None),
        P("fsdp", None),
        P("fsdp", None),
        P("fsdp", None),
        P(None, "fsdp"),
        P(None, "fsdp"),
        P(None, "fsdp"),
        P(None, "fsdp"),
        P("fsdp"),
        P(None, "fsdp"),
        P("fsdp", None),
    )
    out_specs = (
        P(("dp", "fsdp"), None, None),
        P(("dp", "fsdp"), None, None),
        P("fsdp", None),
        P("fsdp", None),
        P("fsdp", None),
        P("fsdp", None),
        P("fsdp", None),
        P(None, "fsdp"),
        P(None, "fsdp"),
        P(None, "fsdp"),
        P(None, "fsdp"),
        P("fsdp"),
        P(None, "fsdp"),
        P("fsdp", None),
    )
    sizes = dict(mesh.shape)
    body = fast_shards if (sizes["dp"], sizes["fsdp"]) == (2, 16) else shards
    return jax.shard_map(body, mesh=mesh, in_specs=in_specs, out_specs=out_specs, check_vma=False)
```
